32 devices in a mesh: patch: 16 (over z, x, core), sample: 2 (over y).
Axes of the slice: x: 2, y: 2, z: 4, core: 2. Of those that a mesh axis runs over, the one named last changes fastest.
Arguments:
- nodes: bfloat16 [8, 8192, 512], P('sample', 'patch'), may hold values from -6 to 6
- neighbours: int32 [8192, 16], P('patch'), may hold values from 0 to 767
- send_rows: int32 [64, 64], P('patch'), may hold values from 0 to 511
- noise_code: float32 [8, 16], P('sample'), may hold values from -5 to 5
- w_query: bfloat16 [512, 512], P(('patch', 'sample')), may hold values from -0.25 to 0.25
- w_key: bfloat16 [512, 512], P(('patch', 'sample')), may hold values from -0.25 to 0.25
- w_value: bfloat16 [512, 512], P(('patch', 'sample')), may hold values from -0.25 to 0.25
- w_out: bfloat16 [512, 512], P(('patch', 'sample')), may hold values from -0.5 to 0.5
- w_up: bfloat16 [512, 2048], P(('patch', 'sample')), may hold values from -0.25 to 0.25
- b_up: bfloat16 [2048], P(('patch', 'sample')), may hold values from -3 to 3
- w_down: bfloat16 [2048, 512], P(('patch', 'sample')), may hold values from -0.1875 to 0.1875
- b_down: bfloat16 [512], P(('patch', 'sample')), may hold values from -3 to 3
- cond_weight: bfloat16 [16, 2048], P(None, ('patch', 'sample')), may hold values from -1 to 1
- cond_bias: bfloat16 [2048], P(('patch', 'sample')), may hold values from -2 to 2
- cotangent: bfloat16 [8, 8192, 512], P('sample', 'patch'), may hold values from -6 to 6
Outputs:
- out_nodes: bfloat16 [8, 8192, 512], P('sample', 'patch')
- grad_nodes: float32 [8, 8192, 512], P('sample', 'patch')
- grad_query: float32 [512, 512], P(('patch', 'sample'))
- grad_key: float32 [512, 512], P(('patch', 'sample'))
- grad_value: float32 [512, 512], P(('patch', 'sample'))
- grad_out: float32 [512, 512], P(('patch', 'sample'))
- grad_up: float32 [512, 2048], P(('patch', 'sample'))
- grad_b_up: float32 [2048], P(('patch', 'sample'))
- grad_down: float32 [2048, 512], P(('patch', 'sample'))
- grad_b_down: float32 [512], P(('patch', 'sample'))
- grad_cond_weight: float32 [16, 2048], P(None, ('patch', 'sample'))
- grad_cond_bias: float32 [2048], P(('patch', 'sample'))
The draws below stay inside these ranges and needn't reach their ends.
Inputs may be any that keep to these rules, and one draw needn't show every extreme that they name: `neighbours`: slot values below 512 name a node of the same patch; higher values name a received row as in the reference program; repeats are allowed. `send_rows`: row 4 q + b lists local node numbers of patch q; repeats are allowed.
All inputs are finite; a program needn't handle non-finite values.
Results may differ from the reference program's by a relative error of at most 0.014.
The reference program's roundings to bfloat16 on the way count: a program that leaves them out, or rounds other values in their place, can miss the bound.
Values may be sent and summed in bfloat16 or wider, within the bound.
No kernel may reach another device: no remote copies, remote signals or barrier semaphores. Data moves between devices by JAX's collectives and lax.ppermute only.
A program may use at most 320 MiB of HBM per device.

```python
import jax
import jax.numpy as jnp
from jax import lax

D = 512
FF = 2048
HEADS = 4
HEAD = 128
NBRS = 16
CODE = 16
STRIDE = 4
NODE_DEV = 512
HR = 64
NODES = 8192
SAMPLES = 8
SENDS = 64
N_PATCH = 16


def set_ends(entries, rng, low, high):
    place = [jax.random.randint(jax.random.fold_in(rng, axis), (), 0, length) for axis, length in enumerate(entries.shape)]
    widest = entries.shape.index(max(entries.shape))
    neighbour = place[:widest] + [(place[widest] + 1) % entries.shape[widest]] + place[widest + 1:]
    return entries.at[tuple(place)].set(low).at[tuple(neighbour)].set(high)


def strengthened(values, stream_key, source, target, blocks, factor):
    owner, partner = [(jnp.arange(values.shape[dim]) // (values.shape[dim] // blocks)).reshape([-1 if axis == dim else 1 for axis in range(values.ndim)]) for dim in (source, target)]
    chosen = jax.random.permutation(stream_key, blocks)[partner]
    strong = (owner == chosen) | (owner == (partner + blocks // 2) % blocks)
    return jnp.where(strong, factor * values, values)


def block_levels(rng, shape, cuts, least, high):
    loudness = 1.0
    for dim, blocks in cuts:
        heights = jax.random.uniform(jax.random.fold_in(jax.random.fold_in(rng, 6), dim), (blocks,), jnp.float32, least / len(cuts), high / len(cuts))
        loudness = loudness * jnp.repeat(jnp.exp(heights), shape[dim] // blocks).reshape((-1,) + (1,) * (len(shape) - 1 - dim))
    return loudness


def gaussian(rng, shape, scale, limit, split=(), kind=jnp.bfloat16):
    entries = jax.random.normal(rng, shape, jnp.float32) * scale
    if len(split) > 0:
        entries = block_levels(rng, shape, split, -0.22, 0.18) * entries
    return jnp.clip(entries, min=-limit, max=limit).astype(kind)


def bell_draw_with(own_key, dims, scale, reach, split, heavy, kind=jnp.bfloat16):
    drawn = scale * jax.random.normal(own_key, dims, jnp.float32)
    if split:
        drawn = drawn * block_levels(own_key, dims, split, -0.22, 0.18)
    return jnp.clip(strengthened(drawn, jax.random.fold_in(own_key, 3), *heavy), -reach, reach).astype(kind)


def setup_inputs(seed: int = 0) -> dict:
    arg_keys = jax.random.split(jax.random.key(seed), 16)
    nodes = bell_draw_with(arg_keys[0], (SAMPLES, NODES, D), 1.0, 6.0, ((0, 2), (1, 16)), (1, 2, 16, 2.0))
    neighbours = set_ends(jax.random.randint(arg_keys[1], (NODES, NBRS), 0, NODE_DEV + 4 * HR), jax.random.fold_in(arg_keys[1], 1), 0, (NODE_DEV + 4 * HR) - 1).astype(jnp.int32)
    send_rows = set_ends(jax.random.randint(arg_keys[2], (SENDS, HR), 0, NODE_DEV), jax.random.fold_in(arg_keys[2], 1), 0, NODE_DEV - 1).astype(jnp.int32)
    noise_code = gaussian(arg_keys[3], (SAMPLES, CODE), 1.0, 5.0, ((0, 2),), jnp.float32)
    w_query = gaussian(arg_keys[4], (D, D), D ** -0.5, 0.25, ((0, 32),))
    w_key = gaussian(arg_keys[5], (D, D), D ** -0.5, 0.25, ((0, 32),))
    w_value = gaussian(arg_keys[6], (D, D), D ** -0.5, 0.25, ((0, 32),))
    w_out = gaussian(arg_keys[7], (D, D), (D // 4) ** -0.5, 0.5, ((0, 32),))
    w_up = gaussian(arg_keys[8], (D, FF), D ** -0.5, 0.25, ((0, 32),))
    b_up = gaussian(arg_keys[9], (FF,), 0.5, 3.0, ((0, 32),))
    w_down = gaussian(arg_keys[10], (FF, D), (FF // 2) ** -0.5, 0.1875, ((0, 32),))
    b_down = gaussian(arg_keys[11], (D,), 0.5, 3.0, ((0, 32),))
    cond_weight = gaussian(arg_keys[12], (CODE, 4 * D), (2 * CODE) ** -0.5, 1.0, ((1, 32),))
    cond_bias = gaussian(arg_keys[13], (4 * D,), 0.3, 2.0, ((0, 32),))
    cotangent = gaussian(arg_keys[14], (SAMPLES, NODES, D), 1.0, 6.0, ((0, 2), (1, 16)))
    return dict(nodes=nodes, neighbours=neighbours, send_rows=send_rows, noise_code=noise_code, w_query=w_query, w_key=w_key, w_value=w_value, w_out=w_out, w_up=w_up, b_up=b_up, w_down=w_down, b_down=b_down, cond_weight=cond_weight, cond_bias=cond_bias, cotangent=cotangent)


@jax.custom_vjp
def low(v):
    return lax.optimization_barrier(v.astype(jnp.bfloat16)).astype(jnp.float32)

@jax.custom_vjp
def low_back(v):
    return v

def low_keep(v):
    return (low(v), None)

def low_pass(kept, grad):
    return (grad,)

def back_keep(v):
    return (v, None)

def back_low(kept, grad):
    return (low(grad),)
low.defvjp(low_keep, low_pass)
low_back.defvjp(back_keep, back_low)
epsilon = 1e-05
highest_precision = lax.Precision.HIGHEST

def layer_normalize(values):
    centre = lax.optimization_barrier(jnp.mean(values, axis=-1, keepdims=True))
    centred = values - centre
    return centred * lax.rsqrt(lax.optimization_barrier(jnp.mean(centred * centred, axis=-1, keepdims=True)) + epsilon)

def project(left_operand, right_operand):
    return jnp.einsum('aor,rm->aom', left_operand, right_operand, precision=highest_precision)

def global_index(neighbours, send_rows):
    node_ids = jnp.arange(NODES, dtype=jnp.int32)
    patch_ids = node_ids // NODE_DEV
    local_node_index = patch_ids[:, None] * NODE_DEV + neighbours
    halo_pos = jnp.maximum(neighbours - NODE_DEV, 0)
    direction = halo_pos // HR
    within = halo_pos % HR
    offsets = jnp.array([1, -1, STRIDE, -STRIDE], jnp.int32)
    source = (patch_ids[:, None] - offsets[direction]) % N_PATCH
    remote = source * NODE_DEV + send_rows[source * 4 + direction, within]
    return jnp.where(neighbours < NODE_DEV, local_node_index, remote).astype(jnp.int32)

def forward(inputs, w_query, w_key, w_value, w_out, w_up, b_up, w_down, b_down, cond_weight, cond_bias, noise_code, index):
    width = inputs.shape[-1]
    modulate = jnp.dot(noise_code, cond_weight, precision=highest_precision) + cond_bias
    scale_one = 1.0 + modulate[:, None, 0:width]
    shift_one = modulate[:, None, width:2 * width]
    scale_two = 1.0 + modulate[:, None, 2 * width:3 * width]
    shift_two = modulate[:, None, 3 * width:]
    act_one = low(layer_normalize(inputs) * scale_one + shift_one)
    queries = low_back(low(project(act_one, w_query)))
    keys = low_back(low(project(act_one, w_key)))
    values = low_back(low(project(act_one, w_value)))
    block = NODE_DEV * 8
    nblock = NODES // block
    key_flat = keys.reshape(SAMPLES * NODES, width)
    value_flat = values.reshape(SAMPLES * NODES, width)
    query_blocks = queries.reshape(SAMPLES * nblock, block, HEADS, HEAD)
    shifted = index[None, :, :] + (jnp.arange(SAMPLES, dtype=jnp.int32) * NODES)[:, None, None]
    index_blocks = shifted.reshape(SAMPLES * nblock, block, NBRS)

    def attend(pair):
        query_block, index_block = pair
        key_near = key_flat[index_block].reshape(block, NBRS, HEADS, HEAD)
        value_near = value_flat[index_block].reshape(block, NBRS, HEADS, HEAD)
        scores = low_back(jnp.einsum('nhd,nkhd->nhk', query_block, key_near, precision=highest_precision) * HEAD ** (-0.5))
        probs = jax.nn.softmax(scores, axis=-1)
        return jnp.einsum('nhk,nkhd->nhd', low(probs), value_near, precision=highest_precision)
    attended = lax.map(jax.checkpoint(attend), (query_blocks, index_blocks)).reshape(SAMPLES, NODES, width)
    attended = low_back(low(attended))
    middle = inputs + low_back(project(attended, w_out))
    act_two = low(layer_normalize(middle) * scale_two + shift_two)
    pre_act = low_back(project(act_two, w_up) + b_up)
    hidden = low(pre_act * jax.nn.sigmoid(pre_act))
    return middle + low_back(project(hidden, w_down)) + b_down

def reference(nodes, neighbours, send_rows, noise_code, w_query, w_key, w_value, w_out, w_up, b_up, w_down, b_down, cond_weight, cond_bias, cotangent):
    index = global_index(neighbours, send_rows)

    def wrapped(inputs, wq_mat, wk_mat, wv_mat, wo_mat, wu_mat, bu_vec, wd_mat, bd_vec, cw_mat, cb_vec):
        return forward(inputs, wq_mat, wk_mat, wv_mat, wo_mat, wu_mat, bu_vec, wd_mat, bd_vec, cw_mat, cb_vec, noise_code, index)
    primals = (nodes.astype(jnp.float32), w_query.astype(jnp.float32), w_key.astype(jnp.float32), w_value.astype(jnp.float32), w_out.astype(jnp.float32), w_up.astype(jnp.float32), b_up.astype(jnp.float32), w_down.astype(jnp.float32), b_down.astype(jnp.float32), cond_weight.astype(jnp.float32), cond_bias.astype(jnp.float32))
    output, pullback = jax.vjp(wrapped, *primals)
    grads = pullback(cotangent.astype(jnp.float32))
    return (output.astype(jnp.bfloat16), grads[0], grads[1], grads[2], grads[3], grads[4], grads[5], grads[6], grads[7], grads[8], grads[9], grads[10])
```

```python
import math

import jax
import jax.numpy as jnp
from jax import lax
from jax.experimental import pallas as pl
from jax.experimental.pallas import tpu as pltpu
from jax.sharding import PartitionSpec as P

HEAD = 128
STRIDE = 4
BLOCK = 16
AXES = ("patch", "sample")
EPSILON = 1e-05
F32 = jnp.float32
BF16 = jnp.bfloat16
VMEM_LIMIT = 60 * 1024 * 1024


def product(left, right):
    return jnp.dot(left, right, preferred_element_type=F32)


def product_t(left, right):
    return lax.dot_general(left, right, (((1,), (1,)), ((), ())), preferred_element_type=F32)


def from_behind(block, distance):
    count = lax.axis_size("patch")
    return lax.ppermute(block, "patch", [((i - distance) % count, i) for i in range(count)])


def swap(block, bits, devices):
    return lax.ppermute(block, AXES, [(i, i ^ bits) for i in range(devices)])


def stage_groups(devices):
    bits = [1 << i for i in reversed(range(devices.bit_length() - 1)) if (1 << i) != 2]
    groups = [bits[i : i + 2] for i in range(0, len(bits), 2)]
    return [combos(g) for g in groups] + [[2]]


def combos(group):
    if len(group) == 1:
        return [group[0]]
    high, low = group
    return [low, high, low | high]


def relative(k, devices):
    shift, out = 0, 0
    for group in stage_groups(devices):
        if len(group) == 1:
            out = out | (((k >> shift) & 1) * group[0])
            shift += 1
        else:
            out = out | (((k >> shift) & 1) * group[0]) | (((k >> (shift + 1)) & 1) * group[1])
            shift += 2
    return out


def gather_shards(shard, devices):
    groups = stage_groups(devices)
    held = shard[None]
    for group in groups[:-1]:
        held = jnp.concatenate([held] + [swap(held, c, devices) for c in group], axis=0)
    return held, swap(held, groups[-1][0], devices)


def scatter_shards(low_half, high_half, devices):
    groups = stage_groups(devices)
    got = swap(high_half, groups[-1][0], devices)
    held = (low_half.astype(F32) + got.astype(F32)).astype(BF16)
    for at, group in reversed(list(enumerate(groups[:-1]))):
        parts = len(group) + 1
        size = held.shape[0] // parts
        total = held[:size].astype(F32)
        pieces = [
            swap(held[(i + 1) * size : (i + 2) * size], c, devices) for i, c in enumerate(group)
        ]
        for piece in pieces:
            total = total + piece.astype(F32)
        held = total if at == 0 else total.astype(BF16)
    return held[0]


def layer_normalize(values):
    centre = jnp.mean(values, axis=-1, keepdims=True)
    centred = values - centre
    inverse = lax.rsqrt(jnp.mean(centred * centred, axis=-1, keepdims=True) + EPSILON)
    return centred * inverse, inverse


def norm_back(grad_hat, normed, inverse):
    first = jnp.mean(grad_hat, axis=-1, keepdims=True)
    second = jnp.mean(grad_hat * normed, axis=-1, keepdims=True)
    return inverse * (grad_hat - first - normed * second)


def whole(shape):
    return pl.BlockSpec(shape, lambda *_: (0,) * len(shape))


def per_sample(shape):
    return pl.BlockSpec((1,) + shape, lambda s, *_: (s,) + (0,) * len(shape))


def params():
    return pltpu.CompilerParams(
        dimension_semantics=("arbitrary",), vmem_limit_bytes=VMEM_LIMIT
    )


def prepare_kernel(nodes_ref, send_ref, nbr_ref, bias_ref, *out_refs):
    samples, count, _ = nodes_ref.shape
    picks = send_ref.shape[0]
    table = bias_ref.shape[0]
    near = nbr_ref.shape[0]
    place = lax.broadcasted_iota(jnp.int32, (table, count), 0)
    total = jnp.zeros((table, count), F32)
    for j in range(near):
        total = total + jnp.where(place == nbr_ref[j : j + 1, :], 1.0, 0.0)
    bias_ref[...] = jnp.where(total > 0.0, jnp.log2(jnp.maximum(total, 1.0)), -1e30)
    lanes = lax.broadcasted_iota(jnp.int32, (picks, count), 1)
    chosen = jnp.where(lanes == send_ref[...], 1.0, 0.0).astype(BF16)
    each = picks // len(out_refs)
    for s in range(samples):
        rows = product(chosen, nodes_ref[s]).astype(BF16)
        for d, out_ref in enumerate(out_refs):
            out_ref[s] = rows[d * each : (d + 1) * each]


def prepare(nodes, neighbours, send_rows):
    samples, count, width = nodes.shape
    ways, each = send_rows.shape
    table = count + ways * each
    send_column = send_rows.reshape(ways * each, 1)
    out = [jax.ShapeDtypeStruct((table, count), F32)] + [
        jax.ShapeDtypeStruct((samples, each, width), BF16)
    ] * ways
    return pl.pallas_call(
        prepare_kernel,
        out_shape=out,
        compiler_params=pltpu.CompilerParams(vmem_limit_bytes=VMEM_LIMIT),
    )(nodes, send_column, neighbours.T)


def spread(rows, step, width):
    reps = jnp.concatenate([rows] * (width // 128), axis=1)
    lane = lax.broadcasted_iota(jnp.int32, reps.shape, 1)
    row = lax.broadcasted_iota(jnp.int32, reps.shape, 0)
    return jnp.sum(jnp.where(lane // step == row, reps, 0.0), axis=0, keepdims=True)


def first_weights_kernel(me_ref, low_ref, high_ref, code_ref, wq_ref, wk_ref, wv_ref, mod_ref, raw):
    half = low_ref.shape[0]
    devices = 2 * half
    samples = code_ref.shape[1]
    width = wq_ref.shape[1]
    step = 4 * width // devices
    code = code_ref[...]
    for k in range(devices):
        source = low_ref if k < half else high_ref
        shard = me_ref[0] ^ relative(k, devices)
        rows = pl.ds(pl.multiple_of(shard * BLOCK, BLOCK), BLOCK)
        wq_ref[rows, :] = source[k % half, 0:BLOCK, :]
        wk_ref[rows, :] = source[k % half, BLOCK : 2 * BLOCK, :]
        wv_ref[rows, :] = source[k % half, 2 * BLOCK : 3 * BLOCK, :]
        cond = source[k % half, 3 * BLOCK : 4 * BLOCK, 0:128].astype(F32)
        bias = source[k % half, 3 * BLOCK : 4 * BLOCK, 128:256].astype(F32)[0:1]
        for s in range(samples):
            value = jnp.sum(cond * code[:, s : s + 1], axis=0, keepdims=True) + bias
            raw[s, pl.ds(shard, 1), :] = value
    each = devices // 4
    for s in range(samples):
        for kind in range(4):
            value = spread(raw[s, kind * each : (kind + 1) * each, :], step, width)
            mod_ref[s, kind : kind + 1, :] = value + 1.0 if kind % 2 == 0 else value


def second_weights_kernel(me_ref, low_ref, high_ref, wo_ref, wu_ref, wd_ref, bu_ref, bd_ref, raw):
    half = low_ref.shape[0]
    devices = 2 * half
    width = wo_ref.shape[1]
    hidden = wu_ref.shape[1]
    wide = hidden // width
    down = hidden // devices
    for k in range(devices):
        source = low_ref if k < half else high_ref
        shard = me_ref[0] ^ relative(k, devices)
        rows = pl.ds(pl.multiple_of(shard * BLOCK, BLOCK), BLOCK)
        long_rows = pl.ds(pl.multiple_of(shard * down, BLOCK), down)
        at = 0
        for c in range(wide):
            wu_ref[rows, c * width : (c + 1) * width] = source[k % half, at : at + BLOCK, :]
            at += BLOCK
        wd_ref[long_rows, :] = source[k % half, at : at + down, :]
        at += down
        wo_ref[rows, :] = source[k % half, at : at + BLOCK, :]
        at += BLOCK
        extra = source[k % half, at : at + BLOCK, 0:256].astype(F32)[0:1]
        raw[0, pl.ds(shard, 1), :] = extra[:, 0:128]
        raw[1, pl.ds(shard, 1), :] = extra[:, 128:256]
    each = devices // wide
    for c in range(wide):
        bu_ref[:, c * width : (c + 1) * width] = spread(
            raw[0, c * each : (c + 1) * each, :], hidden // devices, width
        )
    bd_ref[...] = spread(raw[1], width // devices, width)


def packs(width, devices):
    return width == devices * BLOCK


def gather_plain(wq, wk, wv, cond_weight, cond_bias, noise_code, wo, wu, bu, wd, bd):
    def full(x, axis=0):
        return lax.all_gather(x, AXES, axis=axis, tiled=True)

    mod = jnp.dot(
        noise_code, full(cond_weight, 1).astype(F32), precision=lax.Precision.HIGHEST
    ) + full(cond_bias).astype(F32)
    mod = mod.reshape(noise_code.shape[0], 4, wq.shape[1])
    mod = mod + jnp.array([1.0, 0.0, 1.0, 0.0], F32)[:, None]
    first = (full(wq), full(wk), full(wv), mod)
    biases = (full(bu)[None].astype(F32), full(bd)[None].astype(F32))
    return first, (full(wo), full(wu), full(wd)) + biases


def scatter_plain(sums, axes):
    return [
        lax.psum_scatter(x, AXES, scatter_dimension=axis, tiled=True)
        for x, axis in zip(sums, axes)
    ]


def repeat_lanes(rows, lanes=128):
    return jnp.tile(rows, (1, lanes // rows.shape[1]))


def fit(rows, height, width):
    return jnp.pad(rows, ((0, height - rows.shape[0]), (0, width - rows.shape[1])))


def smem():
    return pl.BlockSpec(memory_space=pltpu.SMEM)


def gather_first(me, wq, wk, wv, cond_weight, cond_bias, noise_code, devices):
    width = wq.shape[1]
    extra = jnp.concatenate(
        [repeat_lanes(cond_weight), fit(repeat_lanes(cond_bias[None]), BLOCK, 128)], axis=1
    )
    shard = jnp.concatenate([wq, wk, wv, fit(extra, BLOCK, width)], axis=0)
    low_half, high_half = gather_shards(shard, devices)
    samples = noise_code.shape[0]
    full = jax.ShapeDtypeStruct((width, width), BF16)
    return pl.pallas_call(
        first_weights_kernel,
        out_shape=[full, full, full, jax.ShapeDtypeStruct((samples, 4, width), F32)],
        in_specs=[smem()] + [pl.BlockSpec(memory_space=pltpu.VMEM)] * 3,
        scratch_shapes=[pltpu.VMEM((samples, devices, 128), F32)],
        compiler_params=pltpu.CompilerParams(vmem_limit_bytes=VMEM_LIMIT),
    )(me, low_half, high_half, noise_code.T)


def gather_second(me, wo, wu, bu, wd, bd, devices):
    width = wo.shape[1]
    hidden = wu.shape[1]
    extra = jnp.concatenate([repeat_lanes(bu[None]), repeat_lanes(bd[None])], axis=1)
    parts = [wu[:, c * width : (c + 1) * width] for c in range(hidden // width)]
    shard = jnp.concatenate(parts + [wd, wo, fit(extra, BLOCK, width)], axis=0)
    low_half, high_half = gather_shards(shard, devices)
    return pl.pallas_call(
        second_weights_kernel,
        out_shape=[
            jax.ShapeDtypeStruct((width, width), BF16),
            jax.ShapeDtypeStruct((width, hidden), BF16),
            jax.ShapeDtypeStruct((hidden, width), BF16),
            jax.ShapeDtypeStruct((1, hidden), F32),
            jax.ShapeDtypeStruct((1, width), F32),
        ],
        in_specs=[smem()] + [pl.BlockSpec(memory_space=pltpu.VMEM)] * 2,
        scratch_shapes=[pltpu.VMEM((2, devices, 128), F32)],
        compiler_params=pltpu.CompilerParams(vmem_limit_bytes=VMEM_LIMIT),
    )(me, low_half, high_half)


def attend_kernel(*refs):
    nodes_ref, h0, h1, h2, h3, mod_ref, wq_ref, wk_ref, wv_ref, bias_ref = refs[:10]
    act_ref, q_ref, k_ref, v_ref, p_ref, att_ref = refs[10:]
    count = nodes_ref.shape[1]
    each = h0.shape[1]
    width = nodes_ref.shape[2]
    scale, shift = mod_ref[0, 0:1, :], mod_ref[0, 1:2, :]

    def activate(rows):
        hat, _ = layer_normalize(rows.astype(F32))
        return (hat * scale + shift).astype(BF16)

    act_ref[0, 0:count, :] = activate(nodes_ref[0])
    for d, ref in enumerate((h0, h1, h2, h3)):
        at = count + d * each
        act_ref[0, at : at + each, :] = activate(ref[0])
    act = act_ref[0]
    q_ref[0] = product(act[0:count], wq_ref[...]).astype(BF16)
    k_ref[0] = product(act, wk_ref[...]).astype(BF16)
    v_ref[0] = product(act, wv_ref[...]).astype(BF16)
    factor = math.log2(math.e) * HEAD ** (-0.5)
    for h in range(width // HEAD):
        cols = slice(h * HEAD, (h + 1) * HEAD)
        scores = product_t(k_ref[0, :, cols], q_ref[0, :, cols]) * factor + bias_ref[...]
        top = jnp.max(scores, axis=0, keepdims=True)
        expo = jnp.exp2(scores - top)
        total = jnp.sum(expo, axis=0, keepdims=True)
        probs = (expo * (1.0 / total)).astype(BF16)
        p_ref[0, h] = probs
        mixed = product(v_ref[0, :, cols].T, probs)
        att_ref[0, :, cols] = mixed.T.astype(BF16)


def attend(nodes, halos, mod, wq, wk, wv, bias):
    samples, count, width = nodes.shape
    table = bias.shape[0]
    heads = width // HEAD
    each = halos[0].shape[1]

    def out(rows):
        return jax.ShapeDtypeStruct((samples, rows, width), BF16)

    return pl.pallas_call(
        attend_kernel,
        grid=(samples,),
        in_specs=[per_sample((count, width))]
        + [per_sample((each, width))] * 4
        + [per_sample((4, width))]
        + [whole((width, width))] * 3
        + [whole((table, count))],
        out_specs=[per_sample((table, width)), per_sample((count, width))]
        + [per_sample((table, width))] * 2
        + [per_sample((heads, table, count)), per_sample((count, width))],
        out_shape=[out(table), out(count), out(table), out(table)]
        + [jax.ShapeDtypeStruct((samples, heads, table, count), BF16), out(count)],
        compiler_params=params(),
    )(nodes, *halos, mod, wq, wk, wv, bias)


def feed_kernel(*refs):
    me_ref, nodes_ref, att_ref, cot_ref, mod_ref, wo_ref, wu_ref, wd_ref, bu_ref, bd_ref = refs[:10]
    out_ref, gmid_ref, gatt_ref, gmod_ref = refs[10:14]
    sums = refs[14:-6]
    up_acc, down_acc, wo_acc, bu_acc, bd_acc, down_rows = refs[-6:]
    s = pl.program_id(0)
    count, width = nodes_ref.shape[1:]
    hidden_size = wu_ref.shape[1]
    wide = hidden_size // width

    @pl.when(s == 0)
    def _():
        up_acc[...] = jnp.zeros_like(up_acc)
        down_acc[...] = jnp.zeros_like(down_acc)
        wo_acc[...] = jnp.zeros_like(wo_acc)
        bu_acc[...] = jnp.zeros_like(bu_acc)
        bd_acc[...] = jnp.zeros_like(bd_acc)

    scale, shift = mod_ref[0, 2:3, :], mod_ref[0, 3:4, :]
    attended = att_ref[0]
    cot = cot_ref[0]
    cot_float = cot.astype(F32)
    middle = nodes_ref[0].astype(F32) + product(attended, wo_ref[...])
    hat, inverse = layer_normalize(middle)
    act = (hat * scale + shift).astype(BF16)
    act_t = act.T
    cot_t = cot.T
    result = middle + bd_ref[...]
    grad_act = jnp.zeros((count, width), F32)
    bd_acc[...] += jnp.sum(cot_float, axis=0, keepdims=True)
    for c in range(wide):
        cols = slice(c * width, (c + 1) * width)
        w_up = wu_ref[:, cols]
        w_down = wd_ref[cols, :]
        pre = product(act, w_up) + bu_ref[:, cols]
        gate = 0.5 * jnp.tanh(0.5 * pre) + 0.5
        value = pre * gate
        hidden = value.astype(BF16)
        result = result + product(hidden, w_down)
        down_acc[:, cols] += product(cot_t, hidden)
        grad_pre = product_t(cot, w_down) * (gate + value * (1.0 - gate))
        low_pre = grad_pre.astype(BF16)
        bu_acc[:, cols] += jnp.sum(low_pre.astype(F32), axis=0, keepdims=True)
        up_acc[:, cols] += product(act_t, low_pre)
        grad_act = grad_act + product_t(low_pre, w_up)
    out_ref[0] = result.astype(BF16)
    gmod_ref[0, 0:1, :] = jnp.sum(grad_act * hat, axis=0, keepdims=True)
    gmod_ref[0, 1:2, :] = jnp.sum(grad_act, axis=0, keepdims=True)
    grad_middle = cot_float + norm_back(grad_act * scale, hat, inverse)
    gmid_ref[0] = grad_middle
    branch = grad_middle.astype(BF16)
    wo_acc[...] += product(attended.T, branch)
    gatt_ref[0] = product_t(branch, wo_ref[...]).astype(BF16)

    @pl.when(s == pl.num_programs(0) - 1)
    def _():
        for c in range(wide):
            cols = slice(c * width, (c + 1) * width)
            down_rows[cols, :] = down_acc[:, cols].T
        if len(sums) > 2:
            for ref, value in zip(sums, (up_acc, down_rows, wo_acc, bu_acc, bd_acc)):
                ref[...] = value[...]
            return
        low_ref, high_ref = sums
        half = low_ref.shape[0]
        devices = 2 * half
        down = hidden_size // devices

        for part, ref in enumerate((low_ref, high_ref)):

            def pack(i, _, part=part, ref=ref):
                shard = me_ref[0] ^ relative(i + part * half, devices)
                rows = pl.ds(pl.multiple_of(shard * BLOCK, BLOCK), BLOCK)
                long_rows = pl.ds(pl.multiple_of(shard * down, BLOCK), down)
                at = 0
                for c in range(wide):
                    ref[i, at : at + BLOCK, :] = up_acc[rows, c * width : (c + 1) * width].astype(
                        BF16
                    )
                    at += BLOCK
                ref[i, at : at + down, :] = down_rows[long_rows, :].astype(BF16)
                at += down
                ref[i, at : at + BLOCK, :] = wo_acc[rows, :].astype(BF16)
                at += BLOCK
                up_tile = pl.multiple_of(((shard * (hidden_size // devices)) // 128) * 128, 128)
                down_tile = pl.multiple_of(((shard * (width // devices)) // 128) * 128, 128)
                ref[i, at : at + BLOCK, 0:128] = jnp.broadcast_to(
                    bu_acc[:, pl.ds(up_tile, 128)], (BLOCK, 128)
                ).astype(BF16)
                ref[i, at : at + BLOCK, 128:256] = jnp.broadcast_to(
                    bd_acc[:, pl.ds(down_tile, 128)], (BLOCK, 128)
                ).astype(BF16)
                ref[i, at : at + BLOCK, 256:] = jnp.zeros((BLOCK, width - 256), BF16)
                return 0

            lax.fori_loop(0, half, pack, 0)


def feed(me, nodes, attended, cot, mod, wo, wu, wd, bu, bd, devices):
    samples, count, width = nodes.shape
    hidden = wu.shape[1]
    rows = hidden // width * BLOCK + hidden // devices + 2 * BLOCK
    half = devices // 2
    tile = per_sample((count, width))
    packed = (half, rows, width)
    sums = [jax.ShapeDtypeStruct(packed, BF16)] * 2
    if not packs(width, devices):
        plain = ((width, hidden), (hidden, width), (width, width), (1, hidden), (1, width))
        sums = [jax.ShapeDtypeStruct(shape, F32) for shape in plain]
    return pl.pallas_call(
        feed_kernel,
        grid=(samples,),
        in_specs=[smem(), tile, tile, tile, per_sample((4, width))]
        + [whole((width, width)), whole((width, hidden)), whole((hidden, width))]
        + [whole((1, hidden)), whole((1, width))],
        out_specs=[tile, tile, tile, per_sample((2, width))] + [whole(x.shape) for x in sums],
        out_shape=[
            jax.ShapeDtypeStruct((samples, count, width), BF16),
            jax.ShapeDtypeStruct((samples, count, width), F32),
            jax.ShapeDtypeStruct((samples, count, width), BF16),
            jax.ShapeDtypeStruct((samples, 2, width), F32),
        ]
        + sums,
        scratch_shapes=[
            pltpu.VMEM((width, hidden), F32),
            pltpu.VMEM((width, hidden), F32),
            pltpu.VMEM((width, width), F32),
            pltpu.VMEM((1, hidden), F32),
            pltpu.VMEM((1, width), F32),
            pltpu.VMEM((hidden, width), F32),
        ],
        compiler_params=params(),
    )(me, nodes, attended, cot, mod, wo, wu, wd, bu, bd)


def attend_back_kernel(*refs):
    me_ref, nodes_ref, h0, h1, h2, h3, code_ref, gmod_ref = refs[:8]
    act_ref, q_ref, k_ref, v_ref, p_ref, gatt_ref, wq_ref, wk_ref, wv_ref = refs[8:17]
    gact_ref, b0, b1, b2, b3 = refs[17:22]
    outs = refs[22:-8]
    gq, gk, gv, q_acc, k_acc, v_acc, cond_acc, bias_acc = refs[-8:]
    s = pl.program_id(0)
    count, width = nodes_ref.shape[1:]
    each = h0.shape[1]
    inv_root = HEAD ** (-0.5)

    @pl.when(s == 0)
    def _():
        q_acc[...] = jnp.zeros_like(q_acc)
        k_acc[...] = jnp.zeros_like(k_acc)
        v_acc[...] = jnp.zeros_like(v_acc)
        cond_acc[...] = jnp.zeros_like(cond_acc)
        bias_acc[...] = jnp.zeros_like(bias_acc)

    for h in range(width // HEAD):
        cols = slice(h * HEAD, (h + 1) * HEAD)
        probs = p_ref[0, h]
        grad_att = gatt_ref[0, :, cols]
        keys = k_ref[0, :, cols]
        probs_float = probs.astype(F32)
        grad_probs = product_t(v_ref[0, :, cols], grad_att)
        inner = jnp.sum(probs_float * grad_probs, axis=0, keepdims=True)
        grad_scores = (probs_float * (grad_probs - inner)).astype(BF16)
        gv[:, cols] = product(probs, grad_att).astype(BF16)
        gk[:, cols] = (product(grad_scores, q_ref[0, :, cols]) * inv_root).astype(BF16)
        gq[:, cols] = (product(keys.T, grad_scores) * inv_root).T.astype(BF16)

    act_t = act_ref[0].T
    q_acc[...] += product(act_t[:, 0:count], gq[...])
    k_acc[...] += product(act_t, gk[...])
    v_acc[...] += product(act_t, gv[...])
    grad_act = (
        product_t(gq[...], wq_ref[...])
        + product_t(gk[0:count, :], wk_ref[...])
        + product_t(gv[0:count, :], wv_ref[...])
    )
    gact_ref[0] = grad_act
    grad_far = product_t(gk[count:, :], wk_ref[...]) + product_t(gv[count:, :], wv_ref[...])
    hat, _ = layer_normalize(nodes_ref[0].astype(F32))
    scale_sum = jnp.sum(grad_act * hat, axis=0, keepdims=True)
    shift_sum = jnp.sum(grad_act, axis=0, keepdims=True)
    for d, (far, back) in enumerate(zip((h0, h1, h2, h3), (b0, b1, b2, b3))):
        part = grad_far[d * each : (d + 1) * each]
        far_hat, _ = layer_normalize(far[0].astype(F32))
        scale_sum = scale_sum + jnp.sum(part * far_hat, axis=0, keepdims=True)
        shift_sum = shift_sum + jnp.sum(part, axis=0, keepdims=True)
        back[0] = part.astype(BF16)
    sums = (scale_sum, shift_sum, gmod_ref[0, 0:1, :], gmod_ref[0, 1:2, :])
    code = code_ref[0]
    for kind, value in enumerate(sums):
        cols = slice(kind * width, (kind + 1) * width)
        cond_acc[:, cols] += code * value
        bias_acc[:, cols] += value

    @pl.when(s == pl.num_programs(0) - 1)
    def _():
        if len(outs) > 2:
            for ref, value in zip(outs, (q_acc, k_acc, v_acc, cond_acc, bias_acc)):
                ref[...] = value[...]
            return
        half = outs[0].shape[0]
        devices = 2 * half
        for part, ref in enumerate(outs):

            def pack(i, _, part=part, ref=ref):
                shard = me_ref[0] ^ relative(i + part * half, devices)
                rows = pl.ds(pl.multiple_of(shard * BLOCK, BLOCK), BLOCK)
                ref[i, 0:BLOCK, :] = q_acc[rows, :].astype(BF16)
                ref[i, BLOCK : 2 * BLOCK, :] = k_acc[rows, :].astype(BF16)
                ref[i, 2 * BLOCK : 3 * BLOCK, :] = v_acc[rows, :].astype(BF16)
                tile = pl.multiple_of(((shard * (4 * width // devices)) // 128) * 128, 128)
                ref[i, 3 * BLOCK : 4 * BLOCK, 0:128] = cond_acc[:, pl.ds(tile, 128)].astype(BF16)
                ref[i, 3 * BLOCK : 4 * BLOCK, 128:256] = jnp.broadcast_to(
                    bias_acc[:, pl.ds(tile, 128)], (BLOCK, 128)
                ).astype(BF16)
                ref[i, 3 * BLOCK : 4 * BLOCK, 256:] = jnp.zeros((BLOCK, width - 256), BF16)
                return 0

            lax.fori_loop(0, half, pack, 0)


def attend_back(me, nodes, halos, noise_code, gmod, saved, gatt, wq, wk, wv, devices):
    samples, count, width = nodes.shape
    act, queries, keys, values, probs = saved
    table = act.shape[1]
    heads = width // HEAD
    each = halos[0].shape[1]
    half = devices // 2
    codes = noise_code.shape[1]
    code = noise_code[:, :, None]
    sums = [jax.ShapeDtypeStruct((half, 4 * BLOCK, width), BF16)] * 2
    if not packs(width, devices):
        plain = [(width, width)] * 3 + [(codes, 4 * width), (1, 4 * width)]
        sums = [jax.ShapeDtypeStruct(shape, F32) for shape in plain]
    tile, long_tile = per_sample((count, width)), per_sample((table, width))
    small = per_sample((each, width))
    return pl.pallas_call(
        attend_back_kernel,
        grid=(samples,),
        in_specs=[smem(), tile]
        + [small] * 4
        + [per_sample((codes, 1)), per_sample((2, width))]
        + [long_tile, tile, long_tile, long_tile]
        + [per_sample((heads, table, count)), tile]
        + [whole((width, width))] * 3,
        out_specs=[tile] + [small] * 4 + [whole(x.shape) for x in sums],
        out_shape=[jax.ShapeDtypeStruct((samples, count, width), F32)]
        + [jax.ShapeDtypeStruct((samples, each, width), BF16)] * 4
        + sums,
        scratch_shapes=[
            pltpu.VMEM((count, width), BF16),
            pltpu.VMEM((table, width), BF16),
            pltpu.VMEM((table, width), BF16),
            pltpu.VMEM((width, width), F32),
            pltpu.VMEM((width, width), F32),
            pltpu.VMEM((width, width), F32),
            pltpu.VMEM((codes, 4 * width), F32),
            pltpu.VMEM((1, 4 * width), F32),
        ],
        compiler_params=params(),
    )(me, nodes, *halos, code, gmod, act, queries, keys, values, probs, gatt, wq, wk, wv)


def finish_kernel(nodes_ref, gact_ref, b0, b1, b2, b3, send_ref, mod_ref, gmid_ref, out_ref):
    count = nodes_ref.shape[1]
    each = b0.shape[1]
    picks = send_ref.shape[1]
    place = lax.broadcasted_iota(jnp.int32, (count, picks), 0)
    chosen = jnp.where(place == send_ref[...], 1.0, 0.0).astype(BF16)
    grad_act = gact_ref[0]
    for d, ref in enumerate((b0, b1, b2, b3)):
        grad_act = grad_act + product(chosen[:, d * each : (d + 1) * each], ref[0])
    hat, inverse = layer_normalize(nodes_ref[0].astype(F32))
    out_ref[0] = gmid_ref[0] + norm_back(grad_act * mod_ref[0, 0:1, :], hat, inverse)


def finish(nodes, gact, backs, send_rows, mod, gmid):
    samples, count, width = nodes.shape
    each = backs[0].shape[1]
    picks = send_rows.size
    tile = per_sample((count, width))
    return pl.pallas_call(
        finish_kernel,
        grid=(samples,),
        in_specs=[tile, tile]
        + [per_sample((each, width))] * 4
        + [whole((1, picks)), per_sample((4, width)), tile],
        out_specs=tile,
        out_shape=jax.ShapeDtypeStruct((samples, count, width), F32),
        compiler_params=params(),
    )(nodes, gact, *backs, send_rows.reshape(1, picks), mod, gmid)


def own(rows, position, size, axis):
    return lax.dynamic_slice_in_dim(rows, (position * size) % 128, size, axis)


def unpack_feed(total, position, width, hidden, devices):
    wide, down = hidden // width, hidden // devices
    grad_up = jnp.concatenate([total[c * BLOCK : (c + 1) * BLOCK] for c in range(wide)], axis=1)
    at = wide * BLOCK
    last = total[at + down + BLOCK]
    return (
        grad_up,
        total[at : at + down],
        total[at + down : at + down + BLOCK],
        own(last[0:128], position, down, 0),
        own(last[128:256], position, width // devices, 0),
    )


def unpack_proj(total, position, width, devices):
    step = 4 * width // devices
    extra = total[3 * BLOCK : 4 * BLOCK]
    return tuple(total[i * BLOCK : (i + 1) * BLOCK] for i in range(3)) + (
        own(extra[:, 0:128], position, step, 1),
        own(extra[0, 128:256], position, step, 0),
    )


def body(
    nodes,
    neighbours,
    send_rows,
    noise_code,
    w_query,
    w_key,
    w_value,
    w_out,
    w_up,
    b_up,
    w_down,
    b_down,
    cond_weight,
    cond_bias,
    cotangent,
):
    devices = lax.axis_size("patch") * lax.axis_size("sample")
    position = lax.axis_index("patch") * lax.axis_size("sample") + lax.axis_index("sample")
    me = position.astype(jnp.int32).reshape(1)
    width = nodes.shape[2]
    hidden = w_up.shape[1]
    offsets = (1, -1, STRIDE, -STRIDE)

    packed = packs(width, devices)
    bias, *sends = prepare(nodes, neighbours, send_rows)
    if packed:
        first = gather_first(
            me, w_query, w_key, w_value, cond_weight, cond_bias, noise_code, devices
        )
        second = gather_second(me, w_out, w_up, b_up, w_down, b_down, devices)
    else:
        first, second = gather_plain(
            w_query,
            w_key,
            w_value,
            cond_weight,
            cond_bias,
            noise_code,
            w_out,
            w_up,
            b_up,
            w_down,
            b_down,
        )
    wq, wk, wv, mod = first
    halos = [from_behind(block, offset) for block, offset in zip(sends, offsets)]
    *saved, attended = attend(nodes, halos, mod, wq, wk, wv, bias)
    result, gmid, gatt, gmod, *feed_sums = feed(
        me, nodes, attended, cotangent, mod, *second, devices
    )
    if packed:
        feed_sums = unpack_feed(
            scatter_shards(*feed_sums, devices), position, width, hidden, devices
        )
    else:
        feed_sums[3:] = [x[0] for x in feed_sums[3:]]
        feed_sums = scatter_plain(feed_sums, (0,) * 5)
    gact, *rest = attend_back(
        me, nodes, halos, noise_code, gmod, saved, gatt, wq, wk, wv, devices
    )
    backs = [from_behind(block, -offset) for block, offset in zip(rest[:4], offsets)]
    if packed:
        proj_sums = unpack_proj(scatter_shards(*rest[4:], devices), position, width, devices)
    else:
        rest[-1] = rest[-1][0]
        proj_sums = scatter_plain(rest[4:], (0, 0, 0, 1, 0))
    grad_nodes = finish(nodes, gact, backs, send_rows, mod, gmid)
    grad_up, grad_down, grad_out, grad_b_up, grad_b_down = feed_sums
    grad_query, grad_key, grad_value, grad_cond, grad_cond_bias = proj_sums
    return (
        result,
        grad_nodes,
        grad_query,
        grad_key,
        grad_value,
        grad_out,
        grad_up,
        grad_b_up,
        grad_down,
        grad_b_down,
        grad_cond,
        grad_cond_bias,
    )


def solution(mesh):
    both = P(("patch", "sample"), None)
    flat = P(("patch", "sample"))
    split = P("sample", "patch", None)
    cond = P(None, ("patch", "sample"))
    return jax.shard_map(
        body,
        mesh=mesh,
        in_specs=(
            split,
            P("patch", None),
            P("patch", None),
            P("sample", None),
            both,
            both,
            both,
            both,
            both,
            flat,
            both,
            flat,
            cond,
            flat,
            split,
        ),
        out_specs=(split, split, both, both, both, both, both, flat, both, flat, cond, flat),
        check_vma=False,
    )
```

```python
import math

import jax
import jax.numpy as jnp
from jax import lax
from jax.experimental import pallas as pl
from jax.experimental.pallas import tpu as pltpu
from jax.sharding import PartitionSpec as P


HEAD = 128
STRIDE = 4
BLOCK = 16
AXES = ("patch", "sample")
EPSILON = 1e-05
F32 = jnp.float32
BF16 = jnp.bfloat16
MIB = 1024 * 1024


def product(left, right):
    return jnp.dot(left, right, preferred_element_type=F32)


def product_t(left, right):
    return lax.dot_general(left, right, (((1,), (1,)), ((), ())), preferred_element_type=F32)


def from_behind(block, distance):
    count = lax.axis_size("patch")
    return lax.ppermute(block, "patch", [((i - distance) % count, i) for i in range(count)])


def swap(block, bits, devices):
    return lax.ppermute(block, AXES, [(i, i ^ bits) for i in range(devices)])


def stage_groups(devices):
    bits = [1 << i for i in reversed(range(devices.bit_length() - 1)) if (1 << i) != 2]
    groups = [bits[i : i + 2] for i in range(0, len(bits), 2)]
    return [combos(g) for g in groups] + [[2]]


def combos(group):
    if len(group) == 1:
        return [group[0]]
    high, low = group
    return [low, high, low | high]


def relative(k, devices):
    shift, out = 0, 0
    for group in stage_groups(devices):
        if len(group) == 1:
            out = out | (((k >> shift) & 1) * group[0])
            shift += 1
        else:
            out = out | (((k >> shift) & 1) * group[0]) | (((k >> (shift + 1)) & 1) * group[1])
            shift += 2
    return out


def join_kernel(*refs):
    at = 0
    for ref in refs[:-1]:
        refs[-1][at : at + ref.shape[0]] = ref[...]
        at += ref.shape[0]


def join(pieces):
    count = sum(piece.shape[0] for piece in pieces)
    return pl.pallas_call(
        join_kernel,
        out_shape=jax.ShapeDtypeStruct((count,) + pieces[0].shape[1:], pieces[0].dtype),
        compiler_params=plain(8),
    )(*pieces)


def after(value, *others):
    return lax.optimization_barrier((value,) + others)[0]


def layer_normalize(values):
    centre = jnp.mean(values, axis=-1, keepdims=True)
    centred = values - centre
    inverse = lax.rsqrt(jnp.mean(centred * centred, axis=-1, keepdims=True) + EPSILON)
    return centred * inverse, inverse


def norm_back(grad_hat, normed, inverse):
    first = jnp.mean(grad_hat, axis=-1, keepdims=True)
    second = jnp.mean(grad_hat * normed, axis=-1, keepdims=True)
    return inverse * (grad_hat - first - normed * second)


def whole(shape):
    return pl.BlockSpec(shape, lambda *_: (0,) * len(shape))


def once(shape):
    return pl.BlockSpec(shape, lambda *_: (0,) * len(shape), pipeline_mode=pl.Buffered(1))


def per_sample(shape, begin=0):
    return pl.BlockSpec((1,) + shape, lambda s, *_: (s + begin,) + (0,) * len(shape))


def anywhere():
    return pl.BlockSpec(memory_space=pl.ANY)


def params(limit, axes=1):
    return pltpu.CompilerParams(
        dimension_semantics=("arbitrary",) * axes, vmem_limit_bytes=limit * MIB
    )


def plain(limit):
    return pltpu.CompilerParams(vmem_limit_bytes=limit * MIB)


def bias_kernel(nbr_ref, bias_ref):
    table, count = bias_ref.shape
    height = 2 * BLOCK
    row = lax.broadcasted_iota(jnp.int32, (height, count), 0)
    slots = nbr_ref[...]

    def block(i, _):
        begin = pl.multiple_of(i * height, height)
        total = jnp.zeros((height, count), F32)
        for j in range(slots.shape[0]):
            total = total + jnp.where(row == slots[j : j + 1, :] - begin, 1.0, 0.0)
        bias_ref[pl.ds(begin, height), :] = jnp.where(
            total > 0.0, jnp.log2(jnp.maximum(total, 1.0)), -1e30
        )
        return 0

    lax.fori_loop(0, table // height, block, 0)


def slot_bias(neighbours, table):
    return pl.pallas_call(
        bias_kernel,
        out_shape=jax.ShapeDtypeStruct((table, neighbours.shape[0]), F32),
        compiler_params=plain(8),
    )(neighbours.T)


def pick_rows(nodes_ref, send_ref, out_refs):
    samples, count, _ = nodes_ref.shape
    each = send_ref.shape[1]
    lanes = lax.broadcasted_iota(jnp.int32, (each, count), 1)
    columns = send_ref[...].T
    for d, out_ref in enumerate(out_refs):
        chosen = jnp.where(lanes == columns[:, d : d + 1], 1.0, 0.0).astype(BF16)
        for s in range(samples):
            out_ref[s] = product(chosen, nodes_ref[s]).astype(BF16)


def blocks_of(ref):
    height, width = ref.shape
    for r in range(0, height, BLOCK):
        for c in range(0, width, 128):
            yield slice(r, r + BLOCK), slice(c, c + 128)


def pack_shards(weights, first_ref, second_ref):
    wq, wk, wv, cw, cb, wo, wu, bu, wd, bd = weights
    for source, ref in (((wq, wk, wv), first_ref), ((wu, wd, wo), second_ref)):
        at = 0
        for part in source:
            for rows, cols in blocks_of(part):
                ref[0, at : at + BLOCK, :] = part[rows, cols]
                at += BLOCK
        ref[0, at : at + BLOCK, :] = jnp.zeros((BLOCK, 128), BF16)
    at = first_ref.shape[1] - BLOCK
    first_ref[0, at : at + BLOCK, 0 : cw.shape[1]] = cw[...]
    first_ref[0, at : at + 1, cb.shape[1] :] = cb[...]
    at = second_ref.shape[1] - BLOCK
    for row, part in enumerate((bu, bd)):
        step = part.shape[1]
        for c in range(0, 128, step):
            second_ref[0, at + row : at + row + 1, c : c + step] = part[...]


def begin_kernel(*refs, ways, given):
    nodes_ref, send_ref = refs[:2]
    weights, out_refs = refs[2 : 2 + given], refs[2 + given : 2 + given + ways]
    pick_rows(nodes_ref, send_ref, out_refs)
    if weights:
        pack_shards(weights, *refs[-2:])


def begin(nodes, send_rows, weights=()):
    samples, _, width = nodes.shape
    ways, each = send_rows.shape
    weights = [w if w.ndim == 2 else w[None] for w in weights]
    shards = []
    if weights:
        wq, wk, wv, _, _, wo, wu, _, wd, _ = weights
        for group in ((wq, wk, wv), (wo, wu, wd)):
            rows = sum(w.size for w in group) // 128 + BLOCK
            shards.append(jax.ShapeDtypeStruct((1, rows, 128), BF16))
    return pl.pallas_call(
        lambda *refs: begin_kernel(*refs, ways=ways, given=len(weights)),
        out_shape=[jax.ShapeDtypeStruct((samples, each, width), BF16)] * ways + shards,
        compiler_params=plain(60),
    )(nodes, send_rows, *weights)


def spread(rows, step, width):
    reps = jnp.concatenate([rows] * (width // 128), axis=1)
    lane = lax.broadcasted_iota(jnp.int32, reps.shape, 1)
    row = lax.broadcasted_iota(jnp.int32, reps.shape, 0)
    return jnp.sum(jnp.where(lane // step == row, reps, 0.0), axis=0, keepdims=True)


def place(source, k, shard, targets):
    at = 0
    for ref, height in targets:
        for r in range(0, height, BLOCK):
            rows = pl.ds(pl.multiple_of(shard * height + r, BLOCK), BLOCK)
            for c in range(0, ref.shape[1], 128):
                ref[rows, c : c + 128] = source[k, at : at + BLOCK, :]
                at += BLOCK
    return at


def shards_of(pieces):
    at = 0
    for ref in pieces:
        for k in range(ref.shape[0]):
            yield at + k, ref, k
        at += ref.shape[0]


def place_first(me_ref, pieces, code_ref, wq_ref, wk_ref, wv_ref, mod_ref, raw):
    devices = sum(ref.shape[0] for ref in pieces)
    samples = code_ref.shape[1]
    width = wq_ref.shape[1]
    step = 4 * width // devices
    lane = lax.broadcasted_iota(jnp.int32, (BLOCK, 128), 1)
    code = [jnp.where(lane < 64, code_ref[:, s : s + 1], 1.0) for s in range(samples)]
    for k, source, i in shards_of(pieces):
        shard = me_ref[0] ^ relative(k, devices)
        targets = ((wq_ref, BLOCK), (wk_ref, BLOCK), (wv_ref, BLOCK))
        at = place(source, i, shard, targets)
        cond = source[i, at : at + BLOCK, :].astype(F32)
        for s in range(samples):
            value = jnp.sum(cond * code[s], axis=0, keepdims=True)
            raw[s, pl.ds(shard, 1), :] = value + pltpu.roll(value, 64, 1)
    each = devices // 4
    for s in range(samples):
        for kind in range(4):
            value = spread(raw[s, kind * each : (kind + 1) * each, :], step, width)
            mod_ref[s, kind : kind + 1, :] = value + 1.0 if kind % 2 == 0 else value


def place_second(me_ref, pieces, wo_ref, wu_ref, wd_ref, bu_ref, bd_ref, raw):
    devices = sum(ref.shape[0] for ref in pieces)
    width = wo_ref.shape[1]
    hidden = wu_ref.shape[1]
    for k, source, i in shards_of(pieces):
        shard = me_ref[0] ^ relative(k, devices)
        targets = ((wu_ref, BLOCK), (wd_ref, hidden // devices), (wo_ref, BLOCK))
        at = place(source, i, shard, targets)
        extra = source[i, at : at + BLOCK, :].astype(F32)
        raw[0, pl.ds(shard, 1), :] = extra[0:1]
        raw[1, pl.ds(shard, 1), :] = extra[1:2]
    each = devices // (hidden // width)
    for c in range(hidden // width):
        bu_ref[:, c * width : (c + 1) * width] = spread(
            raw[0, c * each : (c + 1) * each, :], hidden // devices, width
        )
    bd_ref[...] = spread(raw[1], width // devices, width)


def packs(width, devices):
    return width == devices * BLOCK


def gather_plain(wq, wk, wv, cond_weight, cond_bias, noise_code, wo, wu, bu, wd, bd):
    def full(x, axis=0):
        return lax.all_gather(x, AXES, axis=axis, tiled=True)

    mod = jnp.dot(
        noise_code, full(cond_weight, 1).astype(F32), precision=lax.Precision.HIGHEST
    ) + full(cond_bias).astype(F32)
    mod = mod.reshape(noise_code.shape[0], 4, wq.shape[1])
    mod = mod + jnp.array([1.0, 0.0, 1.0, 0.0], F32)[:, None]
    first = (full(wq), full(wk), full(wv), mod)
    biases = (full(bu)[None].astype(F32), full(bd)[None].astype(F32))
    return first, (full(wo), full(wu), full(wd)) + biases


def scatter_plain(sums, axes):
    return [
        lax.psum_scatter(x, AXES, scatter_dimension=axis, tiled=True)
        for x, axis in zip(sums, axes)
    ]


def add_kernel(own_ref, far_ref, *out_refs):
    size = out_refs[0].shape[0]
    for i, out_ref in enumerate(out_refs):
        part = slice(i * size, (i + 1) * size)
        out_ref[...] = own_ref[part] + far_ref[part]


def add_halves(own_half, far_half, parts):
    count, rows, lanes = own_half.shape
    return pl.pallas_call(
        add_kernel,
        out_shape=[jax.ShapeDtypeStruct((count // parts, rows, lanes), BF16)] * parts,
        compiler_params=plain(16),
    )(own_half, far_half)


def add_more_kernel(*refs):
    sources, outs = refs[: -refs[0].shape[0]], refs[-refs[0].shape[0] :]
    for i, out_ref in enumerate(outs):
        total = sources[0][i].astype(F32)
        for ref in sources[1:]:
            total = total + ref[i].astype(F32)
        out_ref[0] = total.astype(BF16)


def add_pieces(pieces):
    count, rows, lanes = pieces[0].shape
    return pl.pallas_call(
        add_more_kernel,
        out_shape=[jax.ShapeDtypeStruct((1, rows, lanes), BF16)] * count,
        compiler_params=plain(8),
    )(*pieces)


def last_kernel(*refs, pieces, first):
    me_ref = refs[0]
    sources, outs = refs[1 : 1 + pieces], refs[1 + pieces :]
    position = me_ref[0]

    def total(at, height):
        value = sources[0][0, at : at + height, :].astype(F32)
        for ref in sources[1:]:
            value = value + ref[0, at : at + height, :].astype(F32)
        return value

    at = 0
    for ref in outs[:3]:
        for rows, cols in blocks_of(ref):
            ref[rows, cols] = total(at, BLOCK)
            at += BLOCK
    if first:
        cond = total(at, BLOCK)
        step = outs[3].shape[1]
        begin = lax.rem(position * step, 128)
        outs[3][...] = pltpu.roll(cond, 128 - begin, 1)[:, 0:step]
        bias = total(at + BLOCK, BLOCK)
        outs[4][...] = pltpu.roll(bias, 128 - begin, 1)[0:1, 0:step]
    else:
        last = total(at, BLOCK)
        for row, ref in enumerate(outs[3:]):
            step = ref.shape[1]
            begin = lax.rem(position * step, 128)
            ref[...] = pltpu.roll(last, 128 - begin, 1)[row : row + 1, 0:step]


def last_sum(me, pieces, shapes, first):
    return pl.pallas_call(
        lambda *refs: last_kernel(*refs, pieces=len(pieces), first=first),
        out_shape=[jax.ShapeDtypeStruct(shape, F32) for shape in shapes],
        in_specs=[smem()] + [pl.BlockSpec(memory_space=pltpu.VMEM)] * len(pieces),
        compiler_params=plain(60),
    )(me, *pieces)


def smem():
    return pl.BlockSpec(memory_space=pltpu.SMEM)


def attend_kernel(*refs, pieces):
    nodes_ref, h0, h1, h2, h3, bias_ref = refs[:6]
    act_ref, q_ref, k_ref, v_ref, p_ref, att_ref = refs[-6:]
    placed = pieces == 0
    if placed:
        mod_ref, wq_ref, wk_ref, wv_ref = refs[6:10]
    else:
        me_ref, code_ref = refs[6:8]
        shards = refs[8 : 8 + pieces]
        wq_ref, wk_ref, wv_ref, mod_ref = refs[8 + pieces : 12 + pieces]
        raw = refs[-1]
        act_ref, q_ref, k_ref, v_ref, p_ref, att_ref = refs[-7:-1]

        @pl.when(pl.program_id(0) == 0)
        def _():
            place_first(me_ref, shards, code_ref, wq_ref, wk_ref, wv_ref, mod_ref, raw)

    count = nodes_ref.shape[1]
    each = h0.shape[1]
    width = nodes_ref.shape[2]
    at = 0 if placed else pl.program_id(0)
    scale, shift = mod_ref[at, 0:1, :], mod_ref[at, 1:2, :]

    def activate(rows):
        hat, _ = layer_normalize(rows.astype(F32))
        return (hat * scale + shift).astype(BF16)

    act_ref[0, 0:count, :] = activate(nodes_ref[0])
    for d, ref in enumerate((h0, h1, h2, h3)):
        at = count + d * each
        act_ref[0, at : at + each, :] = activate(ref[0])
    act = act_ref[0]
    q_ref[0] = product(act[0:count], wq_ref[...]).astype(BF16)
    k_ref[0] = product(act, wk_ref[...]).astype(BF16)
    v_ref[0] = product(act, wv_ref[...]).astype(BF16)
    factor = math.log2(math.e) * HEAD ** (-0.5)
    heads = [slice(h * HEAD, (h + 1) * HEAD) for h in range(width // HEAD)]
    following = product_t(k_ref[0, :, heads[0]], q_ref[0, :, heads[0]])
    for h, cols in enumerate(heads):
        raw_scores = following
        if h + 1 < len(heads):
            following = product_t(k_ref[0, :, heads[h + 1]], q_ref[0, :, heads[h + 1]])
        scores = raw_scores * factor + bias_ref[...]
        top = jnp.max(scores, axis=0, keepdims=True)
        expo = jnp.exp2(scores - top)
        total = jnp.sum(expo, axis=0, keepdims=True)
        probs = (expo * (1.0 / total)).astype(BF16)
        p_ref[0, h] = probs
        mixed = product(v_ref[0, :, cols].T, probs)
        att_ref[0, :, cols] = mixed.T.astype(BF16)


def attend(nodes, halos, bias, begin, steps, weights=None, shards=None, buffers=()):
    samples, count, width = nodes.shape
    table = bias.shape[0]
    heads = width // HEAD
    each = halos[0].shape[1]
    square = jax.ShapeDtypeStruct((width, width), BF16)
    mod_shape = jax.ShapeDtypeStruct((samples, 4, width), F32)

    def tile(*shape):
        return per_sample(shape, begin)

    def out(*shape):
        return jax.ShapeDtypeStruct((samples,) + shape, BF16)

    in_specs = [tile(count, width)] + [tile(each, width)] * 4 + [once((table, count))]
    args = [nodes, *halos, bias]
    out_specs, out_shape, scratch = [], [], []
    if shards is None:
        wq, wk, wv, mod = weights
        in_specs += [tile(4, width)] + [once((width, width))] * 3
        args += [mod, wq, wk, wv]
    else:
        me, code, *pieces = shards
        in_specs += [smem(), once(code.shape)] + [once(x.shape) for x in pieces]
        args += [me, code] + pieces
        out_specs += [once((width, width))] * 3 + [once(mod_shape.shape)]
        out_shape += [square] * 3 + [mod_shape]
        devices = sum(x.shape[0] for x in pieces)
        scratch = [pltpu.VMEM((samples, devices, 128), F32)]
    tables = [(table, width), (count, width), (table, width), (table, width)]
    tables += [(heads, table, count), (count, width)]
    aliases = {len(args) + i: len(out_shape) + i for i in range(len(buffers))}
    kept = len(buffers)
    first, count_in = 0 if shards is None else len(shards) - 2, len(args)
    return pl.pallas_call(
        lambda *refs: attend_kernel(*refs[:count_in], *refs[count_in + kept :], pieces=first),
        grid=(steps,),
        in_specs=in_specs + [anywhere()] * kept,
        out_specs=out_specs + [tile(*shape) for shape in tables],
        out_shape=out_shape + [out(*shape) for shape in tables],
        scratch_shapes=scratch,
        input_output_aliases=aliases,
        compiler_params=params(60),
    )(*args, *buffers)


def feed_kernel(*refs, shards):
    me_ref, nodes_ref, att_ref, cot_ref, mod_ref = refs[:5]
    scratch = 6 + (6 if shards else 0)
    up_acc, down_acc, wo_acc, bu_acc, bd_acc, down_rows = refs[len(refs) - 6 :]
    if shards:
        pieces = refs[5 : 5 + shards]
        wo_ref, wu_ref, wd_ref, bu_ref, bd_ref, raw = refs[-12:-6]
        outs = refs[5 + shards : -scratch]

        @pl.when(pl.program_id(0) == 0)
        def _():
            place_second(me_ref, pieces, wo_ref, wu_ref, wd_ref, bu_ref, bd_ref, raw)

    else:
        wo_ref, wu_ref, wd_ref, bu_ref, bd_ref = refs[5:10]
        outs = refs[10:-scratch]
    out_ref, gmid_ref, gatt_ref, gmod_ref = outs[:4]
    sums = outs[4:]
    s = pl.program_id(0)
    count, width = nodes_ref.shape[1:]
    hidden_size = wu_ref.shape[1]
    wide = hidden_size // width

    @pl.when(s == 0)
    def _():
        up_acc[...] = jnp.zeros_like(up_acc)
        down_acc[...] = jnp.zeros_like(down_acc)
        wo_acc[...] = jnp.zeros_like(wo_acc)
        bu_acc[...] = jnp.zeros_like(bu_acc)
        bd_acc[...] = jnp.zeros_like(bd_acc)

    scale, shift = mod_ref[0, 2:3, :], mod_ref[0, 3:4, :]
    attended = att_ref[0]
    cot = cot_ref[0]
    cot_float = cot.astype(F32)
    middle = nodes_ref[0].astype(F32) + product(attended, wo_ref[...])
    hat, inverse = layer_normalize(middle)
    act = (hat * scale + shift).astype(BF16)
    act_t = act.T
    cot_t = cot.T
    result = middle + bd_ref[...]
    grad_act = jnp.zeros((count, width), F32)
    bd_acc[...] += jnp.sum(cot_float, axis=0, keepdims=True)
    for c in range(wide):
        cols = slice(c * width, (c + 1) * width)
        w_up = wu_ref[:, cols]
        w_down = wd_ref[cols, :]
        pre = product(act, w_up) + bu_ref[:, cols]
        gate = 0.5 * jnp.tanh(0.5 * pre) + 0.5
        value = pre * gate
        hidden = value.astype(BF16)
        result = result + product(hidden, w_down)
        down_acc[:, cols] += product(cot_t, hidden)
        grad_pre = product_t(cot, w_down) * (gate + value * (1.0 - gate))
        low_pre = grad_pre.astype(BF16)
        bu_acc[:, cols] += jnp.sum(low_pre.astype(F32), axis=0, keepdims=True)
        up_acc[:, cols] += product(act_t, low_pre)
        grad_act = grad_act + product_t(low_pre, w_up)
    out_ref[0] = result.astype(BF16)
    gmod_ref[0, 0:1, :] = jnp.sum(grad_act * hat, axis=0, keepdims=True)
    gmod_ref[0, 1:2, :] = jnp.sum(grad_act, axis=0, keepdims=True)
    grad_middle = cot_float + norm_back(grad_act * scale, hat, inverse)
    gmid_ref[0] = grad_middle
    branch = grad_middle.astype(BF16)
    wo_acc[...] += product(attended.T, branch)
    gatt_ref[0] = product_t(branch, wo_ref[...]).astype(BF16)

    @pl.when(s == pl.num_programs(0) - 1)
    def _():
        for c in range(wide):
            cols = slice(c * width, (c + 1) * width)
            down_rows[cols, :] = down_acc[:, cols].T
        if len(sums) > 2:
            for ref, value in zip(sums, (up_acc, down_rows, wo_acc, bu_acc, bd_acc)):
                ref[...] = value[...]
            return
        low_ref, high_ref = sums
        half = low_ref.shape[0]
        devices = 2 * half
        down = hidden_size // devices

        for part, ref in enumerate((low_ref, high_ref)):

            def pack(i, _, part=part, ref=ref):
                shard = me_ref[0] ^ relative(i + part * half, devices)
                rows = pl.ds(pl.multiple_of(shard * BLOCK, BLOCK), BLOCK)
                at = 0
                for c in range(0, hidden_size, 128):
                    ref[i, at : at + BLOCK, :] = up_acc[rows, c : c + 128].astype(BF16)
                    at += BLOCK
                for r in range(0, down, BLOCK):
                    some = pl.ds(pl.multiple_of(shard * down + r, BLOCK), BLOCK)
                    for c in range(0, width, 128):
                        ref[i, at : at + BLOCK, :] = down_rows[some, c : c + 128].astype(BF16)
                        at += BLOCK
                for c in range(0, width, 128):
                    ref[i, at : at + BLOCK, :] = wo_acc[rows, c : c + 128].astype(BF16)
                    at += BLOCK
                up_tile = pl.multiple_of(((shard * down) // 128) * 128, 128)
                down_tile = pl.multiple_of(((shard * (width // devices)) // 128) * 128, 128)
                row = lax.broadcasted_iota(jnp.int32, (BLOCK, 128), 0)
                ref[i, at : at + BLOCK, :] = jnp.where(
                    row == 0, bu_acc[:, pl.ds(up_tile, 128)], bd_acc[:, pl.ds(down_tile, 128)]
                ).astype(BF16)
                return 0

            lax.fori_loop(0, half, pack, 0)


def feed(me, nodes, attended, cot, mod, hidden, devices, weights=None, shards=None):
    samples, count, width = nodes.shape
    tile = per_sample((count, width))
    scratch = [
        pltpu.VMEM((width, hidden), F32),
        pltpu.VMEM((width, hidden), F32),
        pltpu.VMEM((width, width), F32),
        pltpu.VMEM((1, hidden), F32),
        pltpu.VMEM((1, width), F32),
        pltpu.VMEM((hidden, width), F32),
    ]
    if shards:
        rows = shards[0].shape[1]
        sums = [jax.ShapeDtypeStruct((devices // 2, rows, 128), BF16)] * 2
        extra = list(shards)
        scratch = [
            pltpu.VMEM((width, width), BF16),
            pltpu.VMEM((width, hidden), BF16),
            pltpu.VMEM((hidden, width), BF16),
            pltpu.VMEM((1, hidden), F32),
            pltpu.VMEM((1, width), F32),
            pltpu.VMEM((2, devices, 128), F32),
        ] + scratch
    else:
        shapes = ((width, hidden), (hidden, width), (width, width), (1, hidden), (1, width))
        sums = [jax.ShapeDtypeStruct(shape, F32) for shape in shapes]
        extra = list(weights)
    return pl.pallas_call(
        lambda *refs: feed_kernel(*refs, shards=len(shards or ())),
        grid=(samples,),
        in_specs=[smem(), tile, tile, tile, per_sample((4, width))]
        + [once(x.shape) for x in extra],
        out_specs=[tile, tile, tile, per_sample((2, width))] + [once(x.shape) for x in sums],
        out_shape=[
            jax.ShapeDtypeStruct((samples, count, width), BF16),
            jax.ShapeDtypeStruct((samples, count, width), F32),
            jax.ShapeDtypeStruct((samples, count, width), BF16),
            jax.ShapeDtypeStruct((samples, 2, width), F32),
        ]
        + sums,
        scratch_shapes=scratch,
        compiler_params=params(60),
    )(me, nodes, attended, cot, mod, *extra)


def attend_back_kernel(*refs, started, last):
    me_ref, nodes_ref, h0, h1, h2, h3, code_ref, gmod_ref = refs[:8]
    act_ref, q_ref, k_ref, v_ref, p_ref, gatt_ref, wq_ref, wk_ref, wv_ref = refs[8:17]
    gmid_ref, mod_ref = refs[17:19]
    rest = refs[19:]
    if started:
        before, rest = rest[:5], rest[10:]
    base_ref, b0, b1, b2, b3 = rest[:5]
    gq, gk, gv = rest[-3:]
    if last:
        outs = rest[5:-8]
        sums = q_acc, k_acc, v_acc, cond_acc, bias_acc = rest[-8:-3]
    else:
        sums = q_acc, k_acc, v_acc, cond_acc, bias_acc = rest[5:10]
    s = pl.program_id(0)
    count, width = nodes_ref.shape[1:]
    each = h0.shape[1]
    inv_root = HEAD ** (-0.5)

    @pl.when(s == 0)
    def _():
        for i, ref in enumerate(sums):
            ref[...] = before[i][...] if started else jnp.zeros_like(ref)

    for h in range(width // HEAD):
        cols = slice(h * HEAD, (h + 1) * HEAD)
        probs = p_ref[0, h]
        grad_att = gatt_ref[0, :, cols]
        keys = k_ref[0, :, cols]
        probs_float = probs.astype(F32)
        grad_probs = product_t(v_ref[0, :, cols], grad_att)
        inner = jnp.sum(probs_float * grad_probs, axis=0, keepdims=True)
        grad_scores = (probs_float * (grad_probs - inner)).astype(BF16)
        gv[:, cols] = product(probs, grad_att).astype(BF16)
        gk[:, cols] = (product(grad_scores, q_ref[0, :, cols]) * inv_root).astype(BF16)
        gq[:, cols] = (product(keys.T, grad_scores) * inv_root).T.astype(BF16)

    act_t = act_ref[0].T
    q_acc[...] += product(act_t[:, 0:count], gq[...])
    k_acc[...] += product(act_t, gk[...])
    v_acc[...] += product(act_t, gv[...])
    grad_act = (
        product_t(gq[...], wq_ref[...])
        + product_t(gk[0:count, :], wk_ref[...])
        + product_t(gv[0:count, :], wv_ref[...])
    )
    grad_far = product_t(gk[count:, :], wk_ref[...]) + product_t(gv[count:, :], wv_ref[...])
    hat, inverse = layer_normalize(nodes_ref[0].astype(F32))
    base_ref[0] = gmid_ref[0] + norm_back(grad_act * mod_ref[0, 0:1, :], hat, inverse)
    scale_sum = jnp.sum(grad_act * hat, axis=0, keepdims=True)
    shift_sum = jnp.sum(grad_act, axis=0, keepdims=True)
    for d, (far, back) in enumerate(zip((h0, h1, h2, h3), (b0, b1, b2, b3))):
        part = grad_far[d * each : (d + 1) * each]
        far_hat, _ = layer_normalize(far[0].astype(F32))
        scale_sum = scale_sum + jnp.sum(part * far_hat, axis=0, keepdims=True)
        shift_sum = shift_sum + jnp.sum(part, axis=0, keepdims=True)
        back[0] = part.astype(BF16)
    kinds = (scale_sum, shift_sum, gmod_ref[0, 0:1, :], gmod_ref[0, 1:2, :])
    code = code_ref[0]
    for kind, value in enumerate(kinds):
        cols = slice(kind * width, (kind + 1) * width)
        cond_acc[:, cols] += code * value
        bias_acc[:, cols] += value
    if not last:
        return

    @pl.when(s == pl.num_programs(0) - 1)
    def _():
        if len(outs) > 2:
            for ref, value in zip(outs, sums):
                ref[...] = value[...]
            return
        half = outs[0].shape[0]
        devices = 2 * half
        for part, ref in enumerate(outs):

            def pack(i, _, part=part, ref=ref):
                shard = me_ref[0] ^ relative(i + part * half, devices)
                rows = pl.ds(pl.multiple_of(shard * BLOCK, BLOCK), BLOCK)
                at = 0
                for value in (q_acc, k_acc, v_acc):
                    for c in range(0, width, 128):
                        ref[i, at : at + BLOCK, :] = value[rows, c : c + 128].astype(BF16)
                        at += BLOCK
                tile = pl.multiple_of(((shard * (4 * width // devices)) // 128) * 128, 128)
                ref[i, at : at + BLOCK, :] = cond_acc[:, pl.ds(tile, 128)].astype(BF16)
                at += BLOCK
                ref[i, at : at + BLOCK, :] = jnp.broadcast_to(
                    bias_acc[:, pl.ds(tile, 128)], (BLOCK, 128)
                ).astype(BF16)
                return 0

            lax.fori_loop(0, half, pack, 0)


def attend_back(
    me,
    nodes,
    halos,
    noise_code,
    gmod,
    saved,
    gatt,
    wq,
    wk,
    wv,
    gmid,
    mod,
    devices,
    begin,
    steps,
    carried=(),
):
    samples, count, width = nodes.shape
    act, queries, keys, values, probs = saved
    table = act.shape[1]
    heads = width // HEAD
    each = halos[0].shape[1]
    half = devices // 2
    codes = noise_code.shape[1]
    code = noise_code[:, :, None]
    last = begin + steps == samples
    shapes = [(width, width)] * 3 + [(codes, 4 * width), (1, 4 * width)]
    sums = [jax.ShapeDtypeStruct(shape, F32) for shape in shapes]
    scratch = [
        pltpu.VMEM((count, width), BF16),
        pltpu.VMEM((table, width), BF16),
        pltpu.VMEM((table, width), BF16),
    ]
    if last:
        scratch = [pltpu.VMEM(shape, F32) for shape in shapes] + scratch
        if packs(width, devices):
            rows = 3 * BLOCK * width // 128 + 2 * BLOCK
            sums = [jax.ShapeDtypeStruct((half, rows, 128), BF16)] * 2

    def tile(*shape):
        return per_sample(shape, begin)

    args = [me, nodes, *halos, code, gmod, act, queries, keys, values, probs, gatt, wq, wk, wv]
    args += [gmid, mod]
    aliases = {len(args) + 5 + i: i for i in range(5)} if carried else {}
    return pl.pallas_call(
        lambda *refs: attend_back_kernel(*refs, started=bool(carried), last=last),
        grid=(steps,),
        in_specs=[smem(), tile(count, width)]
        + [tile(each, width)] * 4
        + [tile(codes, 1), tile(2, width)]
        + [tile(table, width), tile(count, width), tile(table, width), tile(table, width)]
        + [tile(heads, table, count), tile(count, width)]
        + [once((width, width))] * 3
        + [tile(count, width), tile(4, width)]
        + ([once(shape) for shape in shapes] + [anywhere()] * 5 if carried else []),
        out_specs=[tile(count, width)]
        + [tile(each, width)] * 4
        + [once(x.shape) for x in sums],
        out_shape=[jax.ShapeDtypeStruct((samples, count, width), F32)]
        + [jax.ShapeDtypeStruct((samples, each, width), BF16)] * 4
        + sums,
        scratch_shapes=scratch,
        input_output_aliases=aliases,
        compiler_params=params(46),
    )(*args, *carried)


def finish_kernel(nodes_ref, base_ref, b0, b1, b2, b3, send_ref, mod_ref, out_ref, far):
    count = nodes_ref.shape[1]
    each = b0.shape[1]
    row = lax.broadcasted_iota(jnp.int32, (count, 4 * each), 0)
    chosen = jnp.where(row == send_ref[...], 1.0, 0.0).astype(BF16)
    for d, ref in enumerate((b0, b1, b2, b3)):
        far[d * each : (d + 1) * each, :] = ref[0]
    grad_act = product(chosen, far[...])
    hat, inverse = layer_normalize(nodes_ref[0].astype(F32))
    out_ref[0] = base_ref[0] + norm_back(grad_act * mod_ref[0, 0:1, :], hat, inverse)


def finish(nodes, base, backs, send_rows, mod):
    samples, count, width = nodes.shape
    each = backs[0].shape[1]
    picks = send_rows.size
    tile = per_sample((count, width))
    return pl.pallas_call(
        finish_kernel,
        grid=(samples,),
        in_specs=[tile, tile]
        + [per_sample((each, width))] * 4
        + [whole((1, picks)), per_sample((4, width))],
        out_specs=tile,
        out_shape=jax.ShapeDtypeStruct((samples, count, width), F32),
        scratch_shapes=[pltpu.VMEM((picks, width), BF16)],
        compiler_params=params(16),
    )(nodes, base, *backs, send_rows.reshape(1, picks), mod)


def layer(
    nodes,
    neighbours,
    send_rows,
    noise_code,
    w_query,
    w_key,
    w_value,
    w_out,
    w_up,
    b_up,
    w_down,
    b_down,
    cond_weight,
    cond_bias,
    cotangent,
):
    devices = lax.axis_size("patch") * lax.axis_size("sample")
    position = lax.axis_index("patch") * lax.axis_size("sample") + lax.axis_index("sample")
    me = position.astype(jnp.int32).reshape(1)
    width = nodes.shape[2]
    hidden = w_up.shape[1]
    offsets = (1, -1, STRIDE, -STRIDE)

    samples, count, _ = nodes.shape
    table = count + send_rows.size
    if not packs(width, devices):
        return plain_body(
            me,
            nodes,
            neighbours,
            send_rows,
            noise_code,
            (w_query, w_key, w_value, cond_weight, cond_bias, noise_code),
            (w_out, w_up, b_up, w_down, b_down),
            cotangent,
            devices,
        )
    z_side, plane, (core,) = stage_groups(devices)

    def swaps(pieces, group):
        return [swap(x, c, devices) for x, c in zip(pieces, group)]

    def cores(pieces):
        return [swap(x, core, devices) for x in pieces]

    def shifts(blocks, sign):
        return [from_behind(x, sign * o) for x, o in zip(blocks, offsets)]

    *sends, first, second = begin(
        nodes,
        send_rows,
        (w_query, w_key, w_value, cond_weight, cond_bias, w_out, w_up, b_up, w_down, b_down),
    )
    far = swaps([first] * 3, z_side)
    far_second = swaps([second] * 3, z_side)
    halos = shifts(sends, 1)
    held = join([first] + far)
    low_first = [held] + swaps([held] * 3, plane)
    bias = slot_bias(neighbours, table)
    high_first = cores(low_first)
    held_second = join([second] + far_second)
    low_second = [held_second] + swaps([held_second] * 3, plane)
    split = samples - 1
    wq, wk, wv, mod, *saved = attend(
        nodes,
        halos,
        after(bias, held_second),
        0,
        split,
        shards=[me, noise_code.T] + low_first + high_first,
    )
    high_second = cores(low_second)
    *saved, attended = attend(
        nodes,
        halos,
        bias,
        split,
        samples - split,
        weights=(wq, wk, wv, mod),
        buffers=saved,
    )
    result, gmid, gatt, gmod, low_feed, high_feed = feed(
        me,
        nodes,
        attended,
        cotangent,
        mod,
        hidden,
        devices,
        shards=low_second + high_second,
    )
    back = (me, nodes, halos, noise_code, gmod, saved, gatt, wq, wk, wv, gmid, mod, devices)
    (got_feed,) = cores([high_feed])
    *arrays, s0, s1, s2, s3, s4 = attend_back(*back, 0, 1)
    own_feed, *parts = add_halves(low_feed, got_feed, 4)
    feed_far = swaps(parts, plane)
    carried = (after(s0, own_feed), s1, s2, s3, s4, *arrays)
    base, *rest = attend_back(*back, 1, samples - 1, carried)
    low_proj, high_proj = rest[4:]
    (got_proj,) = cores([high_proj])
    own_feed, *parts = add_pieces([own_feed] + feed_far)
    feed_last = swaps(parts, z_side)
    own_proj, *parts = add_halves(low_proj, got_proj, 4)
    proj_far = swaps(parts, plane)
    backs = shifts(rest[:4], -1)
    own_proj, *parts = add_pieces([own_proj] + proj_far)
    proj_last = swaps(parts, z_side)
    grad_nodes = finish(nodes, base, backs, send_rows, mod)
    down, thin = hidden // devices, width // devices
    grad_up, grad_down, grad_out, grad_b_up, grad_b_down = last_sum(
        me,
        [own_feed] + feed_last,
        ((BLOCK, hidden), (down, width), (BLOCK, width), (1, down), (1, thin)),
        False,
    )
    step = 4 * width // devices
    grad_query, grad_key, grad_value, grad_cond, grad_cond_bias = last_sum(
        me,
        [own_proj] + proj_last,
        ((BLOCK, width),) * 3 + ((BLOCK, step), (1, step)),
        True,
    )
    grad_b_up, grad_b_down, grad_cond_bias = grad_b_up[0], grad_b_down[0], grad_cond_bias[0]
    return (
        result,
        grad_nodes,
        grad_query,
        grad_key,
        grad_value,
        grad_out,
        grad_up,
        grad_b_up,
        grad_down,
        grad_b_down,
        grad_cond,
        grad_cond_bias,
    )


def plain_body(
    me, nodes, neighbours, send_rows, noise_code, first, second, cotangent, devices
):
    samples, count, _ = nodes.shape
    hidden = second[1].shape[1]
    offsets = (1, -1, STRIDE, -STRIDE)
    bias = slot_bias(neighbours, count + send_rows.size)
    sends = begin(nodes, send_rows)
    halos = [from_behind(block, offset) for block, offset in zip(sends, offsets)]
    (wq, wk, wv, mod), weights = gather_plain(*first, *second)
    *saved, attended = attend(nodes, halos, bias, 0, samples, weights=(wq, wk, wv, mod))
    result, gmid, gatt, gmod, *sums = feed(
        me, nodes, attended, cotangent, mod, hidden, devices, weights=weights
    )
    sums[3:] = [x[0] for x in sums[3:]]
    grad_up, grad_down, grad_out, grad_b_up, grad_b_down = scatter_plain(sums, (0,) * 5)
    base, *rest = attend_back(
        me, nodes, halos, noise_code, gmod, saved, gatt, wq, wk, wv, gmid, mod, devices, 0, samples
    )
    backs = [from_behind(block, -offset) for block, offset in zip(rest[:4], offsets)]
    rest[-1] = rest[-1][0]
    grad_query, grad_key, grad_value, grad_cond, grad_cond_bias = scatter_plain(
        rest[4:], (0, 0, 0, 1, 0)
    )
    grad_nodes = finish(nodes, base, backs, send_rows, mod)
    return (
        result,
        grad_nodes,
        grad_query,
        grad_key,
        grad_value,
        grad_out,
        grad_up,
        grad_b_up,
        grad_down,
        grad_b_down,
        grad_cond,
        grad_cond_bias,
    )


def solution(mesh):
    both = P(("patch", "sample"), None)
    flat = P(("patch", "sample"))
    split = P("sample", "patch", None)
    cond = P(None, ("patch", "sample"))
    return jax.shard_map(
        layer,
        mesh=mesh,
        in_specs=(
            split,
            P("patch", None),
            P("patch", None),
            P("sample", None),
            both,
            both,
            both,
            both,
            both,
            flat,
            both,
            flat,
            cond,
            flat,
            split,
        ),
        out_specs=(split, split, both, both, both, both, both, flat, both, flat, cond, flat),
        check_vma=False,
    )
```

```python
import math

import jax
import jax.numpy as jnp
from jax import lax
from jax.experimental import pallas as pl
from jax.experimental.pallas import tpu as pltpu
from jax.sharding import PartitionSpec as P


HEAD = 128
STRIDE = 4
BLOCK = 16
AXES = ("patch", "sample")
EPSILON = 1e-05
F32 = jnp.float32
BF16 = jnp.bfloat16
MIB = 1024 * 1024


def product(left, right):
    return jnp.dot(left, right, preferred_element_type=F32)


def product_t(left, right):
    return lax.dot_general(left, right, (((1,), (1,)), ((), ())), preferred_element_type=F32)


def from_behind(block, distance):
    count = lax.axis_size("patch")
    return lax.ppermute(block, "patch", [((i - distance) % count, i) for i in range(count)])


def swap(block, bits, devices):
    return lax.ppermute(block, AXES, [(i, i ^ bits) for i in range(devices)])


def stage_groups(devices):
    bits = [1 << i for i in reversed(range(devices.bit_length() - 1)) if (1 << i) != 2]
    groups = [bits[i : i + 2] for i in range(0, len(bits), 2)]
    return [combos(g) for g in groups] + [[2]]


def combos(group):
    if len(group) == 1:
        return [group[0]]
    high, low = group
    return [low, high, low | high]


def relative(k, devices):
    shift, out = 0, 0
    for group in stage_groups(devices):
        if len(group) == 1:
            out = out | (((k >> shift) & 1) * group[0])
            shift += 1
        else:
            out = out | (((k >> shift) & 1) * group[0]) | (((k >> (shift + 1)) & 1) * group[1])
            shift += 2
    return out


def join_kernel(*refs):
    at = 0
    for ref in refs[:-1]:
        refs[-1][at : at + ref.shape[0]] = ref[...]
        at += ref.shape[0]


def join(pieces):
    count = sum(piece.shape[0] for piece in pieces)
    return pl.pallas_call(
        join_kernel,
        out_shape=jax.ShapeDtypeStruct((count,) + pieces[0].shape[1:], pieces[0].dtype),
        compiler_params=plain(8),
    )(*pieces)


def after(value, *others):
    return lax.optimization_barrier((value,) + others)[0]


def layer_normalize(values):
    centre = jnp.mean(values, axis=-1, keepdims=True)
    centred = values - centre
    inverse = lax.rsqrt(jnp.mean(centred * centred, axis=-1, keepdims=True) + EPSILON)
    return centred * inverse, inverse


def norm_back(grad_hat, normed, inverse):
    first = jnp.mean(grad_hat, axis=-1, keepdims=True)
    second = jnp.mean(grad_hat * normed, axis=-1, keepdims=True)
    return inverse * (grad_hat - first - normed * second)


def whole(shape):
    return pl.BlockSpec(shape, lambda *_: (0,) * len(shape))


def once(shape):
    return pl.BlockSpec(shape, lambda *_: (0,) * len(shape), pipeline_mode=pl.Buffered(1))


def per_sample(shape, begin=0):
    return pl.BlockSpec((1,) + shape, lambda s, *_: (s + begin,) + (0,) * len(shape))


def anywhere():
    return pl.BlockSpec(memory_space=pl.ANY)


def params(limit, axes=1):
    return pltpu.CompilerParams(
        dimension_semantics=("arbitrary",) * axes, vmem_limit_bytes=limit * MIB
    )


def plain(limit):
    return pltpu.CompilerParams(vmem_limit_bytes=limit * MIB)


def bias_kernel(nbr_ref, bias_ref):
    table, count = bias_ref.shape
    height = 2 * BLOCK
    row = lax.broadcasted_iota(jnp.int32, (height, count), 0)
    slots = nbr_ref[...]

    def block(i, _):
        begin = pl.multiple_of(i * height, height)
        total = jnp.zeros((height, count), F32)
        for j in range(slots.shape[0]):
            total = total + jnp.where(row == slots[j : j + 1, :] - begin, 1.0, 0.0)
        bias_ref[pl.ds(begin, height), :] = jnp.where(
            total > 0.0, jnp.log2(jnp.maximum(total, 1.0)), -1e30
        )
        return 0

    lax.fori_loop(0, table // height, block, 0)


def slot_bias(neighbours, table):
    return pl.pallas_call(
        bias_kernel,
        out_shape=jax.ShapeDtypeStruct((table, neighbours.shape[0]), F32),
        compiler_params=plain(8),
    )(neighbours.T)


def pick_rows(nodes_ref, send_ref, out_refs):
    samples, count, _ = nodes_ref.shape
    each = send_ref.shape[1]
    lanes = lax.broadcasted_iota(jnp.int32, (each, count), 1)
    columns = send_ref[...].T
    for d, out_ref in enumerate(out_refs):
        chosen = jnp.where(lanes == columns[:, d : d + 1], 1.0, 0.0).astype(BF16)
        for s in range(samples):
            out_ref[s] = product(chosen, nodes_ref[s]).astype(BF16)


def blocks_of(ref):
    height, width = ref.shape
    for r in range(0, height, BLOCK):
        for c in range(0, width, 128):
            yield slice(r, r + BLOCK), slice(c, c + 128)


def pack_shards(weights, first_ref, second_ref):
    wq, wk, wv, cw, cb, wo, wu, bu, wd, bd = weights
    for source, ref in (((wq, wk, wv), first_ref), ((wu, wd, wo), second_ref)):
        at = 0
        for part in source:
            for rows, cols in blocks_of(part):
                ref[0, at : at + BLOCK, :] = part[rows, cols]
                at += BLOCK
        ref[0, at : at + BLOCK, :] = jnp.zeros((BLOCK, 128), BF16)
    at = first_ref.shape[1] - BLOCK
    first_ref[0, at : at + BLOCK, 0 : cw.shape[1]] = cw[...]
    first_ref[0, at : at + 1, cb.shape[1] :] = cb[...]
    at = second_ref.shape[1] - BLOCK
    for row, part in enumerate((bu, bd)):
        step = part.shape[1]
        for c in range(0, 128, step):
            second_ref[0, at + row : at + row + 1, c : c + step] = part[...]


def begin_kernel(*refs, ways, given):
    nodes_ref, send_ref = refs[:2]
    weights, out_refs = refs[2 : 2 + given], refs[2 + given : 2 + given + ways]
    pick_rows(nodes_ref, send_ref, out_refs)
    if weights:
        pack_shards(weights, *refs[-2:])


def begin(nodes, send_rows, weights=()):
    samples, _, width = nodes.shape
    ways, each = send_rows.shape
    weights = [w if w.ndim == 2 else w[None] for w in weights]
    shards = []
    if weights:
        wq, wk, wv, _, _, wo, wu, _, wd, _ = weights
        for group in ((wq, wk, wv), (wo, wu, wd)):
            rows = sum(w.size for w in group) // 128 + BLOCK
            shards.append(jax.ShapeDtypeStruct((1, rows, 128), BF16))
    return pl.pallas_call(
        lambda *refs: begin_kernel(*refs, ways=ways, given=len(weights)),
        out_shape=[jax.ShapeDtypeStruct((samples, each, width), BF16)] * ways + shards,
        compiler_params=plain(60),
    )(nodes, send_rows, *weights)


def spread(rows, step, width):
    reps = jnp.concatenate([rows] * (width // 128), axis=1)
    lane = lax.broadcasted_iota(jnp.int32, reps.shape, 1)
    row = lax.broadcasted_iota(jnp.int32, reps.shape, 0)
    return jnp.sum(jnp.where(lane // step == row, reps, 0.0), axis=0, keepdims=True)


def place(source, k, shard, targets):
    at = 0
    for ref, height in targets:
        for r in range(0, height, BLOCK):
            rows = pl.ds(pl.multiple_of(shard * height + r, BLOCK), BLOCK)
            for c in range(0, ref.shape[1], 128):
                ref[rows, c : c + 128] = source[k, at : at + BLOCK, :]
                at += BLOCK
    return at


def for_shards(pieces, take, arriving=()):
    at = 0
    for n, ref in enumerate(pieces):
        if arriving:
            arriving[n].wait()

        def step(i, _, ref=ref, at=at):
            take(at + i, ref, i)
            return 0

        lax.fori_loop(0, ref.shape[0], step, 0, unroll=2)
        at += ref.shape[0]


def place_first(me_ref, pieces, code_ref, wq_ref, wk_ref, wv_ref, mod_ref, raw):
    devices = sum(ref.shape[0] for ref in pieces)
    samples = code_ref.shape[0]
    width = wq_ref.shape[1]
    step = 4 * width // devices
    lane = lax.broadcasted_iota(jnp.int32, (BLOCK, 128), 1)
    columns = code_ref[...].T
    code = [jnp.where(lane < 64, columns[:, s : s + 1], 1.0) for s in range(samples)]

    def take(k, source, i):
        shard = me_ref[0] ^ relative(k, devices)
        targets = ((wq_ref, BLOCK), (wk_ref, BLOCK), (wv_ref, BLOCK))
        at = place(source, i, shard, targets)
        cond = source[i, at : at + BLOCK, :].astype(F32)
        for s in range(samples):
            value = jnp.sum(cond * code[s], axis=0, keepdims=True)
            raw[s, pl.ds(shard, 1), :] = value + pltpu.roll(value, 64, 1)

    for_shards(pieces, take)
    each = devices // 4
    for s in range(samples):
        for kind in range(4):
            value = spread(raw[s, kind * each : (kind + 1) * each, :], step, width)
            mod_ref[s, kind : kind + 1, :] = value + 1.0 if kind % 2 == 0 else value


def place_second(me_ref, pieces, arriving, wo_ref, wu_ref, wd_ref, bu_ref, bd_ref, raw):
    devices = sum(ref.shape[0] for ref in pieces)
    width = wo_ref.shape[1]
    hidden = wu_ref.shape[1]

    def take(k, source, i):
        shard = me_ref[0] ^ relative(k, devices)
        targets = ((wu_ref, BLOCK), (wd_ref, hidden // devices), (wo_ref, BLOCK))
        at = place(source, i, shard, targets)
        extra = source[i, at : at + BLOCK, :].astype(F32)
        raw[0, pl.ds(shard, 1), :] = extra[0:1]
        raw[1, pl.ds(shard, 1), :] = extra[1:2]

    for_shards(pieces, take, arriving)
    each = devices // (hidden // width)
    for c in range(hidden // width):
        bu_ref[:, c * width : (c + 1) * width] = spread(
            raw[0, c * each : (c + 1) * each, :], hidden // devices, width
        )
    bd_ref[...] = spread(raw[1], width // devices, width)


def packs(width, devices):
    return width == devices * BLOCK


def gather_plain(wq, wk, wv, cond_weight, cond_bias, noise_code, wo, wu, bu, wd, bd):
    def full(x, axis=0):
        return lax.all_gather(x, AXES, axis=axis, tiled=True)

    mod = jnp.dot(
        noise_code, full(cond_weight, 1).astype(F32), precision=lax.Precision.HIGHEST
    ) + full(cond_bias).astype(F32)
    mod = mod.reshape(noise_code.shape[0], 4, wq.shape[1])
    mod = mod + jnp.array([1.0, 0.0, 1.0, 0.0], F32)[:, None]
    first = (full(wq), full(wk), full(wv), mod)
    biases = (full(bu)[None].astype(F32), full(bd)[None].astype(F32))
    return first, (full(wo), full(wu), full(wd)) + biases


def scatter_plain(sums, axes):
    return [
        lax.psum_scatter(x, AXES, scatter_dimension=axis, tiled=True)
        for x, axis in zip(sums, axes)
    ]


def add_kernel(own_ref, far_ref, *out_refs):
    size = out_refs[0].shape[0]
    for i, out_ref in enumerate(out_refs):
        part = slice(i * size, (i + 1) * size)
        out_ref[...] = own_ref[part] + far_ref[part]


def add_halves(own_half, far_half, parts):
    count, rows, lanes = own_half.shape
    return pl.pallas_call(
        add_kernel,
        out_shape=[jax.ShapeDtypeStruct((count // parts, rows, lanes), BF16)] * parts,
        compiler_params=plain(16),
    )(own_half, far_half)


def add_more_kernel(*refs):
    sources, outs = refs[: -refs[0].shape[0]], refs[-refs[0].shape[0] :]
    for i, out_ref in enumerate(outs):
        total = sources[0][i].astype(F32)
        for ref in sources[1:]:
            total = total + ref[i].astype(F32)
        out_ref[0] = total.astype(BF16)


def add_pieces(pieces):
    count, rows, lanes = pieces[0].shape
    return pl.pallas_call(
        add_more_kernel,
        out_shape=[jax.ShapeDtypeStruct((1, rows, lanes), BF16)] * count,
        compiler_params=plain(8),
    )(*pieces)


def last_kernel(*refs, pieces, first):
    me_ref = refs[0]
    sources, outs = refs[1 : 1 + pieces], refs[1 + pieces :]
    position = me_ref[0]

    def total(at, height):
        value = sources[0][0, at : at + height, :].astype(F32)
        for ref in sources[1:]:
            value = value + ref[0, at : at + height, :].astype(F32)
        return value

    at = 0
    for ref in outs[:3]:
        for rows, cols in blocks_of(ref):
            ref[rows, cols] = total(at, BLOCK)
            at += BLOCK
    if first:
        cond = total(at, BLOCK)
        step = outs[3].shape[1]
        begin = lax.rem(position * step, 128)
        outs[3][...] = pltpu.roll(cond, 128 - begin, 1)[:, 0:step]
        bias = total(at + BLOCK, BLOCK)
        outs[4][...] = pltpu.roll(bias, 128 - begin, 1)[0:1, 0:step]
    else:
        last = total(at, BLOCK)
        for row, ref in enumerate(outs[3:]):
            step = ref.shape[1]
            begin = lax.rem(position * step, 128)
            ref[...] = pltpu.roll(last, 128 - begin, 1)[row : row + 1, 0:step]


def last_sum(me, pieces, shapes, first):
    return pl.pallas_call(
        lambda *refs: last_kernel(*refs, pieces=len(pieces), first=first),
        out_shape=[jax.ShapeDtypeStruct(shape, F32) for shape in shapes],
        in_specs=[smem()] + [pl.BlockSpec(memory_space=pltpu.VMEM)] * len(pieces),
        compiler_params=plain(60),
    )(me, *pieces)


def smem():
    return pl.BlockSpec(memory_space=pltpu.SMEM)


def attend_kernel(*refs, pieces):
    nodes_ref, h0, h1, h2, h3, bias_ref = refs[:6]
    buffers, sems = refs[-7:-1], refs[-1]
    act_buf, q_buf, k_buf, v_buf, p_buf, att_buf = buffers
    s, last = pl.program_id(0), pl.num_programs(0) - 1
    if pieces:
        me_ref, code_ref = refs[6:8]
        shards = refs[8 : 8 + pieces]
        wq_ref, wk_ref, wv_ref, mod_ref = refs[8 + pieces : 12 + pieces]
        raw = refs[18 + pieces]
        outs = refs[12 + pieces : 18 + pieces]

        @pl.when(s == 0)
        def _():
            place_first(me_ref, shards, code_ref, wq_ref, wk_ref, wv_ref, mod_ref, raw)

        at = s
    else:
        mod_ref, wq_ref, wk_ref, wv_ref = refs[6:10]
        outs = refs[10:16]
        at = 0
    heads_count = p_buf.shape[1]
    slot = lax.rem(s, 2)

    def copies(sample, place, arrays, some_heads):
        made = [(buffers[i].at[place], outs[i].at[sample], sems.at[place, i]) for i in arrays]
        for h in some_heads:
            made.append((p_buf.at[place, h], outs[4].at[sample, h], sems.at[place, 6 + h]))
        return [pltpu.make_async_copy(*parts) for parts in made]

    def wait_for(sample, place):
        for copy in copies(sample, place, (0, 1, 2, 3, 5), range(heads_count)):
            copy.wait()

    @pl.when(s > 1)
    def _():
        wait_for(s - 2, slot)

    count, _ = nodes_ref.shape[1:]
    each = h0.shape[1]
    scale, shift = mod_ref[at, 0:1, :], mod_ref[at, 1:2, :]

    def activate(rows):
        hat, _ = layer_normalize(rows.astype(F32))
        return (hat * scale + shift).astype(BF16)

    act_buf[slot, 0:count, :] = activate(nodes_ref[0])
    for d, ref in enumerate((h0, h1, h2, h3)):
        begin = count + d * each
        act_buf[slot, begin : begin + each, :] = activate(ref[0])
    act = act_buf[slot]
    for copy in copies(s, slot, (0,), ()):
        copy.start()
    factor = math.log2(math.e) * HEAD ** (-0.5)
    heads = [slice(h * HEAD, (h + 1) * HEAD) for h in range(heads_count)]

    def project(h):
        if h % 2 or h >= heads_count:
            return
        cols = slice(h * HEAD, min(h + 2, heads_count) * HEAD)
        q_buf[slot, :, cols] = product(act[0:count], wq_ref[:, cols]).astype(BF16)
        k_buf[slot, :, cols] = product(act, wk_ref[:, cols]).astype(BF16)
        v_buf[slot, :, cols] = product(act, wv_ref[:, cols]).astype(BF16)

    def score(cols):
        return product_t(k_buf[slot, :, cols], q_buf[slot, :, cols])

    early = max(heads_count - 3, 0)
    project(0)
    following = score(heads[0])
    for h, cols in enumerate(heads):
        scores = following
        project(h + 2)
        if h + 1 < heads_count:
            following = score(heads[h + 1])
        scores = scores * factor + bias_ref[...]
        top = jnp.max(scores, axis=0, keepdims=True)
        expo = jnp.exp2(scores - top)
        total = jnp.sum(expo, axis=0, keepdims=True)
        probs = (expo * (1.0 / total)).astype(BF16)
        p_buf[slot, h] = probs
        att_buf[slot, :, cols] = product(v_buf[slot, :, cols].T, probs).T.astype(BF16)
        if h == early:
            for copy in copies(s, slot, (1, 2, 3), range(early + 1)):
                copy.start()
    for copy in copies(s, slot, (5,), range(early + 1, heads_count)):
        copy.start()

    @pl.when(s == last)
    def _():
        wait_for(s, slot)

        @pl.when(s > 0)
        def _():
            wait_for(s - 1, 1 - slot)


def attend(nodes, halos, bias, weights=None, shards=None):
    samples, count, width = nodes.shape
    table = bias.shape[0]
    heads = width // HEAD
    each = halos[0].shape[1]
    square = jax.ShapeDtypeStruct((width, width), BF16)
    mod_shape = jax.ShapeDtypeStruct((samples, 4, width), F32)
    tile = per_sample
    in_specs = [tile((count, width))] + [tile((each, width))] * 4 + [once((table, count))]
    args = [nodes, *halos, bias]
    out_specs, out_shape, scratch = [], [], []
    if shards is None:
        wq, wk, wv, mod = weights
        in_specs += [tile((4, width))] + [once((width, width))] * 3
        args += [mod, wq, wk, wv]
    else:
        me, code, *pieces = shards
        in_specs += [smem(), once(code.shape)] + [once(x.shape) for x in pieces]
        args += [me, code] + pieces
        out_specs += [once((width, width))] * 3 + [once(mod_shape.shape)]
        out_shape += [square] * 3 + [mod_shape]
        devices = sum(x.shape[0] for x in pieces)
        scratch = [pltpu.VMEM((samples, devices, 128), F32)]
    tables = [(table, width), (count, width), (table, width), (table, width)]
    tables += [(heads, table, count), (count, width)]
    first = 0 if shards is None else len(shards) - 2
    return pl.pallas_call(
        lambda *refs: attend_kernel(*refs, pieces=first),
        grid=(samples,),
        in_specs=in_specs,
        out_specs=out_specs + [anywhere()] * len(tables),
        out_shape=out_shape + [jax.ShapeDtypeStruct((samples,) + t, BF16) for t in tables],
        scratch_shapes=scratch
        + [pltpu.VMEM((2,) + t, BF16) for t in tables]
        + [pltpu.SemaphoreType.DMA((2, 6 + heads))],
        compiler_params=params(60),
    )(*args)


def feed_kernel(*refs, shards):
    me_ref, nodes_ref, att_ref, cot_ref, mod_ref = refs[:5]
    scratch = 6 + (10 + shards if shards else 0)
    up_acc, down_acc, wo_acc, bu_acc, bd_acc, down_rows = refs[len(refs) - 6 :]
    if shards:
        pieces = refs[5 : 5 + shards]
        *piece_bufs, low_buf, high_buf, in_sems, out_sems = refs[-scratch:-12]
        wo_ref, wu_ref, wd_ref, bu_ref, bd_ref, raw = refs[-12:-6]
        outs = refs[5 + shards : -scratch]

        @pl.when(pl.program_id(0) == 0)
        def _():
            arriving = [
                pltpu.make_async_copy(piece, buf, in_sems.at[i])
                for i, (piece, buf) in enumerate(zip(pieces, piece_bufs))
            ]
            for copy in arriving:
                copy.start()
            place_second(
                me_ref, piece_bufs, arriving, wo_ref, wu_ref, wd_ref, bu_ref, bd_ref, raw
            )

    else:
        wo_ref, wu_ref, wd_ref, bu_ref, bd_ref = refs[5:10]
        outs = refs[10:-scratch]
    out_ref, gmid_ref, gatt_ref, gmod_ref = outs[:4]
    sums = outs[4:]
    s = pl.program_id(0)
    count, width = nodes_ref.shape[1:]
    hidden_size = wu_ref.shape[1]
    wide = hidden_size // width

    def add_to(ref, cols, value):
        ref[:, cols] = jnp.where(s == 0, 0.0, ref[:, cols]) + value

    scale, shift = mod_ref[0, 2:3, :], mod_ref[0, 3:4, :]
    blocks = [slice(c * width, (c + 1) * width) for c in range(wide)]
    attended = att_ref[0]
    cot = cot_ref[0]
    middle = nodes_ref[0].astype(F32) + product(attended, wo_ref[...])
    cot_t = cot.T
    grad_ahead = product_t(cot, wd_ref[blocks[0], :])
    add_to(bd_acc, slice(0, width), jnp.sum(cot.astype(F32), axis=0, keepdims=True))
    hat, inverse = layer_normalize(middle)
    act = (hat * scale + shift).astype(BF16)
    act_t = act.T
    result = middle + bd_ref[...]
    grad_act = jnp.zeros((count, width), F32)

    pre_ahead = product(act, wu_ref[:, blocks[0]])
    ready = None
    for c, cols in enumerate(blocks):
        pre, grad_hidden = pre_ahead, grad_ahead
        if c + 1 < wide:
            pre_ahead = product(act, wu_ref[:, blocks[c + 1]])
            grad_ahead = product_t(cot, wd_ref[blocks[c + 1], :])
        if ready:
            old, hidden, low_pre = ready
            result = result + product(hidden, wd_ref[old, :])
            grad_act = grad_act + product_t(low_pre, wu_ref[:, old])
            add_to(down_acc, old, product(cot_t, hidden))
            add_to(up_acc, old, product(act_t, low_pre))
        pre = pre + bu_ref[:, cols]
        gate = 0.5 * jnp.tanh(0.5 * pre) + 0.5
        value = pre * gate
        low_pre = (grad_hidden * (gate + value * (1.0 - gate))).astype(BF16)
        add_to(bu_acc, cols, jnp.sum(low_pre.astype(F32), axis=0, keepdims=True))
        ready = (cols, value.astype(BF16), low_pre)
    old, hidden, low_pre = ready
    grad_act = grad_act + product_t(low_pre, wu_ref[:, old])
    result = result + product(hidden, wd_ref[old, :])
    add_to(down_acc, old, product(cot_t, hidden))
    add_to(up_acc, old, product(act_t, low_pre))
    grad_middle = cot.astype(F32) + norm_back(grad_act * scale, hat, inverse)
    gmid_ref[0] = grad_middle
    branch = grad_middle.astype(BF16)
    out_ref[0] = result.astype(BF16)
    gmod_ref[0, 0:1, :] = jnp.sum(grad_act * hat, axis=0, keepdims=True)
    gmod_ref[0, 1:2, :] = jnp.sum(grad_act, axis=0, keepdims=True)
    gatt_ref[0] = product_t(branch, wo_ref[...]).astype(BF16)
    add_to(wo_acc, slice(0, width), product(attended.T, branch))

    @pl.when(s == pl.num_programs(0) - 1)
    def _():
        for c in range(wide):
            cols = slice(c * width, (c + 1) * width)
            down_rows[cols, :] = down_acc[:, cols].T
        if len(sums) > 2:
            for ref, value in zip(sums, (up_acc, down_rows, wo_acc, bu_acc, bd_acc)):
                ref[...] = value[...]
            return
        half = low_buf.shape[0]
        devices = 2 * half
        down = hidden_size // devices
        leaving = []

        for part, ref in ((1, high_buf), (0, low_buf)):

            def pack(i, _, part=part, ref=ref):
                shard = me_ref[0] ^ relative(i + part * half, devices)
                rows = pl.ds(pl.multiple_of(shard * BLOCK, BLOCK), BLOCK)
                at = 0
                for c in range(0, hidden_size, 128):
                    ref[i, at : at + BLOCK, :] = up_acc[rows, c : c + 128].astype(BF16)
                    at += BLOCK
                for r in range(0, down, BLOCK):
                    some = pl.ds(pl.multiple_of(shard * down + r, BLOCK), BLOCK)
                    for c in range(0, width, 128):
                        ref[i, at : at + BLOCK, :] = down_rows[some, c : c + 128].astype(BF16)
                        at += BLOCK
                for c in range(0, width, 128):
                    ref[i, at : at + BLOCK, :] = wo_acc[rows, c : c + 128].astype(BF16)
                    at += BLOCK
                up_tile = pl.multiple_of(((shard * down) // 128) * 128, 128)
                down_tile = pl.multiple_of(((shard * (width // devices)) // 128) * 128, 128)
                row = lax.broadcasted_iota(jnp.int32, (BLOCK, 128), 0)
                ref[i, at : at + BLOCK, :] = jnp.where(
                    row == 0, bu_acc[:, pl.ds(up_tile, 128)], bd_acc[:, pl.ds(down_tile, 128)]
                ).astype(BF16)
                return 0

            quarter = half // 4
            for q in range(4):
                some = slice(q * quarter, (q + 1) * quarter)
                lax.fori_loop(some.start, some.stop, pack, 0, unroll=2)
                leaving.append(
                    pltpu.make_async_copy(
                        ref.at[some], sums[part].at[some], out_sems.at[part, q]
                    )
                )
                leaving[-1].start()
        for copy in leaving:
            copy.wait()


def feed(me, nodes, attended, cot, mod, hidden, devices, weights=None, shards=None):
    samples, count, width = nodes.shape
    tile = per_sample((count, width))
    scratch = [
        pltpu.VMEM((width, hidden), F32),
        pltpu.VMEM((width, hidden), F32),
        pltpu.VMEM((width, width), F32),
        pltpu.VMEM((1, hidden), F32),
        pltpu.VMEM((1, width), F32),
        pltpu.VMEM((hidden, width), F32),
    ]
    if shards:
        rows = shards[0].shape[1]
        sums = [jax.ShapeDtypeStruct((devices // 2, rows, 128), BF16)] * 2
        extra = list(shards)
        scratch = [pltpu.VMEM(x.shape, BF16) for x in extra + sums] + [
            pltpu.SemaphoreType.DMA((len(extra),)),
            pltpu.SemaphoreType.DMA((2, 4)),
            pltpu.VMEM((width, width), BF16),
            pltpu.VMEM((width, hidden), BF16),
            pltpu.VMEM((hidden, width), BF16),
            pltpu.VMEM((1, hidden), F32),
            pltpu.VMEM((1, width), F32),
            pltpu.VMEM((2, devices, 128), F32),
        ] + scratch
    else:
        shapes = ((width, hidden), (hidden, width), (width, width), (1, hidden), (1, width))
        sums = [jax.ShapeDtypeStruct(shape, F32) for shape in shapes]
        extra = list(weights)
    return pl.pallas_call(
        lambda *refs: feed_kernel(*refs, shards=len(shards or ())),
        grid=(samples,),
        in_specs=[smem(), tile, tile, tile, per_sample((4, width))]
        + [anywhere() if shards else once(x.shape) for x in extra],
        out_specs=[tile, tile, tile, per_sample((2, width))]
        + [anywhere() if shards else once(x.shape) for x in sums],
        out_shape=[
            jax.ShapeDtypeStruct((samples, count, width), BF16),
            jax.ShapeDtypeStruct((samples, count, width), F32),
            jax.ShapeDtypeStruct((samples, count, width), BF16),
            jax.ShapeDtypeStruct((samples, 2, width), F32),
        ]
        + sums,
        scratch_shapes=scratch,
        compiler_params=params(60),
    )(me, nodes, attended, cot, mod, *extra)


def attend_back_kernel(*refs, started, last, begin):
    me_ref, nodes_ref, h0, h1, h2, h3, code_ref, gmod_ref = refs[:8]
    act_ref, q_ref, k_ref, v_ref, p_ref, gatt_ref, wq_ref, wk_ref, wv_ref = refs[8:17]
    gmid_ref, mod_ref = refs[17:19]
    rest = refs[19:]
    if started:
        before, rest = rest[:5], rest[10:]
    base_ref, b0, b1, b2, b3 = rest[:5]
    gq, gk, gv, p_buf, p_sems, sum_sems = rest[-6:]
    if last:
        outs = rest[5:-11]
        sums = q_acc, k_acc, v_acc, cond_acc, bias_acc = rest[-11:-6]
    else:
        sums = q_acc, k_acc, v_acc, cond_acc, bias_acc = rest[5:10]
    s, steps = pl.program_id(0), pl.num_programs(0)
    slot = lax.rem(s, 2)

    def fetch(step, h):
        place = lax.rem(step, 2)
        return pltpu.make_async_copy(
            p_ref.at[begin + step, h], p_buf.at[place, h], p_sems.at[place, h]
        )

    def carry():
        return [
            pltpu.make_async_copy(old, new, sum_sems.at[i])
            for i, (old, new) in enumerate(zip(before, sums))
        ]

    @pl.when(s == 0)
    def _():
        for h in range(p_buf.shape[1]):
            fetch(s, h).start()
        if started:
            for copy in carry():
                copy.start()

    @pl.when(s + 1 < steps)
    def _():
        for h in range(p_buf.shape[1]):
            fetch(s + 1, h).start()

    def add_to(ref, cols, value):
        old = ref[:, cols]
        ref[:, cols] = (old if started else jnp.where(s == 0, 0.0, old)) + value

    count, width = nodes_ref.shape[1:]
    each = h0.shape[1]
    inv_root = HEAD ** (-0.5)

    heads = [slice(h * HEAD, (h + 1) * HEAD) for h in range(width // HEAD)]

    def grad_of_probs(cols):
        return product_t(v_ref[0, :, cols], gatt_ref[0, :, cols])

    def spread_back(cols, grad_scores):
        gk[:, cols] = (product(grad_scores, q_ref[0, :, cols]) * inv_root).astype(BF16)
        gq[:, cols] = (product(k_ref[0, :, cols].T, grad_scores) * inv_root).T.astype(BF16)

    act_t = act_ref[0].T

    def weigh(h):
        cols = slice(h * HEAD, (h + 2) * HEAD)
        add_to(q_acc, cols, product(act_t[:, 0:count], gq[:, cols]))
        add_to(k_acc, cols, product(act_t, gk[:, cols]))
        add_to(v_acc, cols, product(act_t, gv[:, cols]))

    following = grad_of_probs(heads[0])
    hat, inverse = layer_normalize(nodes_ref[0].astype(F32))
    ready = None
    for h, cols in enumerate(heads):
        grad_probs = following
        if h + 1 < len(heads):
            following = grad_of_probs(heads[h + 1])
        if h % 2 == 0:
            for i in range(h, min(h + 2, len(heads))):
                fetch(s, i).wait()
        if h == 2 and started:

            @pl.when(s == 0)
            def _():
                for copy in carry():
                    copy.wait()

        gv[:, cols] = product(p_buf[slot, h], gatt_ref[0, :, cols]).astype(BF16)
        if ready:
            spread_back(*ready)
        if h == 2:
            weigh(0)
        probs = p_buf[slot, h].astype(F32)
        inner = jnp.sum(probs * grad_probs, axis=0, keepdims=True)
        ready = (cols, (probs * (grad_probs - inner)).astype(BF16))
    spread_back(*ready)

    grad_act = (
        product_t(gq[...], wq_ref[...])
        + product_t(gk[0:count, :], wk_ref[...])
        + product_t(gv[0:count, :], wv_ref[...])
    )
    grad_far = product_t(gk[count:, :], wk_ref[...]) + product_t(gv[count:, :], wv_ref[...])
    for h in range(2, len(heads), 2):
        weigh(h)
    base_ref[0] = gmid_ref[0] + norm_back(grad_act * mod_ref[0, 0:1, :], hat, inverse)
    scale_sum = jnp.sum(grad_act * hat, axis=0, keepdims=True)
    shift_sum = jnp.sum(grad_act, axis=0, keepdims=True)
    for d, (far, back) in enumerate(zip((h0, h1, h2, h3), (b0, b1, b2, b3))):
        part = grad_far[d * each : (d + 1) * each]
        far_hat, _ = layer_normalize(far[0].astype(F32))
        scale_sum = scale_sum + jnp.sum(part * far_hat, axis=0, keepdims=True)
        shift_sum = shift_sum + jnp.sum(part, axis=0, keepdims=True)
        back[0] = part.astype(BF16)
    kinds = (scale_sum, shift_sum, gmod_ref[0, 0:1, :], gmod_ref[0, 1:2, :])
    columns = code_ref[...].T
    mine = lax.broadcasted_iota(jnp.int32, columns.shape, 1) == s + begin
    code = jnp.sum(jnp.where(mine, columns, 0.0), axis=1, keepdims=True)
    for kind, value in enumerate(kinds):
        cols = slice(kind * width, (kind + 1) * width)
        add_to(cond_acc, cols, code * value)
        add_to(bias_acc, cols, value)
    if not last:
        return

    @pl.when(s == pl.num_programs(0) - 1)
    def _():
        if len(outs) > 2:
            for ref, value in zip(outs, sums):
                ref[...] = value[...]
            return
        half = outs[0].shape[0]
        devices = 2 * half
        for part, ref in enumerate(outs):

            def pack(i, _, part=part, ref=ref):
                shard = me_ref[0] ^ relative(i + part * half, devices)
                rows = pl.ds(pl.multiple_of(shard * BLOCK, BLOCK), BLOCK)
                at = 0
                for value in (q_acc, k_acc, v_acc):
                    for c in range(0, width, 128):
                        ref[i, at : at + BLOCK, :] = value[rows, c : c + 128].astype(BF16)
                        at += BLOCK
                tile = pl.multiple_of(((shard * (4 * width // devices)) // 128) * 128, 128)
                ref[i, at : at + BLOCK, :] = cond_acc[:, pl.ds(tile, 128)].astype(BF16)
                at += BLOCK
                ref[i, at : at + BLOCK, :] = jnp.broadcast_to(
                    bias_acc[:, pl.ds(tile, 128)], (BLOCK, 128)
                ).astype(BF16)
                return 0

            lax.fori_loop(0, half, pack, 0, unroll=2)


def attend_back(
    me,
    nodes,
    halos,
    noise_code,
    gmod,
    saved,
    gatt,
    wq,
    wk,
    wv,
    gmid,
    mod,
    devices,
    begin,
    steps,
    carried=(),
):
    samples, count, width = nodes.shape
    act, queries, keys, values, probs = saved
    table = act.shape[1]
    heads = width // HEAD
    each = halos[0].shape[1]
    half = devices // 2
    codes = noise_code.shape[1]
    last = begin + steps == samples
    shapes = [(width, width)] * 3 + [(codes, 4 * width), (1, 4 * width)]
    sums = [jax.ShapeDtypeStruct(shape, F32) for shape in shapes]
    scratch = [
        pltpu.VMEM((count, width), BF16),
        pltpu.VMEM((table, width), BF16),
        pltpu.VMEM((table, width), BF16),
        pltpu.VMEM((2, heads, table, count), BF16),
        pltpu.SemaphoreType.DMA((2, heads)),
        pltpu.SemaphoreType.DMA((5,)),
    ]
    if last:
        scratch = [pltpu.VMEM(shape, F32) for shape in shapes] + scratch
        if packs(width, devices):
            rows = 3 * BLOCK * width // 128 + 2 * BLOCK
            sums = [jax.ShapeDtypeStruct((half, rows, 128), BF16)] * 2

    def tile(*shape):
        return per_sample(shape, begin)

    args = [me, nodes, *halos, noise_code, gmod, act, queries, keys, values, probs, gatt, wq, wk, wv]
    args += [gmid, mod]
    aliases = {len(args) + 5 + i: i for i in range(5)} if carried else {}
    return pl.pallas_call(
        lambda *refs: attend_back_kernel(*refs, started=bool(carried), last=last, begin=begin),
        grid=(steps,),
        in_specs=[smem(), tile(count, width)]
        + [tile(each, width)] * 4
        + [once(noise_code.shape), tile(2, width)]
        + [tile(table, width), tile(count, width), tile(table, width), tile(table, width)]
        + [anywhere(), tile(count, width)]
        + [once((width, width))] * 3
        + [tile(count, width), tile(4, width)]
        + ([anywhere()] * 5 + [anywhere()] * 5 if carried else []),
        out_specs=[tile(count, width)]
        + [tile(each, width)] * 4
        + [once(x.shape) for x in sums],
        out_shape=[jax.ShapeDtypeStruct((samples, count, width), F32)]
        + [jax.ShapeDtypeStruct((samples, each, width), BF16)] * 4
        + sums,
        scratch_shapes=scratch,
        input_output_aliases=aliases,
        compiler_params=params(46),
    )(*args, *carried)


def finish_kernel(nodes_ref, base_ref, b0, b1, b2, b3, send_ref, mod_ref, out_ref, far):
    count = nodes_ref.shape[1]
    each = b0.shape[1]
    row = lax.broadcasted_iota(jnp.int32, (count, 4 * each), 0)
    chosen = jnp.where(row == send_ref[...], 1.0, 0.0).astype(BF16)
    for d, ref in enumerate((b0, b1, b2, b3)):
        far[d * each : (d + 1) * each, :] = ref[0]
    grad_act = product(chosen, far[...])
    hat, inverse = layer_normalize(nodes_ref[0].astype(F32))
    out_ref[0] = base_ref[0] + norm_back(grad_act * mod_ref[0, 0:1, :], hat, inverse)


def finish(nodes, base, backs, send_rows, mod):
    samples, count, width = nodes.shape
    each = backs[0].shape[1]
    picks = send_rows.size
    tile = per_sample((count, width))
    return pl.pallas_call(
        finish_kernel,
        grid=(samples,),
        in_specs=[tile, tile]
        + [per_sample((each, width))] * 4
        + [whole((1, picks)), per_sample((4, width))],
        out_specs=tile,
        out_shape=jax.ShapeDtypeStruct((samples, count, width), F32),
        scratch_shapes=[pltpu.VMEM((picks, width), BF16)],
        compiler_params=params(16),
    )(nodes, base, *backs, send_rows.reshape(1, picks), mod)


def layer(
    nodes,
    neighbours,
    send_rows,
    noise_code,
    w_query,
    w_key,
    w_value,
    w_out,
    w_up,
    b_up,
    w_down,
    b_down,
    cond_weight,
    cond_bias,
    cotangent,
):
    devices = lax.axis_size("patch") * lax.axis_size("sample")
    position = lax.axis_index("patch") * lax.axis_size("sample") + lax.axis_index("sample")
    me = position.astype(jnp.int32).reshape(1)
    width = nodes.shape[2]
    hidden = w_up.shape[1]
    offsets = (1, -1, STRIDE, -STRIDE)

    samples, count, _ = nodes.shape
    table = count + send_rows.size
    if not packs(width, devices):
        return plain_body(
            me,
            nodes,
            neighbours,
            send_rows,
            noise_code,
            (w_query, w_key, w_value, cond_weight, cond_bias, noise_code),
            (w_out, w_up, b_up, w_down, b_down),
            cotangent,
            devices,
        )
    z_side, plane, (core,) = stage_groups(devices)

    def swaps(pieces, group):
        return [swap(x, c, devices) for x, c in zip(pieces, group)]

    def cores(pieces):
        return [swap(x, core, devices) for x in pieces]

    def shifts(blocks, sign):
        return [from_behind(x, sign * o) for x, o in zip(blocks, offsets)]

    *sends, first, second = begin(
        nodes,
        send_rows,
        (w_query, w_key, w_value, cond_weight, cond_bias, w_out, w_up, b_up, w_down, b_down),
    )
    far = swaps([first] * 3, z_side)
    far_second = swaps([second] * 3, z_side)
    bias = slot_bias(neighbours, table)
    halos = shifts([after(x, bias) for x in sends], 1)
    held = join([first] + far)
    low_first = [held] + swaps([held] * 3, plane)
    high_first = cores(low_first)
    held_second = join([second] + far_second)
    low_second = [held_second] + swaps([held_second] * 3, plane)
    wq, wk, wv, mod, *saved, attended = attend(
        nodes, halos, bias, shards=[me, noise_code] + low_first + high_first
    )
    high_second = cores(low_second)
    result, gmid, gatt, gmod, low_feed, high_feed = feed(
        me,
        nodes,
        attended,
        cotangent,
        mod,
        hidden,
        devices,
        shards=low_second + high_second,
    )
    back = (me, nodes, halos, noise_code, gmod, saved, gatt, wq, wk, wv, gmid, mod, devices)
    (got_feed,) = cores([high_feed])
    *arrays, s0, s1, s2, s3, s4 = attend_back(*back, 0, 1)
    own_feed, *parts = add_halves(low_feed, got_feed, 4)
    feed_far = swaps(parts, plane)
    carried = (after(s0, own_feed), s1, s2, s3, s4, *arrays)
    base, *rest = attend_back(*back, 1, samples - 1, carried)
    low_proj, high_proj = rest[4:]
    (got_proj,) = cores([high_proj])
    own_feed, *parts = add_pieces([own_feed] + feed_far)
    feed_last = swaps(parts, z_side)
    own_proj, *parts = add_halves(low_proj, got_proj, 4)
    proj_far = swaps(parts, plane)
    backs = shifts(rest[:4], -1)
    own_proj, *parts = add_pieces([own_proj] + proj_far)
    proj_last = swaps(parts, z_side)
    grad_nodes = finish(nodes, base, backs, send_rows, mod)
    down, thin = hidden // devices, width // devices
    grad_up, grad_down, grad_out, grad_b_up, grad_b_down = last_sum(
        me,
        [own_feed] + feed_last,
        ((BLOCK, hidden), (down, width), (BLOCK, width), (1, down), (1, thin)),
        False,
    )
    step = 4 * width // devices
    grad_query, grad_key, grad_value, grad_cond, grad_cond_bias = last_sum(
        me,
        [own_proj] + proj_last,
        ((BLOCK, width),) * 3 + ((BLOCK, step), (1, step)),
        True,
    )
    grad_b_up, grad_b_down, grad_cond_bias = grad_b_up[0], grad_b_down[0], grad_cond_bias[0]
    return (
        result,
        grad_nodes,
        grad_query,
        grad_key,
        grad_value,
        grad_out,
        grad_up,
        grad_b_up,
        grad_down,
        grad_b_down,
        grad_cond,
        grad_cond_bias,
    )


def plain_body(
    me, nodes, neighbours, send_rows, noise_code, first, second, cotangent, devices
):
    samples, count, _ = nodes.shape
    hidden = second[1].shape[1]
    offsets = (1, -1, STRIDE, -STRIDE)
    bias = slot_bias(neighbours, count + send_rows.size)
    sends = begin(nodes, send_rows)
    halos = [from_behind(block, offset) for block, offset in zip(sends, offsets)]
    (wq, wk, wv, mod), weights = gather_plain(*first, *second)
    *saved, attended = attend(nodes, halos, bias, weights=(wq, wk, wv, mod))
    result, gmid, gatt, gmod, *sums = feed(
        me, nodes, attended, cotangent, mod, hidden, devices, weights=weights
    )
    sums[3:] = [x[0] for x in sums[3:]]
    grad_up, grad_down, grad_out, grad_b_up, grad_b_down = scatter_plain(sums, (0,) * 5)
    base, *rest = attend_back(
        me, nodes, halos, noise_code, gmod, saved, gatt, wq, wk, wv, gmid, mod, devices, 0, samples
    )
    backs = [from_behind(block, -offset) for block, offset in zip(rest[:4], offsets)]
    rest[-1] = rest[-1][0]
    grad_query, grad_key, grad_value, grad_cond, grad_cond_bias = scatter_plain(
        rest[4:], (0, 0, 0, 1, 0)
    )
    grad_nodes = finish(nodes, base, backs, send_rows, mod)
    return (
        result,
        grad_nodes,
        grad_query,
        grad_key,
        grad_value,
        grad_out,
        grad_up,
        grad_b_up,
        grad_down,
        grad_b_down,
        grad_cond,
        grad_cond_bias,
    )


def solution(mesh):
    both = P(("patch", "sample"), None)
    flat = P(("patch", "sample"))
    split = P("sample", "patch", None)
    cond = P(None, ("patch", "sample"))
    return jax.shard_map(
        layer,
        mesh=mesh,
        in_specs=(
            split,
            P("patch", None),
            P("patch", None),
            P("sample", None),
            both,
            both,
            both,
            both,
            both,
            flat,
            both,
            flat,
            cond,
            flat,
            split,
        ),
        out_specs=(split, split, both, both, both, both, both, flat, both, flat, cond, flat),
        check_vma=False,
    )
```

```python
import math

import jax
import jax.numpy as jnp
from jax import lax
from jax.experimental import pallas as pl
from jax.experimental.pallas import tpu as pltpu
from jax.sharding import PartitionSpec as P


HEAD = 128
STRIDE = 4
BLOCK = 16
AXES = ("patch", "sample")
EPSILON = 1e-05
F32 = jnp.float32
BF16 = jnp.bfloat16
MIB = 1024 * 1024
EMIT_LIMIT = 20


def product(left, right):
    return jnp.dot(left, right, preferred_element_type=F32)


def product_t(left, right):
    return lax.dot_general(left, right, (((1,), (1,)), ((), ())), preferred_element_type=F32)


def from_behind(block, distance):
    count = lax.axis_size("patch")
    return lax.ppermute(block, "patch", [((i - distance) % count, i) for i in range(count)])


def swap(block, bits, devices):
    return lax.ppermute(block, AXES, [(i, i ^ bits) for i in range(devices)])


def stage_groups(devices):
    bits = [1 << i for i in reversed(range(devices.bit_length() - 1)) if (1 << i) != 2]
    groups = [bits[i : i + 2] for i in range(0, len(bits), 2)]
    return [combos(g) for g in groups] + [[2]]


def combos(group):
    if len(group) == 1:
        return [group[0]]
    high, low = group
    return [low, high, low | high]


def relative(k, devices):
    shift, out = 0, 0
    for group in stage_groups(devices):
        if len(group) == 1:
            out = out | (((k >> shift) & 1) * group[0])
            shift += 1
        else:
            out = out | (((k >> shift) & 1) * group[0]) | (((k >> (shift + 1)) & 1) * group[1])
            shift += 2
    return out


def join_kernel(*refs):
    at = 0
    for ref in refs[:-1]:
        refs[-1][at : at + ref.shape[0]] = ref[...]
        at += ref.shape[0]


def join(pieces):
    count = sum(piece.shape[0] for piece in pieces)
    return pl.pallas_call(
        join_kernel,
        out_shape=jax.ShapeDtypeStruct((count,) + pieces[0].shape[1:], pieces[0].dtype),
        compiler_params=plain(8),
    )(*pieces)


def after(value, *others):
    return lax.optimization_barrier((value,) + others)[0]


def layer_normalize(values):
    centre = jnp.mean(values, axis=-1, keepdims=True)
    centred = values - centre
    inverse = lax.rsqrt(jnp.mean(centred * centred, axis=-1, keepdims=True) + EPSILON)
    return centred * inverse, inverse


def norm_back(grad_hat, normed, inverse):
    first = jnp.mean(grad_hat, axis=-1, keepdims=True)
    second = jnp.mean(grad_hat * normed, axis=-1, keepdims=True)
    return inverse * (grad_hat - first - normed * second)


def whole(shape):
    return pl.BlockSpec(shape, lambda *_: (0,) * len(shape))


def once(shape):
    return pl.BlockSpec(shape, lambda *_: (0,) * len(shape), pipeline_mode=pl.Buffered(1))


def per_sample(shape, begin=0):
    return pl.BlockSpec((1,) + shape, lambda s, *_: (s + begin,) + (0,) * len(shape))


def anywhere():
    return pl.BlockSpec(memory_space=pl.ANY)


def params(limit, axes=1):
    return pltpu.CompilerParams(
        dimension_semantics=("arbitrary",) * axes, vmem_limit_bytes=limit * MIB
    )


def plain(limit):
    return pltpu.CompilerParams(vmem_limit_bytes=limit * MIB)


def bias_kernel(nbr_ref, bias_ref):
    table, count = bias_ref.shape
    height = 2 * BLOCK
    row = lax.broadcasted_iota(jnp.int32, (height, count), 0)
    slots = nbr_ref[...]

    def block(i, _):
        begin = pl.multiple_of(i * height, height)
        total = jnp.zeros((height, count), F32)
        for j in range(slots.shape[0]):
            total = total + jnp.where(row == slots[j : j + 1, :] - begin, 1.0, 0.0)
        bias_ref[pl.ds(begin, height), :] = jnp.where(
            total > 0.0, jnp.log2(jnp.maximum(total, 1.0)), -1e30
        )
        return 0

    lax.fori_loop(0, table // height, block, 0)


def slot_bias(neighbours, table):
    return pl.pallas_call(
        bias_kernel,
        out_shape=jax.ShapeDtypeStruct((table, neighbours.shape[0]), F32),
        compiler_params=plain(8),
    )(neighbours.T)


def pick_rows(nodes_ref, send_ref, out_refs):
    samples, count, _ = nodes_ref.shape
    each = send_ref.shape[1]
    lanes = lax.broadcasted_iota(jnp.int32, (each, count), 1)
    columns = send_ref[...].T
    for d, out_ref in enumerate(out_refs):
        chosen = jnp.where(lanes == columns[:, d : d + 1], 1.0, 0.0).astype(BF16)
        for s in range(samples):
            out_ref[s] = product(chosen, nodes_ref[s]).astype(BF16)


def blocks_of(ref):
    height, width = ref.shape
    for r in range(0, height, BLOCK):
        for c in range(0, width, 128):
            yield slice(r, r + BLOCK), slice(c, c + 128)


def pack_shards(weights, first_ref, second_ref):
    wq, wk, wv, cw, cb, wo, wu, bu, wd, bd = weights
    for source, ref in (((wq, wk, wv), first_ref), ((wu, wd, wo), second_ref)):
        at = 0
        for part in source:
            for rows, cols in blocks_of(part):
                ref[0, at : at + BLOCK, :] = part[rows, cols]
                at += BLOCK
        ref[0, at : at + BLOCK, :] = jnp.zeros((BLOCK, 128), BF16)
    at = first_ref.shape[1] - BLOCK
    first_ref[0, at : at + BLOCK, 0 : cw.shape[1]] = cw[...]
    first_ref[0, at : at + 1, cb.shape[1] :] = cb[...]
    at = second_ref.shape[1] - BLOCK
    for row, part in enumerate((bu, bd)):
        step = part.shape[1]
        for c in range(0, 128, step):
            second_ref[0, at + row : at + row + 1, c : c + step] = part[...]


def begin_kernel(*refs, ways, given):
    nodes_ref, send_ref = refs[:2]
    weights, out_refs = refs[2 : 2 + given], refs[2 + given : 2 + given + ways]
    pick_rows(nodes_ref, send_ref, out_refs)
    if weights:
        pack_shards(weights, *refs[-2:])


def begin(nodes, send_rows, weights=()):
    samples, _, width = nodes.shape
    ways, each = send_rows.shape
    weights = [w if w.ndim == 2 else w[None] for w in weights]
    shards = []
    if weights:
        wq, wk, wv, _, _, wo, wu, _, wd, _ = weights
        for group in ((wq, wk, wv), (wo, wu, wd)):
            rows = sum(w.size for w in group) // 128 + BLOCK
            shards.append(jax.ShapeDtypeStruct((1, rows, 128), BF16))
    return pl.pallas_call(
        lambda *refs: begin_kernel(*refs, ways=ways, given=len(weights)),
        out_shape=[jax.ShapeDtypeStruct((samples, each, width), BF16)] * ways + shards,
        compiler_params=plain(60),
    )(nodes, send_rows, *weights)


def spread(rows, step, width):
    reps = jnp.concatenate([rows] * (width // 128), axis=1)
    lane = lax.broadcasted_iota(jnp.int32, reps.shape, 1)
    row = lax.broadcasted_iota(jnp.int32, reps.shape, 0)
    return jnp.sum(jnp.where(lane // step == row, reps, 0.0), axis=0, keepdims=True)


def place(source, k, shard, targets):
    at = 0
    for ref, height in targets:
        for r in range(0, height, BLOCK):
            rows = pl.ds(pl.multiple_of(shard * height + r, BLOCK), BLOCK)
            for c in range(0, ref.shape[1], 128):
                ref[rows, c : c + 128] = source[k, at : at + BLOCK, :]
                at += BLOCK
    return at


def for_shards(pieces, take, arriving=()):
    at = 0
    for n, ref in enumerate(pieces):
        if arriving:
            arriving[n].wait()

        def step(i, _, ref=ref, at=at):
            take(at + i, ref, i)
            return 0

        lax.fori_loop(0, ref.shape[0], step, 0, unroll=2)
        at += ref.shape[0]


def place_first(me_ref, pieces, code_ref, wq_ref, wk_ref, wv_ref, mod_ref, raw):
    devices = sum(ref.shape[0] for ref in pieces)
    samples = code_ref.shape[0]
    width = wq_ref.shape[1]
    step = 4 * width // devices
    lane = lax.broadcasted_iota(jnp.int32, (BLOCK, 128), 1)
    columns = code_ref[...].T
    code = [jnp.where(lane < 64, columns[:, s : s + 1], 1.0) for s in range(samples)]

    def take(k, source, i):
        shard = me_ref[0] ^ relative(k, devices)
        targets = ((wq_ref, BLOCK), (wk_ref, BLOCK), (wv_ref, BLOCK))
        at = place(source, i, shard, targets)
        cond = source[i, at : at + BLOCK, :].astype(F32)
        for s in range(samples):
            value = jnp.sum(cond * code[s], axis=0, keepdims=True)
            raw[s, pl.ds(shard, 1), :] = value + pltpu.roll(value, 64, 1)

    for_shards(pieces, take)
    each = devices // 4
    for s in range(samples):
        for kind in range(4):
            value = spread(raw[s, kind * each : (kind + 1) * each, :], step, width)
            mod_ref[s, kind : kind + 1, :] = value + 1.0 if kind % 2 == 0 else value


def place_second(me_ref, pieces, arriving, wo_ref, wu_ref, wd_ref, bu_ref, bd_ref, raw):
    devices = sum(ref.shape[0] for ref in pieces)
    width = wo_ref.shape[1]
    hidden = wu_ref.shape[1]

    def take(k, source, i):
        shard = me_ref[0] ^ relative(k, devices)
        targets = ((wu_ref, BLOCK), (wd_ref, hidden // devices), (wo_ref, BLOCK))
        at = place(source, i, shard, targets)
        extra = source[i, at : at + BLOCK, :].astype(F32)
        raw[0, pl.ds(shard, 1), :] = extra[0:1]
        raw[1, pl.ds(shard, 1), :] = extra[1:2]

    for_shards(pieces, take, arriving)
    each = devices // (hidden // width)
    for c in range(hidden // width):
        bu_ref[:, c * width : (c + 1) * width] = spread(
            raw[0, c * each : (c + 1) * each, :], hidden // devices, width
        )
    bd_ref[...] = spread(raw[1], width // devices, width)


def packs(width, devices):
    return width == devices * BLOCK


def gather_plain(wq, wk, wv, cond_weight, cond_bias, noise_code, wo, wu, bu, wd, bd):
    def full(x, axis=0):
        return lax.all_gather(x, AXES, axis=axis, tiled=True)

    mod = jnp.dot(
        noise_code, full(cond_weight, 1).astype(F32), precision=lax.Precision.HIGHEST
    ) + full(cond_bias).astype(F32)
    mod = mod.reshape(noise_code.shape[0], 4, wq.shape[1])
    mod = mod + jnp.array([1.0, 0.0, 1.0, 0.0], F32)[:, None]
    first = (full(wq), full(wk), full(wv), mod)
    biases = (full(bu)[None].astype(F32), full(bd)[None].astype(F32))
    return first, (full(wo), full(wu), full(wd)) + biases


def scatter_plain(sums, axes):
    return [
        lax.psum_scatter(x, AXES, scatter_dimension=axis, tiled=True)
        for x, axis in zip(sums, axes)
    ]


def add_kernel(own_ref, far_ref, *out_refs):
    size = out_refs[0].shape[0]
    for i, out_ref in enumerate(out_refs):
        part = slice(i * size, (i + 1) * size)
        out_ref[...] = own_ref[part] + far_ref[part]


def add_halves(own_half, far_half, parts):
    count, rows, lanes = own_half.shape
    return pl.pallas_call(
        add_kernel,
        out_shape=[jax.ShapeDtypeStruct((count // parts, rows, lanes), BF16)] * parts,
        compiler_params=plain(16),
    )(own_half, far_half)


def add_more_kernel(*refs):
    sources, outs = refs[: -refs[0].shape[0]], refs[-refs[0].shape[0] :]
    for i, out_ref in enumerate(outs):
        total = sources[0][i].astype(F32)
        for ref in sources[1:]:
            total = total + ref[i].astype(F32)
        out_ref[0] = total.astype(BF16)


def add_pieces(pieces):
    count, rows, lanes = pieces[0].shape
    return pl.pallas_call(
        add_more_kernel,
        out_shape=[jax.ShapeDtypeStruct((1, rows, lanes), BF16)] * count,
        compiler_params=plain(8),
    )(*pieces)


def last_kernel(me_ref, *refs, pieces):
    feed_refs, proj_refs = refs[: pieces[0]], refs[pieces[0] : sum(pieces)]
    outs = refs[sum(pieces) :]
    position = me_ref[0]

    def total(sources, at):
        value = sources[0][0, at : at + BLOCK, :].astype(F32)
        for ref in sources[1:]:
            value = value + ref[0, at : at + BLOCK, :].astype(F32)
        return value

    def own(value, step, row, height):
        shift = 128 - lax.rem(position * step, 128)
        return pltpu.roll(value, shift, 1)[row : row + height, 0:step]

    def unpack(sources, refs):
        at = 0
        for ref in refs:
            for rows, cols in blocks_of(ref):
                ref[rows, cols] = total(sources, at)
                at += BLOCK
        return at

    at = unpack(feed_refs, outs[:3])
    biases = total(feed_refs, at)
    for row, ref in enumerate(outs[3:5]):
        ref[...] = own(biases, ref.shape[1], row, 1)
    at = unpack(proj_refs, outs[5:8])
    step = outs[8].shape[1]
    outs[8][...] = own(total(proj_refs, at), step, 0, BLOCK)
    outs[9][...] = own(total(proj_refs, at + BLOCK), step, 0, 1)


def last_sum(me, feed_pieces, proj_pieces, shapes):
    pieces = (len(feed_pieces), len(proj_pieces))
    return pl.pallas_call(
        lambda *refs: last_kernel(*refs, pieces=pieces),
        out_shape=[jax.ShapeDtypeStruct(shape, F32) for shape in shapes],
        in_specs=[smem()] + [pl.BlockSpec(memory_space=pltpu.VMEM)] * sum(pieces),
        compiler_params=plain(60),
    )(me, *feed_pieces, *proj_pieces)


def smem():
    return pl.BlockSpec(memory_space=pltpu.SMEM)


def attend_kernel(*refs, pieces):
    nodes_ref, h0, h1, h2, h3, bias_ref = refs[:6]
    buffers, sems = refs[-7:-1], refs[-1]
    act_buf, q_buf, k_buf, v_buf, p_buf, att_buf = buffers
    s, last = pl.program_id(0), pl.num_programs(0) - 1
    if pieces:
        me_ref, code_ref = refs[6:8]
        shards = refs[8 : 8 + pieces]
        wq_ref, wk_ref, wv_ref, mod_ref = refs[8 + pieces : 12 + pieces]
        raw = refs[18 + pieces]
        outs = refs[12 + pieces : 18 + pieces]

        @pl.when(s == 0)
        def _():
            place_first(me_ref, shards, code_ref, wq_ref, wk_ref, wv_ref, mod_ref, raw)

        at = s
    else:
        mod_ref, wq_ref, wk_ref, wv_ref = refs[6:10]
        outs = refs[10:16]
        at = 0
    heads_count = p_buf.shape[1]
    slot = lax.rem(s, 2)

    def copies(sample, place, arrays, some_heads):
        made = [(buffers[i].at[place], outs[i].at[sample], sems.at[place, i]) for i in arrays]
        for h in some_heads:
            made.append((p_buf.at[place, h], outs[4].at[sample, h], sems.at[place, 6 + h]))
        return [pltpu.make_async_copy(*parts) for parts in made]

    def wait_for(sample, place):
        for copy in copies(sample, place, (0, 1, 2, 3, 5), range(heads_count)):
            copy.wait()

    @pl.when(s > 1)
    def _():
        wait_for(s - 2, slot)

    count, _ = nodes_ref.shape[1:]
    each = h0.shape[1]
    scale, shift = mod_ref[at, 0:1, :], mod_ref[at, 1:2, :]

    def activate(rows):
        hat, _ = layer_normalize(rows.astype(F32))
        return (hat * scale + shift).astype(BF16)

    act_buf[slot, 0:count, :] = activate(nodes_ref[0])
    for d, ref in enumerate((h0, h1, h2, h3)):
        begin = count + d * each
        act_buf[slot, begin : begin + each, :] = activate(ref[0])
    act = act_buf[slot]
    for copy in copies(s, slot, (0,), ()):
        copy.start()
    factor = math.log2(math.e) * HEAD ** (-0.5)
    heads = [slice(h * HEAD, (h + 1) * HEAD) for h in range(heads_count)]

    def project(h):
        if h % 2 or h >= heads_count:
            return
        cols = slice(h * HEAD, min(h + 2, heads_count) * HEAD)
        q_buf[slot, :, cols] = product(act[0:count], wq_ref[:, cols]).astype(BF16)
        k_buf[slot, :, cols] = product(act, wk_ref[:, cols]).astype(BF16)
        v_buf[slot, :, cols] = product(act, wv_ref[:, cols]).astype(BF16)

    def score(cols):
        return product_t(k_buf[slot, :, cols], q_buf[slot, :, cols])

    early = max(heads_count - 3, 0)
    project(0)
    following = score(heads[0])
    for h, cols in enumerate(heads):
        scores = following
        project(h + 2)
        if h + 1 < heads_count:
            following = score(heads[h + 1])
        scores = scores * factor + bias_ref[...]
        top = jnp.max(scores, axis=0, keepdims=True)
        expo = jnp.exp2(scores - top)
        total = jnp.sum(expo, axis=0, keepdims=True)
        probs = (expo * (1.0 / total)).astype(BF16)
        p_buf[slot, h] = probs
        att_buf[slot, :, cols] = product(v_buf[slot, :, cols].T, probs).T.astype(BF16)
        if h == early:
            for copy in copies(s, slot, (1, 2, 3), range(early + 1)):
                copy.start()
    for copy in copies(s, slot, (5,), range(early + 1, heads_count)):
        copy.start()

    @pl.when(s == last)
    def _():
        wait_for(s, slot)

        @pl.when(s > 0)
        def _():
            wait_for(s - 1, 1 - slot)


def attend(nodes, halos, bias, weights=None, shards=None):
    samples, count, width = nodes.shape
    table = bias.shape[0]
    heads = width // HEAD
    each = halos[0].shape[1]
    square = jax.ShapeDtypeStruct((width, width), BF16)
    mod_shape = jax.ShapeDtypeStruct((samples, 4, width), F32)
    tile = per_sample
    in_specs = [tile((count, width))] + [tile((each, width))] * 4 + [once((table, count))]
    args = [nodes, *halos, bias]
    out_specs, out_shape, scratch = [], [], []
    if shards is None:
        wq, wk, wv, mod = weights
        in_specs += [tile((4, width))] + [once((width, width))] * 3
        args += [mod, wq, wk, wv]
    else:
        me, code, *pieces = shards
        in_specs += [smem(), once(code.shape)] + [once(x.shape) for x in pieces]
        args += [me, code] + pieces
        out_specs += [once((width, width))] * 3 + [once(mod_shape.shape)]
        out_shape += [square] * 3 + [mod_shape]
        devices = sum(x.shape[0] for x in pieces)
        scratch = [pltpu.VMEM((samples, devices, 128), F32)]
    tables = [(table, width), (count, width), (table, width), (table, width)]
    tables += [(heads, table, count), (count, width)]
    first = 0 if shards is None else len(shards) - 2
    return pl.pallas_call(
        lambda *refs: attend_kernel(*refs, pieces=first),
        grid=(samples,),
        in_specs=in_specs,
        out_specs=out_specs + [anywhere()] * len(tables),
        out_shape=out_shape + [jax.ShapeDtypeStruct((samples,) + t, BF16) for t in tables],
        scratch_shapes=scratch
        + [pltpu.VMEM((2,) + t, BF16) for t in tables]
        + [pltpu.SemaphoreType.DMA((2, 6 + heads))],
        compiler_params=params(60),
    )(*args)


def feed_kernel(*refs, shards):
    me_ref, nodes_ref, att_ref, cot_ref, mod_ref = refs[:5]
    scratch = 9 + (10 + shards if shards else 0)
    up_acc, down_acc, wo_acc, bu_acc, bd_acc, down_rows = refs[-9:-3]
    hid_buf, hid_sems, wd_sem = refs[-3:]
    if shards:
        pieces = refs[5 : 5 + shards]
        *piece_bufs, low_buf, high_buf, in_sems, out_sems = refs[-scratch:-15]
        wo_ref, wu_ref, wd_ref, bu_ref, bd_ref, raw = refs[-15:-9]
        outs = refs[5 + shards : -scratch]

        @pl.when(pl.program_id(0) == 0)
        def _():
            arriving = [
                pltpu.make_async_copy(piece, buf, in_sems.at[i])
                for i, (piece, buf) in enumerate(zip(pieces, piece_bufs))
            ]
            for copy in arriving:
                copy.start()
            place_second(
                me_ref, piece_bufs, arriving, wo_ref, wu_ref, wd_ref, bu_ref, bd_ref, raw
            )

    else:
        wo_ref, wu_ref, wd_ref, bu_ref, bd_ref = refs[5:10]
        outs = refs[10:-scratch]
    part_ref, gmid_ref, gatt_ref, gmod_ref, hid_ref = outs[:5]
    sums = outs[5:]
    if shards:
        down_copy = pltpu.make_async_copy(wd_ref, outs[5], wd_sem.at[0])
        sums = outs[6:]

        @pl.when(pl.program_id(0) == 0)
        def _():
            down_copy.start()

    s = pl.program_id(0)
    count, width = nodes_ref.shape[1:]
    hidden_size = wu_ref.shape[1]
    wide = hidden_size // width

    def add_to(ref, cols, value):
        ref[:, cols] = jnp.where(s == 0, 0.0, ref[:, cols]) + value

    slot = lax.rem(s, 2)

    def hid_copy(sample, place):
        return pltpu.make_async_copy(hid_buf.at[place], hid_ref.at[sample], hid_sems.at[place])

    @pl.when(s > 1)
    def _():
        hid_copy(s - 2, slot).wait()

    scale, shift = mod_ref[0, 2:3, :], mod_ref[0, 3:4, :]
    blocks = [slice(c * width, (c + 1) * width) for c in range(wide)]
    attended = att_ref[0]
    cot = cot_ref[0]
    middle = nodes_ref[0].astype(F32) + product(attended, wo_ref[...])
    cot_t = cot.T
    grad_ahead = product_t(cot, wd_ref[blocks[0], :])
    add_to(bd_acc, slice(0, width), jnp.sum(cot.astype(F32), axis=0, keepdims=True))
    hat, inverse = layer_normalize(middle)
    act = (hat * scale + shift).astype(BF16)
    act_t = act.T
    part_ref[0] = middle + bd_ref[...]
    grad_act = jnp.zeros((count, width), F32)

    pre_ahead = product(act, wu_ref[:, blocks[0]])
    ready = None
    for c, cols in enumerate(blocks):
        pre, grad_hidden = pre_ahead, grad_ahead
        if c + 1 < wide:
            pre_ahead = product(act, wu_ref[:, blocks[c + 1]])
            grad_ahead = product_t(cot, wd_ref[blocks[c + 1], :])
        if ready:
            old, hidden, low_pre = ready
            grad_act = grad_act + product_t(low_pre, wu_ref[:, old])
            add_to(down_acc, old, product(cot_t, hidden))
            add_to(up_acc, old, product(act_t, low_pre))
        pre = pre + bu_ref[:, cols]
        gate = 0.5 * jnp.tanh(0.5 * pre) + 0.5
        value = pre * gate
        low_pre = (grad_hidden * (gate + value * (1.0 - gate))).astype(BF16)
        add_to(bu_acc, cols, jnp.sum(low_pre.astype(F32), axis=0, keepdims=True))
        ready = (cols, value.astype(BF16), low_pre)
        hid_buf[slot, :, cols] = ready[1]
    hid_copy(s, slot).start()
    old, hidden, low_pre = ready
    grad_act = grad_act + product_t(low_pre, wu_ref[:, old])
    add_to(down_acc, old, product(cot_t, hidden))
    add_to(up_acc, old, product(act_t, low_pre))
    grad_middle = cot.astype(F32) + norm_back(grad_act * scale, hat, inverse)
    gmid_ref[0] = grad_middle
    branch = grad_middle.astype(BF16)
    gmod_ref[0, 0:1, :] = jnp.sum(grad_act * hat, axis=0, keepdims=True)
    gmod_ref[0, 1:2, :] = jnp.sum(grad_act, axis=0, keepdims=True)
    gatt_ref[0] = product_t(branch, wo_ref[...]).astype(BF16)
    add_to(wo_acc, slice(0, width), product(attended.T, branch))

    @pl.when(s == pl.num_programs(0) - 1)
    def _():
        hid_copy(s, slot).wait()

        @pl.when(s > 0)
        def _():
            hid_copy(s - 1, 1 - slot).wait()

        if shards:
            down_copy.wait()
        for c in range(wide):
            cols = slice(c * width, (c + 1) * width)
            down_rows[cols, :] = down_acc[:, cols].T
        if len(sums) > 2:
            for ref, value in zip(sums, (up_acc, down_rows, wo_acc, bu_acc, bd_acc)):
                ref[...] = value[...]
            return
        half = low_buf.shape[0]
        devices = 2 * half
        down = hidden_size // devices
        leaving = []

        for part, ref in ((1, high_buf), (0, low_buf)):

            def pack(i, _, part=part, ref=ref):
                shard = me_ref[0] ^ relative(i + part * half, devices)
                rows = pl.ds(pl.multiple_of(shard * BLOCK, BLOCK), BLOCK)
                at = 0
                for c in range(0, hidden_size, 128):
                    ref[i, at : at + BLOCK, :] = up_acc[rows, c : c + 128].astype(BF16)
                    at += BLOCK
                for r in range(0, down, BLOCK):
                    some = pl.ds(pl.multiple_of(shard * down + r, BLOCK), BLOCK)
                    for c in range(0, width, 128):
                        ref[i, at : at + BLOCK, :] = down_rows[some, c : c + 128].astype(BF16)
                        at += BLOCK
                for c in range(0, width, 128):
                    ref[i, at : at + BLOCK, :] = wo_acc[rows, c : c + 128].astype(BF16)
                    at += BLOCK
                up_tile = pl.multiple_of(((shard * down) // 128) * 128, 128)
                down_tile = pl.multiple_of(((shard * (width // devices)) // 128) * 128, 128)
                row = lax.broadcasted_iota(jnp.int32, (BLOCK, 128), 0)
                ref[i, at : at + BLOCK, :] = jnp.where(
                    row == 0, bu_acc[:, pl.ds(up_tile, 128)], bd_acc[:, pl.ds(down_tile, 128)]
                ).astype(BF16)
                return 0

            quarter = half // 4
            for q in range(4):
                some = slice(q * quarter, (q + 1) * quarter)
                lax.fori_loop(some.start, some.stop, pack, 0, unroll=2)
                leaving.append(
                    pltpu.make_async_copy(
                        ref.at[some], sums[part].at[some], out_sems.at[part, q]
                    )
                )
                leaving[-1].start()
        for copy in leaving:
            copy.wait()


def feed(me, nodes, attended, cot, mod, hidden, devices, weights=None, shards=None):
    samples, count, width = nodes.shape
    tile = per_sample((count, width))
    scratch = [
        pltpu.VMEM((width, hidden), F32),
        pltpu.VMEM((width, hidden), F32),
        pltpu.VMEM((width, width), F32),
        pltpu.VMEM((1, hidden), F32),
        pltpu.VMEM((1, width), F32),
        pltpu.VMEM((hidden, width), F32),
        pltpu.VMEM((2, count, hidden), BF16),
        pltpu.SemaphoreType.DMA((2,)),
        pltpu.SemaphoreType.DMA((1,)),
    ]
    down = [jax.ShapeDtypeStruct((hidden, width), BF16)] if shards else []
    if shards:
        rows = shards[0].shape[1]
        sums = [jax.ShapeDtypeStruct((devices // 2, rows, 128), BF16)] * 2
        extra = list(shards)
        scratch = [pltpu.VMEM(x.shape, BF16) for x in extra + sums] + [
            pltpu.SemaphoreType.DMA((len(extra),)),
            pltpu.SemaphoreType.DMA((2, 4)),
            pltpu.VMEM((width, width), BF16),
            pltpu.VMEM((width, hidden), BF16),
            pltpu.VMEM((hidden, width), BF16),
            pltpu.VMEM((1, hidden), F32),
            pltpu.VMEM((1, width), F32),
            pltpu.VMEM((2, devices, 128), F32),
        ] + scratch
    else:
        shapes = ((width, hidden), (hidden, width), (width, width), (1, hidden), (1, width))
        sums = [jax.ShapeDtypeStruct(shape, F32) for shape in shapes]
        extra = list(weights)
    return pl.pallas_call(
        lambda *refs: feed_kernel(*refs, shards=len(shards or ())),
        grid=(samples,),
        in_specs=[smem(), tile, tile, tile, per_sample((4, width))]
        + [anywhere() if shards else once(x.shape) for x in extra],
        out_specs=[tile, tile, tile, per_sample((2, width)), anywhere()]
        + [anywhere()] * len(down)
        + [anywhere() if shards else once(x.shape) for x in sums],
        out_shape=[
            jax.ShapeDtypeStruct((samples, count, width), F32),
            jax.ShapeDtypeStruct((samples, count, width), F32),
            jax.ShapeDtypeStruct((samples, count, width), BF16),
            jax.ShapeDtypeStruct((samples, 2, width), F32),
            jax.ShapeDtypeStruct((samples, count, hidden), BF16),
        ]
        + down
        + sums,
        scratch_shapes=scratch,
        compiler_params=params(60),
    )(me, nodes, attended, cot, mod, *extra)


def emit_kernel(hid_ref, wd_ref, part_ref, out_ref):
    out_ref[0] = (part_ref[0] + product(hid_ref[0], wd_ref[...])).astype(BF16)


def emit(hid, wd, part):
    samples, count, width = part.shape
    hidden = wd.shape[0]
    tile = per_sample((count, width))
    return pl.pallas_call(
        emit_kernel,
        grid=(samples,),
        in_specs=[per_sample((count, hidden)), once((hidden, width)), tile],
        out_specs=tile,
        out_shape=jax.ShapeDtypeStruct(part.shape, BF16),
        compiler_params=params(EMIT_LIMIT),
    )(hid, wd, part)


def attend_back_kernel(*refs, started, last, begin):
    me_ref, nodes_ref, h0, h1, h2, h3, code_ref, gmod_ref = refs[:8]
    act_ref, q_ref, k_ref, v_ref, p_ref, gatt_ref, wq_ref, wk_ref, wv_ref = refs[8:17]
    gmid_ref, mod_ref = refs[17:19]
    rest = refs[19:]
    if started:
        before, rest = rest[:5], rest[10:]
    base_ref, b0, b1, b2, b3 = rest[:5]
    gq, gk, gv, p_buf, p_sems, sum_sems = rest[-6:]
    if last:
        outs = rest[5:-11]
        sums = q_acc, k_acc, v_acc, cond_acc, bias_acc = rest[-11:-6]
    else:
        sums = q_acc, k_acc, v_acc, cond_acc, bias_acc = rest[5:10]
    s, steps = pl.program_id(0), pl.num_programs(0)
    slot = lax.rem(s, 2)

    def fetch(step, h):
        place = lax.rem(step, 2)
        return pltpu.make_async_copy(
            p_ref.at[begin + step, h], p_buf.at[place, h], p_sems.at[place, h]
        )

    def carry():
        return [
            pltpu.make_async_copy(old, new, sum_sems.at[i])
            for i, (old, new) in enumerate(zip(before, sums))
        ]

    @pl.when(s == 0)
    def _():
        for h in range(p_buf.shape[1]):
            fetch(s, h).start()
        if started:
            for copy in carry():
                copy.start()

    @pl.when(s + 1 < steps)
    def _():
        for h in range(p_buf.shape[1]):
            fetch(s + 1, h).start()

    def add_to(ref, cols, value):
        old = ref[:, cols]
        ref[:, cols] = (old if started else jnp.where(s == 0, 0.0, old)) + value

    count, width = nodes_ref.shape[1:]
    each = h0.shape[1]
    inv_root = HEAD ** (-0.5)

    heads = [slice(h * HEAD, (h + 1) * HEAD) for h in range(width // HEAD)]

    def grad_of_probs(cols):
        return product_t(v_ref[0, :, cols], gatt_ref[0, :, cols])

    def spread_back(cols, grad_scores):
        gk[:, cols] = (product(grad_scores, q_ref[0, :, cols]) * inv_root).astype(BF16)
        gq[:, cols] = (product(k_ref[0, :, cols].T, grad_scores) * inv_root).T.astype(BF16)

    act_t = act_ref[0].T

    def weigh(h):
        cols = slice(h * HEAD, (h + 2) * HEAD)
        add_to(q_acc, cols, product(act_t[:, 0:count], gq[:, cols]))
        add_to(k_acc, cols, product(act_t, gk[:, cols]))
        add_to(v_acc, cols, product(act_t, gv[:, cols]))

    following = grad_of_probs(heads[0])
    hat, inverse = layer_normalize(nodes_ref[0].astype(F32))
    ready = None
    for h, cols in enumerate(heads):
        grad_probs = following
        if h + 1 < len(heads):
            following = grad_of_probs(heads[h + 1])
        if h % 2 == 0:
            for i in range(h, min(h + 2, len(heads))):
                fetch(s, i).wait()
        if h == 2 and started:

            @pl.when(s == 0)
            def _():
                for copy in carry():
                    copy.wait()

        gv[:, cols] = product(p_buf[slot, h], gatt_ref[0, :, cols]).astype(BF16)
        if ready:
            spread_back(*ready)
        if h == 2:
            weigh(0)
        probs = p_buf[slot, h].astype(F32)
        inner = jnp.sum(probs * grad_probs, axis=0, keepdims=True)
        ready = (cols, (probs * (grad_probs - inner)).astype(BF16))
    spread_back(*ready)

    grad_act = (
        product_t(gq[...], wq_ref[...])
        + product_t(gk[0:count, :], wk_ref[...])
        + product_t(gv[0:count, :], wv_ref[...])
    )
    grad_far = product_t(gk[count:, :], wk_ref[...]) + product_t(gv[count:, :], wv_ref[...])
    for h in range(2, len(heads), 2):
        weigh(h)
    base_ref[0] = gmid_ref[0] + norm_back(grad_act * mod_ref[0, 0:1, :], hat, inverse)
    scale_sum = jnp.sum(grad_act * hat, axis=0, keepdims=True)
    shift_sum = jnp.sum(grad_act, axis=0, keepdims=True)
    for d, (far, back) in enumerate(zip((h0, h1, h2, h3), (b0, b1, b2, b3))):
        part = grad_far[d * each : (d + 1) * each]
        far_hat, _ = layer_normalize(far[0].astype(F32))
        scale_sum = scale_sum + jnp.sum(part * far_hat, axis=0, keepdims=True)
        shift_sum = shift_sum + jnp.sum(part, axis=0, keepdims=True)
        back[0] = part.astype(BF16)
    kinds = (scale_sum, shift_sum, gmod_ref[0, 0:1, :], gmod_ref[0, 1:2, :])
    columns = code_ref[...].T
    mine = lax.broadcasted_iota(jnp.int32, columns.shape, 1) == s + begin
    code = jnp.sum(jnp.where(mine, columns, 0.0), axis=1, keepdims=True)
    for kind, value in enumerate(kinds):
        cols = slice(kind * width, (kind + 1) * width)
        add_to(cond_acc, cols, code * value)
        add_to(bias_acc, cols, value)
    if not last:
        return

    @pl.when(s == pl.num_programs(0) - 1)
    def _():
        if len(outs) > 2:
            for ref, value in zip(outs, sums):
                ref[...] = value[...]
            return
        half = outs[0].shape[0]
        devices = 2 * half
        for part, ref in enumerate(outs):

            def pack(i, _, part=part, ref=ref):
                shard = me_ref[0] ^ relative(i + part * half, devices)
                rows = pl.ds(pl.multiple_of(shard * BLOCK, BLOCK), BLOCK)
                at = 0
                for value in (q_acc, k_acc, v_acc):
                    for c in range(0, width, 128):
                        ref[i, at : at + BLOCK, :] = value[rows, c : c + 128].astype(BF16)
                        at += BLOCK
                tile = pl.multiple_of(((shard * (4 * width // devices)) // 128) * 128, 128)
                ref[i, at : at + BLOCK, :] = cond_acc[:, pl.ds(tile, 128)].astype(BF16)
                at += BLOCK
                ref[i, at : at + BLOCK, :] = jnp.broadcast_to(
                    bias_acc[:, pl.ds(tile, 128)], (BLOCK, 128)
                ).astype(BF16)
                return 0

            lax.fori_loop(0, half, pack, 0, unroll=2)


def attend_back(
    me,
    nodes,
    halos,
    noise_code,
    gmod,
    saved,
    gatt,
    wq,
    wk,
    wv,
    gmid,
    mod,
    devices,
    begin,
    steps,
    carried=(),
):
    samples, count, width = nodes.shape
    act, queries, keys, values, probs = saved
    table = act.shape[1]
    heads = width // HEAD
    each = halos[0].shape[1]
    half = devices // 2
    codes = noise_code.shape[1]
    last = begin + steps == samples
    shapes = [(width, width)] * 3 + [(codes, 4 * width), (1, 4 * width)]
    sums = [jax.ShapeDtypeStruct(shape, F32) for shape in shapes]
    scratch = [
        pltpu.VMEM((count, width), BF16),
        pltpu.VMEM((table, width), BF16),
        pltpu.VMEM((table, width), BF16),
        pltpu.VMEM((2, heads, table, count), BF16),
        pltpu.SemaphoreType.DMA((2, heads)),
        pltpu.SemaphoreType.DMA((5,)),
    ]
    if last:
        scratch = [pltpu.VMEM(shape, F32) for shape in shapes] + scratch
        if packs(width, devices):
            rows = 3 * BLOCK * width // 128 + 2 * BLOCK
            sums = [jax.ShapeDtypeStruct((half, rows, 128), BF16)] * 2

    def tile(*shape):
        return per_sample(shape, begin)

    args = [me, nodes, *halos, noise_code, gmod, act, queries, keys, values, probs, gatt, wq, wk, wv]
    args += [gmid, mod]
    aliases = {len(args) + 5 + i: i for i in range(5)} if carried else {}
    return pl.pallas_call(
        lambda *refs: attend_back_kernel(*refs, started=bool(carried), last=last, begin=begin),
        grid=(steps,),
        in_specs=[smem(), tile(count, width)]
        + [tile(each, width)] * 4
        + [once(noise_code.shape), tile(2, width)]
        + [tile(table, width), tile(count, width), tile(table, width), tile(table, width)]
        + [anywhere(), tile(count, width)]
        + [once((width, width))] * 3
        + [tile(count, width), tile(4, width)]
        + ([anywhere()] * 5 + [anywhere()] * 5 if carried else []),
        out_specs=[tile(count, width)]
        + [tile(each, width)] * 4
        + [once(x.shape) for x in sums],
        out_shape=[jax.ShapeDtypeStruct((samples, count, width), F32)]
        + [jax.ShapeDtypeStruct((samples, each, width), BF16)] * 4
        + sums,
        scratch_shapes=scratch,
        input_output_aliases=aliases,
        compiler_params=params(46),
    )(*args, *carried)


def finish_kernel(nodes_ref, base_ref, b0, b1, b2, b3, send_ref, mod_ref, out_ref, far):
    count = nodes_ref.shape[1]
    each = b0.shape[1]
    row = lax.broadcasted_iota(jnp.int32, (count, 4 * each), 0)
    chosen = jnp.where(row == send_ref[...], 1.0, 0.0).astype(BF16)
    for d, ref in enumerate((b0, b1, b2, b3)):
        far[d * each : (d + 1) * each, :] = ref[0]
    grad_act = product(chosen, far[...])
    hat, inverse = layer_normalize(nodes_ref[0].astype(F32))
    out_ref[0] = base_ref[0] + norm_back(grad_act * mod_ref[0, 0:1, :], hat, inverse)


def finish(nodes, base, backs, send_rows, mod):
    samples, count, width = nodes.shape
    each = backs[0].shape[1]
    picks = send_rows.size
    tile = per_sample((count, width))
    return pl.pallas_call(
        finish_kernel,
        grid=(samples,),
        in_specs=[tile, tile]
        + [per_sample((each, width))] * 4
        + [whole((1, picks)), per_sample((4, width))],
        out_specs=tile,
        out_shape=jax.ShapeDtypeStruct((samples, count, width), F32),
        scratch_shapes=[pltpu.VMEM((picks, width), BF16)],
        compiler_params=params(16),
    )(nodes, base, *backs, send_rows.reshape(1, picks), mod)


def layer(
    nodes,
    neighbours,
    send_rows,
    noise_code,
    w_query,
    w_key,
    w_value,
    w_out,
    w_up,
    b_up,
    w_down,
    b_down,
    cond_weight,
    cond_bias,
    cotangent,
):
    devices = lax.axis_size("patch") * lax.axis_size("sample")
    position = lax.axis_index("patch") * lax.axis_size("sample") + lax.axis_index("sample")
    me = position.astype(jnp.int32).reshape(1)
    width = nodes.shape[2]
    hidden = w_up.shape[1]
    offsets = (1, -1, STRIDE, -STRIDE)

    samples, count, _ = nodes.shape
    table = count + send_rows.size
    if not packs(width, devices):
        return plain_body(
            me,
            nodes,
            neighbours,
            send_rows,
            noise_code,
            (w_query, w_key, w_value, cond_weight, cond_bias, noise_code),
            (w_out, w_up, b_up, w_down, b_down),
            cotangent,
            devices,
        )
    z_side, plane, (core,) = stage_groups(devices)

    def swaps(pieces, group):
        return [swap(x, c, devices) for x, c in zip(pieces, group)]

    def cores(pieces):
        return [swap(x, core, devices) for x in pieces]

    def shifts(blocks, sign):
        return [from_behind(x, sign * o) for x, o in zip(blocks, offsets)]

    *sends, first, second = begin(
        nodes,
        send_rows,
        (w_query, w_key, w_value, cond_weight, cond_bias, w_out, w_up, b_up, w_down, b_down),
    )
    far = swaps([first] * 3, z_side)
    far_second = swaps([second] * 3, z_side)
    bias = slot_bias(neighbours, table)
    halos = shifts([after(x, bias) for x in sends], 1)
    held = join([first] + far)
    low_first = [held] + swaps([held] * 3, plane)
    high_first = cores(low_first)
    held_second = join([second] + far_second)
    low_second = [held_second] + swaps([held_second] * 3, plane)
    wq, wk, wv, mod, *saved, attended = attend(
        nodes, halos, bias, shards=[me, noise_code] + low_first + high_first
    )
    high_second = cores(low_second)
    part, gmid, gatt, gmod, hid, down_whole, low_feed, high_feed = feed(
        me,
        nodes,
        attended,
        cotangent,
        mod,
        hidden,
        devices,
        shards=low_second + high_second,
    )
    back = (me, nodes, halos, noise_code, gmod, saved, gatt, wq, wk, wv, gmid, mod, devices)
    (got_feed,) = cores([high_feed])
    *arrays, s0, s1, s2, s3, s4 = attend_back(*back, 0, 1)
    own_feed, *parts = add_halves(low_feed, got_feed, 4)
    feed_far = swaps(parts, plane)
    carried = (after(s0, own_feed), s1, s2, s3, s4, *arrays)
    base, *rest = attend_back(*back, 1, samples - 1, carried)
    low_proj, high_proj = rest[4:]
    (got_proj,) = cores([high_proj])
    own_feed, *parts = add_pieces([own_feed] + feed_far)
    feed_last = swaps(parts, z_side)
    own_proj, *parts = add_halves(low_proj, got_proj, 4)
    proj_far = swaps(parts, plane)
    backs = shifts(rest[:4], -1)
    result = emit(hid, down_whole, after(part, own_feed))
    own_proj, *parts = add_pieces([own_proj] + proj_far)
    proj_last = swaps(parts, z_side)
    grad_nodes = finish(nodes, base, backs, send_rows, mod)
    down, thin = hidden // devices, width // devices
    step = 4 * width // devices
    (
        grad_up,
        grad_down,
        grad_out,
        grad_b_up,
        grad_b_down,
        grad_query,
        grad_key,
        grad_value,
        grad_cond,
        grad_cond_bias,
    ) = last_sum(
        me,
        [own_feed] + feed_last,
        [own_proj] + proj_last,
        ((BLOCK, hidden), (down, width), (BLOCK, width), (1, down), (1, thin))
        + ((BLOCK, width),) * 3
        + ((BLOCK, step), (1, step)),
    )
    grad_b_up, grad_b_down, grad_cond_bias = grad_b_up[0], grad_b_down[0], grad_cond_bias[0]
    return (
        result,
        grad_nodes,
        grad_query,
        grad_key,
        grad_value,
        grad_out,
        grad_up,
        grad_b_up,
        grad_down,
        grad_b_down,
        grad_cond,
        grad_cond_bias,
    )


def plain_body(
    me, nodes, neighbours, send_rows, noise_code, first, second, cotangent, devices
):
    samples, count, _ = nodes.shape
    hidden = second[1].shape[1]
    offsets = (1, -1, STRIDE, -STRIDE)
    bias = slot_bias(neighbours, count + send_rows.size)
    sends = begin(nodes, send_rows)
    halos = [from_behind(block, offset) for block, offset in zip(sends, offsets)]
    (wq, wk, wv, mod), weights = gather_plain(*first, *second)
    *saved, attended = attend(nodes, halos, bias, weights=(wq, wk, wv, mod))
    part, gmid, gatt, gmod, hid, *sums = feed(
        me, nodes, attended, cotangent, mod, hidden, devices, weights=weights
    )
    result = emit(hid, weights[2], part)
    sums[3:] = [x[0] for x in sums[3:]]
    grad_up, grad_down, grad_out, grad_b_up, grad_b_down = scatter_plain(sums, (0,) * 5)
    base, *rest = attend_back(
        me, nodes, halos, noise_code, gmod, saved, gatt, wq, wk, wv, gmid, mod, devices, 0, samples
    )
    backs = [from_behind(block, -offset) for block, offset in zip(rest[:4], offsets)]
    rest[-1] = rest[-1][0]
    grad_query, grad_key, grad_value, grad_cond, grad_cond_bias = scatter_plain(
        rest[4:], (0, 0, 0, 1, 0)
    )
    grad_nodes = finish(nodes, base, backs, send_rows, mod)
    return (
        result,
        grad_nodes,
        grad_query,
        grad_key,
        grad_value,
        grad_out,
        grad_up,
        grad_b_up,
        grad_down,
        grad_b_down,
        grad_cond,
        grad_cond_bias,
    )


def solution(mesh):
    both = P(("patch", "sample"), None)
    flat = P(("patch", "sample"))
    split = P("sample", "patch", None)
    cond = P(None, ("patch", "sample"))
    return jax.shard_map(
        layer,
        mesh=mesh,
        in_specs=(
            split,
            P("patch", None),
            P("patch", None),
            P("sample", None),
            both,
            both,
            both,
            both,
            both,
            flat,
            both,
            flat,
            cond,
            flat,
            split,
        ),
        out_specs=(split, split, both, both, both, both, both, flat, both, flat, cond, flat),
        check_vma=False,
    )
```

```python
import math

import jax
import jax.numpy as jnp
from jax import lax
from jax.experimental import pallas as pl
from jax.experimental.pallas import tpu as pltpu
from jax.sharding import PartitionSpec as P


HEAD = 128
STRIDE = 4
BLOCK = 16
AXES = ("patch", "sample")
EPSILON = 1e-05
F32 = jnp.float32
BF16 = jnp.bfloat16
MIB = 1024 * 1024
EMIT_LIMIT = 20


def product(left, right):
    return jnp.dot(left, right, preferred_element_type=F32)


def product_t(left, right):
    return lax.dot_general(left, right, (((1,), (1,)), ((), ())), preferred_element_type=F32)


def from_behind(block, distance):
    count = lax.axis_size("patch")
    return lax.ppermute(block, "patch", [((i - distance) % count, i) for i in range(count)])


def swap(block, bits, devices):
    return lax.ppermute(block, AXES, [(i, i ^ bits) for i in range(devices)])


def stage_groups(devices):
    bits = [1 << i for i in reversed(range(devices.bit_length() - 1)) if (1 << i) != 2]
    groups = [bits[i : i + 2] for i in range(0, len(bits), 2)]
    return [combos(g) for g in groups] + [[2]]


def combos(group):
    if len(group) == 1:
        return [group[0]]
    high, low = group
    return [low, high, low | high]


def relative(k, devices):
    shift, out = 0, 0
    for group in stage_groups(devices):
        if len(group) == 1:
            out = out | (((k >> shift) & 1) * group[0])
            shift += 1
        else:
            out = out | (((k >> shift) & 1) * group[0]) | (((k >> (shift + 1)) & 1) * group[1])
            shift += 2
    return out


def join_kernel(*refs):
    at = 0
    for ref in refs[:-1]:
        refs[-1][at : at + ref.shape[0]] = ref[...]
        at += ref.shape[0]


def join(pieces):
    count = sum(piece.shape[0] for piece in pieces)
    return pl.pallas_call(
        join_kernel,
        out_shape=jax.ShapeDtypeStruct((count,) + pieces[0].shape[1:], pieces[0].dtype),
        compiler_params=plain(8),
    )(*pieces)


def after(value, *others):
    return lax.optimization_barrier((value,) + others)[0]


def layer_normalize(values):
    centre = jnp.mean(values, axis=-1, keepdims=True)
    centred = values - centre
    inverse = lax.rsqrt(jnp.mean(centred * centred, axis=-1, keepdims=True) + EPSILON)
    return centred * inverse, inverse


def norm_back(grad_hat, normed, inverse):
    first = jnp.mean(grad_hat, axis=-1, keepdims=True)
    second = jnp.mean(grad_hat * normed, axis=-1, keepdims=True)
    return inverse * (grad_hat - first - normed * second)


def whole(shape):
    return pl.BlockSpec(shape, lambda *_: (0,) * len(shape))


def once(shape):
    return pl.BlockSpec(shape, lambda *_: (0,) * len(shape), pipeline_mode=pl.Buffered(1))


def per_sample(shape, begin=0):
    return pl.BlockSpec((1,) + shape, lambda s, *_: (s + begin,) + (0,) * len(shape))


def anywhere():
    return pl.BlockSpec(memory_space=pl.ANY)


def params(limit, axes=1):
    return pltpu.CompilerParams(
        dimension_semantics=("arbitrary",) * axes, vmem_limit_bytes=limit * MIB
    )


def plain(limit):
    return pltpu.CompilerParams(vmem_limit_bytes=limit * MIB)


def bias_kernel(nbr_ref, bias_ref):
    table, count = bias_ref.shape
    height = 2 * BLOCK
    row = lax.broadcasted_iota(jnp.int32, (height, count), 0)
    slots = nbr_ref[...]

    def block(i, _):
        begin = pl.multiple_of(i * height, height)
        total = jnp.zeros((height, count), F32)
        for j in range(slots.shape[0]):
            total = total + jnp.where(row == slots[j : j + 1, :] - begin, 1.0, 0.0)
        bias_ref[pl.ds(begin, height), :] = jnp.where(
            total > 0.0, jnp.log2(jnp.maximum(total, 1.0)), -1e30
        )
        return 0

    lax.fori_loop(0, table // height, block, 0)


def slot_bias(neighbours, table):
    return pl.pallas_call(
        bias_kernel,
        out_shape=jax.ShapeDtypeStruct((table, neighbours.shape[0]), F32),
        compiler_params=plain(8),
    )(neighbours.T)


def pick_rows(nodes_ref, send_ref, out_refs):
    samples, count, _ = nodes_ref.shape
    each = send_ref.shape[1]
    lanes = lax.broadcasted_iota(jnp.int32, (each, count), 1)
    columns = send_ref[...].T
    for d, out_ref in enumerate(out_refs):
        chosen = jnp.where(lanes == columns[:, d : d + 1], 1.0, 0.0).astype(BF16)
        for s in range(samples):
            out_ref[s] = product(chosen, nodes_ref[s]).astype(BF16)


def blocks_of(ref):
    height, width = ref.shape
    for r in range(0, height, BLOCK):
        for c in range(0, width, 128):
            yield slice(r, r + BLOCK), slice(c, c + 128)


def pack_shards(weights, first_ref, second_ref):
    wq, wk, wv, cw, cb, wo, wu, bu, wd, bd = weights
    for source, ref in (((wq, wk, wv), first_ref), ((wu, wd, wo), second_ref)):
        at = 0
        for part in source:
            for rows, cols in blocks_of(part):
                ref[0, at : at + BLOCK, :] = part[rows, cols]
                at += BLOCK
        ref[0, at : at + BLOCK, :] = jnp.zeros((BLOCK, 128), BF16)
    at = first_ref.shape[1] - BLOCK
    first_ref[0, at : at + BLOCK, 0 : cw.shape[1]] = cw[...]
    first_ref[0, at : at + 1, cb.shape[1] :] = cb[...]
    at = second_ref.shape[1] - BLOCK
    for row, part in enumerate((bu, bd)):
        step = part.shape[1]
        for c in range(0, 128, step):
            second_ref[0, at + row : at + row + 1, c : c + step] = part[...]


def begin_kernel(*refs, ways, given):
    nodes_ref, send_ref = refs[:2]
    weights, out_refs = refs[2 : 2 + given], refs[2 + given : 2 + given + ways]
    pick_rows(nodes_ref, send_ref, out_refs)
    if weights:
        pack_shards(weights, *refs[-2:])


def begin(nodes, send_rows, weights=()):
    samples, _, width = nodes.shape
    ways, each = send_rows.shape
    weights = [w if w.ndim == 2 else w[None] for w in weights]
    shards = []
    if weights:
        wq, wk, wv, _, _, wo, wu, _, wd, _ = weights
        for group in ((wq, wk, wv), (wo, wu, wd)):
            rows = sum(w.size for w in group) // 128 + BLOCK
            shards.append(jax.ShapeDtypeStruct((1, rows, 128), BF16))
    return pl.pallas_call(
        lambda *refs: begin_kernel(*refs, ways=ways, given=len(weights)),
        out_shape=[jax.ShapeDtypeStruct((samples, each, width), BF16)] * ways + shards,
        compiler_params=plain(60),
    )(nodes, send_rows, *weights)


def spread(rows, step, width):
    reps = jnp.concatenate([rows] * (width // 128), axis=1)
    lane = lax.broadcasted_iota(jnp.int32, reps.shape, 1)
    row = lax.broadcasted_iota(jnp.int32, reps.shape, 0)
    return jnp.sum(jnp.where(lane // step == row, reps, 0.0), axis=0, keepdims=True)


def place(source, k, shard, targets):
    at = 0
    for ref, height in targets:
        for r in range(0, height, BLOCK):
            rows = pl.ds(pl.multiple_of(shard * height + r, BLOCK), BLOCK)
            for c in range(0, ref.shape[1], 128):
                ref[rows, c : c + 128] = source[k, at : at + BLOCK, :]
                at += BLOCK
    return at


def for_shards(pieces, take, arriving=()):
    at = 0
    for n, ref in enumerate(pieces):
        if arriving:
            arriving[n].wait()

        def step(i, _, ref=ref, at=at):
            take(at + i, ref, i)
            return 0

        lax.fori_loop(0, ref.shape[0], step, 0, unroll=2)
        at += ref.shape[0]


def place_first(me_ref, pieces, code_ref, wq_ref, wk_ref, wv_ref, mod_ref, raw):
    devices = sum(ref.shape[0] for ref in pieces)
    samples = code_ref.shape[0]
    width = wq_ref.shape[1]
    step = 4 * width // devices
    lane = lax.broadcasted_iota(jnp.int32, (BLOCK, 128), 1)
    columns = code_ref[...].T
    code = [jnp.where(lane < 64, columns[:, s : s + 1], 1.0) for s in range(samples)]

    def take(k, source, i):
        shard = me_ref[0] ^ relative(k, devices)
        targets = ((wq_ref, BLOCK), (wk_ref, BLOCK), (wv_ref, BLOCK))
        at = place(source, i, shard, targets)
        cond = source[i, at : at + BLOCK, :].astype(F32)
        for s in range(samples):
            value = jnp.sum(cond * code[s], axis=0, keepdims=True)
            raw[s, pl.ds(shard, 1), :] = value + pltpu.roll(value, 64, 1)

    for_shards(pieces, take)
    each = devices // 4
    for s in range(samples):
        for kind in range(4):
            value = spread(raw[s, kind * each : (kind + 1) * each, :], step, width)
            mod_ref[s, kind : kind + 1, :] = value + 1.0 if kind % 2 == 0 else value


def place_second(me_ref, pieces, arriving, wo_ref, wu_ref, wd_ref, bu_ref, bd_ref, raw):
    devices = sum(ref.shape[0] for ref in pieces)
    width = wo_ref.shape[1]
    hidden = wu_ref.shape[1]

    def take(k, source, i):
        shard = me_ref[0] ^ relative(k, devices)
        targets = ((wu_ref, BLOCK), (wd_ref, hidden // devices), (wo_ref, BLOCK))
        at = place(source, i, shard, targets)
        extra = source[i, at : at + BLOCK, :].astype(F32)
        raw[0, pl.ds(shard, 1), :] = extra[0:1]
        raw[1, pl.ds(shard, 1), :] = extra[1:2]

    for_shards(pieces, take, arriving)
    each = devices // (hidden // width)
    for c in range(hidden // width):
        bu_ref[:, c * width : (c + 1) * width] = spread(
            raw[0, c * each : (c + 1) * each, :], hidden // devices, width
        )
    bd_ref[...] = spread(raw[1], width // devices, width)


def packs(width, devices):
    return width == devices * BLOCK


def gather_plain(wq, wk, wv, cond_weight, cond_bias, noise_code, wo, wu, bu, wd, bd):
    def full(x, axis=0):
        return lax.all_gather(x, AXES, axis=axis, tiled=True)

    mod = jnp.dot(
        noise_code, full(cond_weight, 1).astype(F32), precision=lax.Precision.HIGHEST
    ) + full(cond_bias).astype(F32)
    mod = mod.reshape(noise_code.shape[0], 4, wq.shape[1])
    mod = mod + jnp.array([1.0, 0.0, 1.0, 0.0], F32)[:, None]
    first = (full(wq), full(wk), full(wv), mod)
    biases = (full(bu)[None].astype(F32), full(bd)[None].astype(F32))
    return first, (full(wo), full(wu), full(wd)) + biases


def scatter_plain(sums, axes):
    return [
        lax.psum_scatter(x, AXES, scatter_dimension=axis, tiled=True)
        for x, axis in zip(sums, axes)
    ]


def add_kernel(own_ref, far_ref, *out_refs):
    size = out_refs[0].shape[0]
    for i, out_ref in enumerate(out_refs):
        part = slice(i * size, (i + 1) * size)
        out_ref[...] = own_ref[part] + far_ref[part]


def add_halves(own_half, far_half, parts):
    count, rows, lanes = own_half.shape
    return pl.pallas_call(
        add_kernel,
        out_shape=[jax.ShapeDtypeStruct((count // parts, rows, lanes), BF16)] * parts,
        compiler_params=plain(16),
    )(own_half, far_half)


def add_more_kernel(*refs):
    sources, outs = refs[: -refs[0].shape[0]], refs[-refs[0].shape[0] :]
    for i, out_ref in enumerate(outs):
        total = sources[0][i].astype(F32)
        for ref in sources[1:]:
            total = total + ref[i].astype(F32)
        out_ref[0] = total.astype(BF16)


def add_pieces(pieces):
    count, rows, lanes = pieces[0].shape
    return pl.pallas_call(
        add_more_kernel,
        out_shape=[jax.ShapeDtypeStruct((1, rows, lanes), BF16)] * count,
        compiler_params=plain(8),
    )(*pieces)


def last_kernel(me_ref, *refs, pieces):
    feed_refs, proj_refs = refs[: pieces[0]], refs[pieces[0] : sum(pieces)]
    outs = refs[sum(pieces) :]
    position = me_ref[0]

    def total(sources, at):
        value = sources[0][0, at : at + BLOCK, :].astype(F32)
        for ref in sources[1:]:
            value = value + ref[0, at : at + BLOCK, :].astype(F32)
        return value

    def own(value, step, row, height):
        shift = 128 - lax.rem(position * step, 128)
        return pltpu.roll(value, shift, 1)[row : row + height, 0:step]

    def unpack(sources, refs):
        at = 0
        for ref in refs:
            for rows, cols in blocks_of(ref):
                ref[rows, cols] = total(sources, at)
                at += BLOCK
        return at

    at = unpack(feed_refs, outs[:3])
    biases = total(feed_refs, at)
    for row, ref in enumerate(outs[3:5]):
        ref[...] = own(biases, ref.shape[1], row, 1)
    at = unpack(proj_refs, outs[5:8])
    step = outs[8].shape[1]
    outs[8][...] = own(total(proj_refs, at), step, 0, BLOCK)
    outs[9][...] = own(total(proj_refs, at + BLOCK), step, 0, 1)


def last_sum(me, feed_pieces, proj_pieces, shapes):
    pieces = (len(feed_pieces), len(proj_pieces))
    return pl.pallas_call(
        lambda *refs: last_kernel(*refs, pieces=pieces),
        out_shape=[jax.ShapeDtypeStruct(shape, F32) for shape in shapes],
        in_specs=[smem()] + [pl.BlockSpec(memory_space=pltpu.VMEM)] * sum(pieces),
        compiler_params=plain(60),
    )(me, *feed_pieces, *proj_pieces)


def smem():
    return pl.BlockSpec(memory_space=pltpu.SMEM)


def activate(rows, mod):
    hat, _ = layer_normalize(rows.astype(F32))
    return (hat * mod[0:1] + mod[1:2]).astype(BF16)


def project_kernel(*refs, pieces):
    nodes_ref = refs[0]
    s = pl.program_id(0)
    if pieces:
        me_ref, code_ref = refs[1:3]
        shards = refs[3 : 3 + pieces]
        wq_ref, wk_ref, wv_ref, mod_ref = refs[3 + pieces : 7 + pieces]
        act_ref, q_ref, k_ref, v_ref, raw = refs[7 + pieces :]

        @pl.when(s == 0)
        def _():
            place_first(me_ref, shards, code_ref, wq_ref, wk_ref, wv_ref, mod_ref, raw)

        mod = mod_ref[s]
    else:
        mod_ref, wq_ref, wk_ref, wv_ref, act_ref, q_ref, k_ref, v_ref = refs[1:]
        mod = mod_ref[0]
    act = activate(nodes_ref[0], mod)
    act_ref[0] = act
    q_ref[0] = product(act, wq_ref[...]).astype(BF16)
    k_ref[0] = product(act, wk_ref[...]).astype(BF16)
    v_ref[0] = product(act, wv_ref[...]).astype(BF16)


def project(nodes, weights=None, shards=None):
    samples, count, width = nodes.shape
    tile = per_sample((count, width))
    in_specs, args = [tile], [nodes]
    out_specs, out_shape, scratch, first = [], [], [], 0
    if shards is None:
        wq, wk, wv, mod = weights
        in_specs += [per_sample((4, width))] + [once((width, width))] * 3
        args += [mod, wq, wk, wv]
    else:
        me, code, *pieces = shards
        first = len(pieces)
        in_specs += [smem(), once(code.shape)] + [once(x.shape) for x in pieces]
        args += [me, code] + pieces
        square = jax.ShapeDtypeStruct((width, width), BF16)
        out_shape += [square] * 3 + [jax.ShapeDtypeStruct((samples, 4, width), F32)]
        out_specs += [once(x.shape) for x in out_shape]
        scratch = [pltpu.VMEM((samples, sum(x.shape[0] for x in pieces), 128), F32)]
    return pl.pallas_call(
        lambda *refs: project_kernel(*refs, pieces=first),
        grid=(samples,),
        in_specs=in_specs,
        out_specs=out_specs + [tile] * 4,
        out_shape=out_shape + [jax.ShapeDtypeStruct(nodes.shape, BF16)] * 4,
        scratch_shapes=scratch,
        compiler_params=params(60),
    )(*args)


def attend_kernel(*refs):
    h0, h1, h2, h3, bias_ref, mod_ref, wk_ref, wv_ref, own_act, q_ref, own_k, own_v = refs[:12]
    outs, buffers, sems = refs[12:17], refs[17:22], refs[22]
    act_buf, k_buf, v_buf, p_buf, att_buf = buffers
    s, last = pl.program_id(0), pl.num_programs(0) - 1
    heads_count = p_buf.shape[1]
    slot = lax.rem(s, 2)

    def copies(sample, place, arrays, some_heads):
        made = [(buffers[i].at[place], outs[i].at[sample], sems.at[place, i]) for i in arrays]
        for h in some_heads:
            made.append((p_buf.at[place, h], outs[3].at[sample, h], sems.at[place, 5 + h]))
        return [pltpu.make_async_copy(*parts) for parts in made]

    def wait_for(sample, place):
        for copy in copies(sample, place, (0, 1, 2, 4), range(heads_count)):
            copy.wait()

    @pl.when(s > 1)
    def _():
        wait_for(s - 2, slot)

    count = q_ref.shape[1]
    each = h0.shape[1]
    for buf, own in ((act_buf, own_act), (k_buf, own_k), (v_buf, own_v)):
        buf[slot, 0:count, :] = own[0]
    for d, ref in enumerate((h0, h1, h2, h3)):
        begin = count + d * each
        act_buf[slot, begin : begin + each, :] = activate(ref[0], mod_ref[0])
    far = act_buf[slot, count:, :]
    k_buf[slot, count:, :] = product(far, wk_ref[...]).astype(BF16)
    v_buf[slot, count:, :] = product(far, wv_ref[...]).astype(BF16)
    for copy in copies(s, slot, (0, 1, 2), ()):
        copy.start()
    factor = math.log2(math.e) * HEAD ** (-0.5)
    heads = [slice(h * HEAD, (h + 1) * HEAD) for h in range(heads_count)]

    def score(cols):
        return product_t(k_buf[slot, :, cols], q_ref[0, :, cols])

    following = score(heads[0])
    for h, cols in enumerate(heads):
        scores = following
        if h + 1 < heads_count:
            following = score(heads[h + 1])
        scores = scores * factor + bias_ref[...]
        top = jnp.max(scores, axis=0, keepdims=True)
        expo = jnp.exp2(scores - top)
        total = jnp.sum(expo, axis=0, keepdims=True)
        probs = (expo * (1.0 / total)).astype(BF16)
        p_buf[slot, h] = probs
        att_buf[slot, :, cols] = product(v_buf[slot, :, cols].T, probs).T.astype(BF16)
        if h == heads_count // 2 - 1:
            for copy in copies(s, slot, (), range(h + 1)):
                copy.start()
    for copy in copies(s, slot, (4,), range(heads_count // 2, heads_count)):
        copy.start()

    @pl.when(s == last)
    def _():
        wait_for(s, slot)

        @pl.when(s > 0)
        def _():
            wait_for(s - 1, 1 - slot)


def attend(halos, bias, mod, wk, wv, own):
    own_act, queries, own_k, own_v = own
    samples, count, width = queries.shape
    table = bias.shape[0]
    heads = width // HEAD
    each = halos[0].shape[1]
    tables = [(table, width)] * 3 + [(heads, table, count), (count, width)]
    act, keys, values, probs, attended = pl.pallas_call(
        attend_kernel,
        grid=(samples,),
        in_specs=[per_sample((each, width))] * 4
        + [once((table, count)), per_sample((4, width))]
        + [once((width, width))] * 2
        + [per_sample((count, width))] * 4,
        out_specs=[anywhere()] * len(tables),
        out_shape=[jax.ShapeDtypeStruct((samples,) + t, BF16) for t in tables],
        scratch_shapes=[pltpu.VMEM((2,) + t, BF16) for t in tables]
        + [pltpu.SemaphoreType.DMA((2, 5 + heads))],
        compiler_params=params(60),
    )(*halos, bias, mod, wk, wv, own_act, queries, own_k, own_v)
    return [act, queries, keys, values, probs], attended


def feed_kernel(*refs, shards):
    me_ref, nodes_ref, att_ref, cot_ref, mod_ref = refs[:5]
    scratch = 9 + (10 + shards if shards else 0)
    up_acc, down_acc, wo_acc, bu_acc, bd_acc, down_rows = refs[-9:-3]
    hid_buf, hid_sems, wd_sem = refs[-3:]
    if shards:
        pieces = refs[5 : 5 + shards]
        *piece_bufs, low_buf, high_buf, in_sems, out_sems = refs[-scratch:-15]
        wo_ref, wu_ref, wd_ref, bu_ref, bd_ref, raw = refs[-15:-9]
        outs = refs[5 + shards : -scratch]

        @pl.when(pl.program_id(0) == 0)
        def _():
            arriving = [
                pltpu.make_async_copy(piece, buf, in_sems.at[i])
                for i, (piece, buf) in enumerate(zip(pieces, piece_bufs))
            ]
            for copy in arriving:
                copy.start()
            place_second(
                me_ref, piece_bufs, arriving, wo_ref, wu_ref, wd_ref, bu_ref, bd_ref, raw
            )

    else:
        wo_ref, wu_ref, wd_ref, bu_ref, bd_ref = refs[5:10]
        outs = refs[10:-scratch]
    part_ref, gmid_ref, gatt_ref, gmod_ref, hid_ref = outs[:5]
    sums = outs[5:]
    if shards:
        down_copy = pltpu.make_async_copy(wd_ref, outs[5], wd_sem.at[0])
        sums = outs[6:]

        @pl.when(pl.program_id(0) == 0)
        def _():
            down_copy.start()

    s = pl.program_id(0)
    count, width = nodes_ref.shape[1:]
    hidden_size = wu_ref.shape[1]
    wide = hidden_size // width

    def add_to(ref, cols, value):
        ref[:, cols] = jnp.where(s == 0, 0.0, ref[:, cols]) + value

    slot = lax.rem(s, 2)

    def hid_copy(sample, place):
        return pltpu.make_async_copy(hid_buf.at[place], hid_ref.at[sample], hid_sems.at[place])

    @pl.when(s > 1)
    def _():
        hid_copy(s - 2, slot).wait()

    scale, shift = mod_ref[0, 2:3, :], mod_ref[0, 3:4, :]
    blocks = [slice(c * width, (c + 1) * width) for c in range(wide)]
    attended = att_ref[0]
    cot = cot_ref[0]
    middle = nodes_ref[0].astype(F32) + product(attended, wo_ref[...])
    cot_t = cot.T
    grad_ahead = product_t(cot, wd_ref[blocks[0], :])
    add_to(bd_acc, slice(0, width), jnp.sum(cot.astype(F32), axis=0, keepdims=True))
    hat, inverse = layer_normalize(middle)
    act = (hat * scale + shift).astype(BF16)
    act_t = act.T
    part_ref[0] = middle + bd_ref[...]
    grad_act = jnp.zeros((count, width), F32)

    pre_ahead = product(act, wu_ref[:, blocks[0]])
    ready = None
    for c, cols in enumerate(blocks):
        pre, grad_hidden = pre_ahead, grad_ahead
        if c + 1 < wide:
            pre_ahead = product(act, wu_ref[:, blocks[c + 1]])
            grad_ahead = product_t(cot, wd_ref[blocks[c + 1], :])
        if ready:
            old, hidden, low_pre = ready
            grad_act = grad_act + product_t(low_pre, wu_ref[:, old])
            add_to(down_acc, old, product(cot_t, hidden))
            add_to(up_acc, old, product(act_t, low_pre))
        pre = pre + bu_ref[:, cols]
        gate = 0.5 * jnp.tanh(0.5 * pre) + 0.5
        value = pre * gate
        low_pre = (grad_hidden * (gate + value * (1.0 - gate))).astype(BF16)
        add_to(bu_acc, cols, jnp.sum(low_pre.astype(F32), axis=0, keepdims=True))
        ready = (cols, value.astype(BF16), low_pre)
        hid_buf[slot, :, cols] = ready[1]
    hid_copy(s, slot).start()
    old, hidden, low_pre = ready
    grad_act = grad_act + product_t(low_pre, wu_ref[:, old])
    add_to(down_acc, old, product(cot_t, hidden))
    add_to(up_acc, old, product(act_t, low_pre))
    grad_middle = cot.astype(F32) + norm_back(grad_act * scale, hat, inverse)
    gmid_ref[0] = grad_middle
    branch = grad_middle.astype(BF16)
    gmod_ref[0, 0:1, :] = jnp.sum(grad_act * hat, axis=0, keepdims=True)
    gmod_ref[0, 1:2, :] = jnp.sum(grad_act, axis=0, keepdims=True)
    gatt_ref[0] = product_t(branch, wo_ref[...]).astype(BF16)
    add_to(wo_acc, slice(0, width), product(attended.T, branch))

    @pl.when(s == pl.num_programs(0) - 1)
    def _():
        hid_copy(s, slot).wait()

        @pl.when(s > 0)
        def _():
            hid_copy(s - 1, 1 - slot).wait()

        if shards:
            down_copy.wait()
        for c in range(wide):
            cols = slice(c * width, (c + 1) * width)
            down_rows[cols, :] = down_acc[:, cols].T
        if len(sums) > 2:
            for ref, value in zip(sums, (up_acc, down_rows, wo_acc, bu_acc, bd_acc)):
                ref[...] = value[...]
            return
        half = low_buf.shape[0]
        devices = 2 * half
        down = hidden_size // devices
        leaving = []

        for part, ref in ((1, high_buf), (0, low_buf)):

            def pack(i, _, part=part, ref=ref):
                shard = me_ref[0] ^ relative(i + part * half, devices)
                rows = pl.ds(pl.multiple_of(shard * BLOCK, BLOCK), BLOCK)
                at = 0
                for c in range(0, hidden_size, 128):
                    ref[i, at : at + BLOCK, :] = up_acc[rows, c : c + 128].astype(BF16)
                    at += BLOCK
                for r in range(0, down, BLOCK):
                    some = pl.ds(pl.multiple_of(shard * down + r, BLOCK), BLOCK)
                    for c in range(0, width, 128):
                        ref[i, at : at + BLOCK, :] = down_rows[some, c : c + 128].astype(BF16)
                        at += BLOCK
                for c in range(0, width, 128):
                    ref[i, at : at + BLOCK, :] = wo_acc[rows, c : c + 128].astype(BF16)
                    at += BLOCK
                up_tile = pl.multiple_of(((shard * down) // 128) * 128, 128)
                down_tile = pl.multiple_of(((shard * (width // devices)) // 128) * 128, 128)
                row = lax.broadcasted_iota(jnp.int32, (BLOCK, 128), 0)
                ref[i, at : at + BLOCK, :] = jnp.where(
                    row == 0, bu_acc[:, pl.ds(up_tile, 128)], bd_acc[:, pl.ds(down_tile, 128)]
                ).astype(BF16)
                return 0

            quarter = half // 4
            for q in range(4):
                some = slice(q * quarter, (q + 1) * quarter)
                lax.fori_loop(some.start, some.stop, pack, 0, unroll=2)
                leaving.append(
                    pltpu.make_async_copy(
                        ref.at[some], sums[part].at[some], out_sems.at[part, q]
                    )
                )
                leaving[-1].start()
        for copy in leaving:
            copy.wait()


def feed(me, nodes, attended, cot, mod, hidden, devices, weights=None, shards=None):
    samples, count, width = nodes.shape
    tile = per_sample((count, width))
    scratch = [
        pltpu.VMEM((width, hidden), F32),
        pltpu.VMEM((width, hidden), F32),
        pltpu.VMEM((width, width), F32),
        pltpu.VMEM((1, hidden), F32),
        pltpu.VMEM((1, width), F32),
        pltpu.VMEM((hidden, width), F32),
        pltpu.VMEM((2, count, hidden), BF16),
        pltpu.SemaphoreType.DMA((2,)),
        pltpu.SemaphoreType.DMA((1,)),
    ]
    down = [jax.ShapeDtypeStruct((hidden, width), BF16)] if shards else []
    if shards:
        rows = shards[0].shape[1]
        sums = [jax.ShapeDtypeStruct((devices // 2, rows, 128), BF16)] * 2
        extra = list(shards)
        scratch = [pltpu.VMEM(x.shape, BF16) for x in extra + sums] + [
            pltpu.SemaphoreType.DMA((len(extra),)),
            pltpu.SemaphoreType.DMA((2, 4)),
            pltpu.VMEM((width, width), BF16),
            pltpu.VMEM((width, hidden), BF16),
            pltpu.VMEM((hidden, width), BF16),
            pltpu.VMEM((1, hidden), F32),
            pltpu.VMEM((1, width), F32),
            pltpu.VMEM((2, devices, 128), F32),
        ] + scratch
    else:
        shapes = ((width, hidden), (hidden, width), (width, width), (1, hidden), (1, width))
        sums = [jax.ShapeDtypeStruct(shape, F32) for shape in shapes]
        extra = list(weights)
    return pl.pallas_call(
        lambda *refs: feed_kernel(*refs, shards=len(shards or ())),
        grid=(samples,),
        in_specs=[smem(), tile, tile, tile, per_sample((4, width))]
        + [anywhere() if shards else once(x.shape) for x in extra],
        out_specs=[tile, tile, tile, per_sample((2, width)), anywhere()]
        + [anywhere()] * len(down)
        + [anywhere() if shards else once(x.shape) for x in sums],
        out_shape=[
            jax.ShapeDtypeStruct((samples, count, width), F32),
            jax.ShapeDtypeStruct((samples, count, width), F32),
            jax.ShapeDtypeStruct((samples, count, width), BF16),
            jax.ShapeDtypeStruct((samples, 2, width), F32),
            jax.ShapeDtypeStruct((samples, count, hidden), BF16),
        ]
        + down
        + sums,
        scratch_shapes=scratch,
        compiler_params=params(60),
    )(me, nodes, attended, cot, mod, *extra)


def emit_kernel(hid_ref, wd_ref, part_ref, out_ref):
    out_ref[0] = (part_ref[0] + product(hid_ref[0], wd_ref[...])).astype(BF16)


def emit(hid, wd, part):
    samples, count, width = part.shape
    hidden = wd.shape[0]
    tile = per_sample((count, width))
    return pl.pallas_call(
        emit_kernel,
        grid=(samples,),
        in_specs=[per_sample((count, hidden)), once((hidden, width)), tile],
        out_specs=tile,
        out_shape=jax.ShapeDtypeStruct(part.shape, BF16),
        compiler_params=params(EMIT_LIMIT),
    )(hid, wd, part)


def attend_back_kernel(*refs, started, last, begin):
    me_ref, nodes_ref, h0, h1, h2, h3, code_ref, gmod_ref = refs[:8]
    act_ref, q_ref, k_ref, v_ref, p_ref, gatt_ref, wq_ref, wk_ref, wv_ref = refs[8:17]
    gmid_ref, mod_ref = refs[17:19]
    rest = refs[19:]
    if started:
        before, rest = rest[:5], rest[10:]
    base_ref, b0, b1, b2, b3 = rest[:5]
    gq, gk, gv, p_buf, p_sems, sum_sems = rest[-6:]
    if last:
        outs = rest[5:-11]
        sums = q_acc, k_acc, v_acc, cond_acc, bias_acc = rest[-11:-6]
    else:
        sums = q_acc, k_acc, v_acc, cond_acc, bias_acc = rest[5:10]
    s, steps = pl.program_id(0), pl.num_programs(0)
    slot = lax.rem(s, 2)

    def fetch(step, h):
        place = lax.rem(step, 2)
        return pltpu.make_async_copy(
            p_ref.at[begin + step, h], p_buf.at[place, h], p_sems.at[place, h]
        )

    def carry():
        return [
            pltpu.make_async_copy(old, new, sum_sems.at[i])
            for i, (old, new) in enumerate(zip(before, sums))
        ]

    @pl.when(s == 0)
    def _():
        for h in range(p_buf.shape[1]):
            fetch(s, h).start()
        if started:
            for copy in carry():
                copy.start()

    @pl.when(s + 1 < steps)
    def _():
        for h in range(p_buf.shape[1]):
            fetch(s + 1, h).start()

    def add_to(ref, cols, value):
        old = ref[:, cols]
        ref[:, cols] = (old if started else jnp.where(s == 0, 0.0, old)) + value

    count, width = nodes_ref.shape[1:]
    each = h0.shape[1]
    inv_root = HEAD ** (-0.5)

    heads = [slice(h * HEAD, (h + 1) * HEAD) for h in range(width // HEAD)]

    def grad_of_probs(cols):
        return product_t(v_ref[0, :, cols], gatt_ref[0, :, cols])

    def spread_back(cols, grad_scores):
        gk[:, cols] = (product(grad_scores, q_ref[0, :, cols]) * inv_root).astype(BF16)
        gq[:, cols] = (product(k_ref[0, :, cols].T, grad_scores) * inv_root).T.astype(BF16)

    act_t = act_ref[0].T

    def weigh(h):
        cols = slice(h * HEAD, (h + 2) * HEAD)
        add_to(q_acc, cols, product(act_t[:, 0:count], gq[:, cols]))
        add_to(k_acc, cols, product(act_t, gk[:, cols]))
        add_to(v_acc, cols, product(act_t, gv[:, cols]))

    following = grad_of_probs(heads[0])
    hat, inverse = layer_normalize(nodes_ref[0].astype(F32))
    ready = None
    for h, cols in enumerate(heads):
        grad_probs = following
        if h + 1 < len(heads):
            following = grad_of_probs(heads[h + 1])
        if h % 2 == 0:
            for i in range(h, min(h + 2, len(heads))):
                fetch(s, i).wait()
        if h == 2 and started:

            @pl.when(s == 0)
            def _():
                for copy in carry():
                    copy.wait()

        gv[:, cols] = product(p_buf[slot, h], gatt_ref[0, :, cols]).astype(BF16)
        if ready:
            spread_back(*ready)
        if h == 2:
            weigh(0)
        probs = p_buf[slot, h].astype(F32)
        inner = jnp.sum(probs * grad_probs, axis=0, keepdims=True)
        ready = (cols, (probs * (grad_probs - inner)).astype(BF16))
    spread_back(*ready)

    grad_act = (
        product_t(gq[...], wq_ref[...])
        + product_t(gk[0:count, :], wk_ref[...])
        + product_t(gv[0:count, :], wv_ref[...])
    )
    grad_far = product_t(gk[count:, :], wk_ref[...]) + product_t(gv[count:, :], wv_ref[...])
    for h in range(2, len(heads), 2):
        weigh(h)
    base_ref[0] = gmid_ref[0] + norm_back(grad_act * mod_ref[0, 0:1, :], hat, inverse)
    scale_sum = jnp.sum(grad_act * hat, axis=0, keepdims=True)
    shift_sum = jnp.sum(grad_act, axis=0, keepdims=True)
    for d, (far, back) in enumerate(zip((h0, h1, h2, h3), (b0, b1, b2, b3))):
        part = grad_far[d * each : (d + 1) * each]
        far_hat, _ = layer_normalize(far[0].astype(F32))
        scale_sum = scale_sum + jnp.sum(part * far_hat, axis=0, keepdims=True)
        shift_sum = shift_sum + jnp.sum(part, axis=0, keepdims=True)
        back[0] = part.astype(BF16)
    kinds = (scale_sum, shift_sum, gmod_ref[0, 0:1, :], gmod_ref[0, 1:2, :])
    columns = code_ref[...].T
    mine = lax.broadcasted_iota(jnp.int32, columns.shape, 1) == s + begin
    code = jnp.sum(jnp.where(mine, columns, 0.0), axis=1, keepdims=True)
    for kind, value in enumerate(kinds):
        cols = slice(kind * width, (kind + 1) * width)
        add_to(cond_acc, cols, code * value)
        add_to(bias_acc, cols, value)
    if not last:
        return

    @pl.when(s == pl.num_programs(0) - 1)
    def _():
        if len(outs) > 2:
            for ref, value in zip(outs, sums):
                ref[...] = value[...]
            return
        half = outs[0].shape[0]
        devices = 2 * half
        for part, ref in enumerate(outs):

            def pack(i, _, part=part, ref=ref):
                shard = me_ref[0] ^ relative(i + part * half, devices)
                rows = pl.ds(pl.multiple_of(shard * BLOCK, BLOCK), BLOCK)
                at = 0
                for value in (q_acc, k_acc, v_acc):
                    for c in range(0, width, 128):
                        ref[i, at : at + BLOCK, :] = value[rows, c : c + 128].astype(BF16)
                        at += BLOCK
                tile = pl.multiple_of(((shard * (4 * width // devices)) // 128) * 128, 128)
                ref[i, at : at + BLOCK, :] = cond_acc[:, pl.ds(tile, 128)].astype(BF16)
                at += BLOCK
                ref[i, at : at + BLOCK, :] = jnp.broadcast_to(
                    bias_acc[:, pl.ds(tile, 128)], (BLOCK, 128)
                ).astype(BF16)
                return 0

            lax.fori_loop(0, half, pack, 0, unroll=2)


def attend_back(
    me,
    nodes,
    halos,
    noise_code,
    gmod,
    saved,
    gatt,
    wq,
    wk,
    wv,
    gmid,
    mod,
    devices,
    begin,
    steps,
    carried=(),
):
    samples, count, width = nodes.shape
    act, queries, keys, values, probs = saved
    table = act.shape[1]
    heads = width // HEAD
    each = halos[0].shape[1]
    half = devices // 2
    codes = noise_code.shape[1]
    last = begin + steps == samples
    shapes = [(width, width)] * 3 + [(codes, 4 * width), (1, 4 * width)]
    sums = [jax.ShapeDtypeStruct(shape, F32) for shape in shapes]
    scratch = [
        pltpu.VMEM((count, width), BF16),
        pltpu.VMEM((table, width), BF16),
        pltpu.VMEM((table, width), BF16),
        pltpu.VMEM((2, heads, table, count), BF16),
        pltpu.SemaphoreType.DMA((2, heads)),
        pltpu.SemaphoreType.DMA((5,)),
    ]
    if last:
        scratch = [pltpu.VMEM(shape, F32) for shape in shapes] + scratch
        if packs(width, devices):
            rows = 3 * BLOCK * width // 128 + 2 * BLOCK
            sums = [jax.ShapeDtypeStruct((half, rows, 128), BF16)] * 2

    def tile(*shape):
        return per_sample(shape, begin)

    args = [me, nodes, *halos, noise_code, gmod, act, queries, keys, values, probs, gatt, wq, wk, wv]
    args += [gmid, mod]
    aliases = {len(args) + 5 + i: i for i in range(5)} if carried else {}
    return pl.pallas_call(
        lambda *refs: attend_back_kernel(*refs, started=bool(carried), last=last, begin=begin),
        grid=(steps,),
        in_specs=[smem(), tile(count, width)]
        + [tile(each, width)] * 4
        + [once(noise_code.shape), tile(2, width)]
        + [tile(table, width), tile(count, width), tile(table, width), tile(table, width)]
        + [anywhere(), tile(count, width)]
        + [once((width, width))] * 3
        + [tile(count, width), tile(4, width)]
        + ([anywhere()] * 5 + [anywhere()] * 5 if carried else []),
        out_specs=[tile(count, width)]
        + [tile(each, width)] * 4
        + [once(x.shape) for x in sums],
        out_shape=[jax.ShapeDtypeStruct((samples, count, width), F32)]
        + [jax.ShapeDtypeStruct((samples, each, width), BF16)] * 4
        + sums,
        scratch_shapes=scratch,
        input_output_aliases=aliases,
        compiler_params=params(46),
    )(*args, *carried)


def finish_kernel(nodes_ref, base_ref, b0, b1, b2, b3, send_ref, mod_ref, out_ref, far):
    count = nodes_ref.shape[1]
    each = b0.shape[1]
    row = lax.broadcasted_iota(jnp.int32, (count, 4 * each), 0)
    chosen = jnp.where(row == send_ref[...], 1.0, 0.0).astype(BF16)
    for d, ref in enumerate((b0, b1, b2, b3)):
        far[d * each : (d + 1) * each, :] = ref[0]
    grad_act = product(chosen, far[...])
    hat, inverse = layer_normalize(nodes_ref[0].astype(F32))
    out_ref[0] = base_ref[0] + norm_back(grad_act * mod_ref[0, 0:1, :], hat, inverse)


def finish(nodes, base, backs, send_rows, mod):
    samples, count, width = nodes.shape
    each = backs[0].shape[1]
    picks = send_rows.size
    tile = per_sample((count, width))
    return pl.pallas_call(
        finish_kernel,
        grid=(samples,),
        in_specs=[tile, tile]
        + [per_sample((each, width))] * 4
        + [whole((1, picks)), per_sample((4, width))],
        out_specs=tile,
        out_shape=jax.ShapeDtypeStruct((samples, count, width), F32),
        scratch_shapes=[pltpu.VMEM((picks, width), BF16)],
        compiler_params=params(16),
    )(nodes, base, *backs, send_rows.reshape(1, picks), mod)


def layer(
    nodes,
    neighbours,
    send_rows,
    noise_code,
    w_query,
    w_key,
    w_value,
    w_out,
    w_up,
    b_up,
    w_down,
    b_down,
    cond_weight,
    cond_bias,
    cotangent,
):
    devices = lax.axis_size("patch") * lax.axis_size("sample")
    position = lax.axis_index("patch") * lax.axis_size("sample") + lax.axis_index("sample")
    me = position.astype(jnp.int32).reshape(1)
    width = nodes.shape[2]
    hidden = w_up.shape[1]
    offsets = (1, -1, STRIDE, -STRIDE)

    samples, count, _ = nodes.shape
    table = count + send_rows.size
    if not packs(width, devices):
        return plain_body(
            me,
            nodes,
            neighbours,
            send_rows,
            noise_code,
            (w_query, w_key, w_value, cond_weight, cond_bias, noise_code),
            (w_out, w_up, b_up, w_down, b_down),
            cotangent,
            devices,
        )
    z_side, plane, (core,) = stage_groups(devices)

    def swaps(pieces, group):
        return [swap(x, c, devices) for x, c in zip(pieces, group)]

    def cores(pieces):
        return [swap(x, core, devices) for x in pieces]

    def shifts(blocks, sign):
        return [from_behind(x, sign * o) for x, o in zip(blocks, offsets)]

    *sends, first, second = begin(
        nodes,
        send_rows,
        (w_query, w_key, w_value, cond_weight, cond_bias, w_out, w_up, b_up, w_down, b_down),
    )
    far = swaps([first] * 3, z_side)
    far_second = swaps([second] * 3, z_side)
    bias = slot_bias(neighbours, table)
    halos = shifts([after(x, bias) for x in sends], 1)
    held = join([first] + far)
    low_first = [held] + swaps([held] * 3, plane)
    high_first = cores(low_first)
    wq, wk, wv, mod, *own = project(nodes, shards=[me, noise_code] + low_first + high_first)
    held_second = join([second] + far_second)
    low_second = [held_second] + swaps([held_second] * 3, plane)
    saved, attended = attend(halos, bias, mod, wk, wv, own)
    high_second = cores(low_second)
    part, gmid, gatt, gmod, hid, down_whole, low_feed, high_feed = feed(
        me,
        nodes,
        attended,
        cotangent,
        mod,
        hidden,
        devices,
        shards=low_second + high_second,
    )
    back = (me, nodes, halos, noise_code, gmod, saved, gatt, wq, wk, wv, gmid, mod, devices)
    (got_feed,) = cores([high_feed])
    *arrays, s0, s1, s2, s3, s4 = attend_back(*back, 0, 1)
    own_feed, *parts = add_halves(low_feed, got_feed, 4)
    feed_far = swaps(parts, plane)
    carried = (after(s0, own_feed), s1, s2, s3, s4, *arrays)
    base, *rest = attend_back(*back, 1, samples - 1, carried)
    low_proj, high_proj = rest[4:]
    (got_proj,) = cores([high_proj])
    own_feed, *parts = add_pieces([own_feed] + feed_far)
    feed_last = swaps(parts, z_side)
    own_proj, *parts = add_halves(low_proj, got_proj, 4)
    proj_far = swaps(parts, plane)
    backs = shifts(rest[:4], -1)
    result = emit(hid, down_whole, after(part, own_feed))
    own_proj, *parts = add_pieces([own_proj] + proj_far)
    proj_last = swaps(parts, z_side)
    grad_nodes = finish(nodes, base, backs, send_rows, mod)
    down, thin = hidden // devices, width // devices
    step = 4 * width // devices
    (
        grad_up,
        grad_down,
        grad_out,
        grad_b_up,
        grad_b_down,
        grad_query,
        grad_key,
        grad_value,
        grad_cond,
        grad_cond_bias,
    ) = last_sum(
        me,
        [own_feed] + feed_last,
        [own_proj] + proj_last,
        ((BLOCK, hidden), (down, width), (BLOCK, width), (1, down), (1, thin))
        + ((BLOCK, width),) * 3
        + ((BLOCK, step), (1, step)),
    )
    grad_b_up, grad_b_down, grad_cond_bias = grad_b_up[0], grad_b_down[0], grad_cond_bias[0]
    return (
        result,
        grad_nodes,
        grad_query,
        grad_key,
        grad_value,
        grad_out,
        grad_up,
        grad_b_up,
        grad_down,
        grad_b_down,
        grad_cond,
        grad_cond_bias,
    )


def plain_body(
    me, nodes, neighbours, send_rows, noise_code, first, second, cotangent, devices
):
    samples, count, _ = nodes.shape
    hidden = second[1].shape[1]
    offsets = (1, -1, STRIDE, -STRIDE)
    bias = slot_bias(neighbours, count + send_rows.size)
    sends = begin(nodes, send_rows)
    halos = [from_behind(block, offset) for block, offset in zip(sends, offsets)]
    (wq, wk, wv, mod), weights = gather_plain(*first, *second)
    own = project(nodes, weights=(wq, wk, wv, mod))
    saved, attended = attend(halos, bias, mod, wk, wv, own)
    part, gmid, gatt, gmod, hid, *sums = feed(
        me, nodes, attended, cotangent, mod, hidden, devices, weights=weights
    )
    result = emit(hid, weights[2], part)
    sums[3:] = [x[0] for x in sums[3:]]
    grad_up, grad_down, grad_out, grad_b_up, grad_b_down = scatter_plain(sums, (0,) * 5)
    base, *rest = attend_back(
        me, nodes, halos, noise_code, gmod, saved, gatt, wq, wk, wv, gmid, mod, devices, 0, samples
    )
    backs = [from_behind(block, -offset) for block, offset in zip(rest[:4], offsets)]
    rest[-1] = rest[-1][0]
    grad_query, grad_key, grad_value, grad_cond, grad_cond_bias = scatter_plain(
        rest[4:], (0, 0, 0, 1, 0)
    )
    grad_nodes = finish(nodes, base, backs, send_rows, mod)
    return (
        result,
        grad_nodes,
        grad_query,
        grad_key,
        grad_value,
        grad_out,
        grad_up,
        grad_b_up,
        grad_down,
        grad_b_down,
        grad_cond,
        grad_cond_bias,
    )


def solution(mesh):
    both = P(("patch", "sample"), None)
    flat = P(("patch", "sample"))
    split = P("sample", "patch", None)
    cond = P(None, ("patch", "sample"))
    return jax.shard_map(
        layer,
        mesh=mesh,
        in_specs=(
            split,
            P("patch", None),
            P("patch", None),
            P("sample", None),
            both,
            both,
            both,
            both,
            both,
            flat,
            both,
            flat,
            cond,
            flat,
            split,
        ),
        out_specs=(split, split, both, both, both, both, both, flat, both, flat, cond, flat),
        check_vma=False,
    )
```

```python
import math

import jax
import jax.numpy as jnp
from jax import lax
from jax.experimental import pallas as pl
from jax.experimental.pallas import tpu as pltpu
from jax.sharding import PartitionSpec as P


HEAD = 128
STRIDE = 4
BLOCK = 16
AXES = ("patch", "sample")
EPSILON = 1e-05
F32 = jnp.float32
BF16 = jnp.bfloat16
MIB = 1024 * 1024
EMIT_LIMIT = 20


def product(left, right):
    return jnp.dot(left, right, preferred_element_type=F32)


def product_t(left, right):
    return lax.dot_general(left, right, (((1,), (1,)), ((), ())), preferred_element_type=F32)


def from_behind(block, distance):
    count = lax.axis_size("patch")
    return lax.ppermute(block, "patch", [((i - distance) % count, i) for i in range(count)])


def swap(block, bits, devices):
    return lax.ppermute(block, AXES, [(i, i ^ bits) for i in range(devices)])


def stage_groups(devices):
    bits = [1 << i for i in reversed(range(devices.bit_length() - 1)) if (1 << i) != 2]
    groups = [bits[i : i + 2] for i in range(0, len(bits), 2)]
    return [combos(g) for g in groups] + [[2]]


def combos(group):
    if len(group) == 1:
        return [group[0]]
    high, low = group
    return [low, high, low | high]


def relative(k, devices):
    shift, out = 0, 0
    for group in stage_groups(devices):
        if len(group) == 1:
            out = out | (((k >> shift) & 1) * group[0])
            shift += 1
        else:
            out = out | (((k >> shift) & 1) * group[0]) | (((k >> (shift + 1)) & 1) * group[1])
            shift += 2
    return out


def join_kernel(*refs):
    at = 0
    for ref in refs[:-1]:
        refs[-1][at : at + ref.shape[0]] = ref[...]
        at += ref.shape[0]


def join(pieces):
    count = sum(piece.shape[0] for piece in pieces)
    return pl.pallas_call(
        join_kernel,
        out_shape=jax.ShapeDtypeStruct((count,) + pieces[0].shape[1:], pieces[0].dtype),
        compiler_params=plain(8),
    )(*pieces)


def after(value, *others):
    return lax.optimization_barrier((value,) + others)[0]


def layer_normalize(values):
    centre = jnp.mean(values, axis=-1, keepdims=True)
    centred = values - centre
    inverse = lax.rsqrt(jnp.mean(centred * centred, axis=-1, keepdims=True) + EPSILON)
    return centred * inverse, inverse


def norm_back(grad_hat, normed, inverse):
    first = jnp.mean(grad_hat, axis=-1, keepdims=True)
    second = jnp.mean(grad_hat * normed, axis=-1, keepdims=True)
    return inverse * (grad_hat - first - normed * second)


def whole(shape):
    return pl.BlockSpec(shape, lambda *_: (0,) * len(shape))


def once(shape):
    return pl.BlockSpec(shape, lambda *_: (0,) * len(shape), pipeline_mode=pl.Buffered(1))


def per_sample(shape, begin=0):
    return pl.BlockSpec((1,) + shape, lambda s, *_: (s + begin,) + (0,) * len(shape))


def anywhere():
    return pl.BlockSpec(memory_space=pl.ANY)


def params(limit, axes=1):
    return pltpu.CompilerParams(
        dimension_semantics=("arbitrary",) * axes, vmem_limit_bytes=limit * MIB
    )


def plain(limit):
    return pltpu.CompilerParams(vmem_limit_bytes=limit * MIB)


def bias_kernel(nbr_ref, bias_ref):
    table, count = bias_ref.shape
    height = 2 * BLOCK
    row = lax.broadcasted_iota(jnp.int32, (height, count), 0)
    slots = nbr_ref[...]

    def block(i, _):
        begin = pl.multiple_of(i * height, height)
        total = jnp.zeros((height, count), F32)
        for j in range(slots.shape[0]):
            total = total + jnp.where(row == slots[j : j + 1, :] - begin, 1.0, 0.0)
        bias_ref[pl.ds(begin, height), :] = jnp.where(
            total > 0.0, jnp.log2(jnp.maximum(total, 1.0)), -1e30
        )
        return 0

    lax.fori_loop(0, table // height, block, 0)


def slot_bias(neighbours, table):
    return pl.pallas_call(
        bias_kernel,
        out_shape=jax.ShapeDtypeStruct((table, neighbours.shape[0]), F32),
        compiler_params=plain(8),
    )(neighbours.T)


def pick_rows(nodes_ref, send_ref, out_refs):
    samples, count, _ = nodes_ref.shape
    each = send_ref.shape[1]
    lanes = lax.broadcasted_iota(jnp.int32, (each, count), 1)
    columns = send_ref[...].T
    for d, out_ref in enumerate(out_refs):
        chosen = jnp.where(lanes == columns[:, d : d + 1], 1.0, 0.0).astype(BF16)
        for s in range(samples):
            out_ref[s] = product(chosen, nodes_ref[s]).astype(BF16)


def blocks_of(ref):
    height, width = ref.shape
    for r in range(0, height, BLOCK):
        for c in range(0, width, 128):
            yield slice(r, r + BLOCK), slice(c, c + 128)


def pack_shards(weights, first_ref, second_ref):
    wq, wk, wv, cw, cb, wo, wu, bu, wd, bd = weights
    for source, ref in (((wq, wk, wv), first_ref), ((wu, wd, wo), second_ref)):
        at = 0
        for part in source:
            for rows, cols in blocks_of(part):
                ref[0, at : at + BLOCK, :] = part[rows, cols]
                at += BLOCK
        ref[0, at : at + BLOCK, :] = jnp.zeros((BLOCK, 128), BF16)
    at = first_ref.shape[1] - BLOCK
    first_ref[0, at : at + BLOCK, 0 : cw.shape[1]] = cw[...]
    first_ref[0, at : at + 1, cb.shape[1] :] = cb[...]
    at = second_ref.shape[1] - BLOCK
    for row, part in enumerate((bu, bd)):
        step = part.shape[1]
        for c in range(0, 128, step):
            second_ref[0, at + row : at + row + 1, c : c + step] = part[...]


def begin_kernel(*refs, ways, given):
    nodes_ref, send_ref = refs[:2]
    weights, out_refs = refs[2 : 2 + given], refs[2 + given : 2 + given + ways]
    pick_rows(nodes_ref, send_ref, out_refs)
    if weights:
        pack_shards(weights, *refs[-2:])


def begin(nodes, send_rows, weights=()):
    samples, _, width = nodes.shape
    ways, each = send_rows.shape
    weights = [w if w.ndim == 2 else w[None] for w in weights]
    shards = []
    if weights:
        wq, wk, wv, _, _, wo, wu, _, wd, _ = weights
        for group in ((wq, wk, wv), (wo, wu, wd)):
            rows = sum(w.size for w in group) // 128 + BLOCK
            shards.append(jax.ShapeDtypeStruct((1, rows, 128), BF16))
    return pl.pallas_call(
        lambda *refs: begin_kernel(*refs, ways=ways, given=len(weights)),
        out_shape=[jax.ShapeDtypeStruct((samples, each, width), BF16)] * ways + shards,
        compiler_params=plain(60),
    )(nodes, send_rows, *weights)


def spread(rows, step, width):
    reps = jnp.concatenate([rows] * (width // 128), axis=1)
    lane = lax.broadcasted_iota(jnp.int32, reps.shape, 1)
    row = lax.broadcasted_iota(jnp.int32, reps.shape, 0)
    return jnp.sum(jnp.where(lane // step == row, reps, 0.0), axis=0, keepdims=True)


def place(source, k, shard, targets):
    at = 0
    for ref, height in targets:
        for r in range(0, height, BLOCK):
            rows = pl.ds(pl.multiple_of(shard * height + r, BLOCK), BLOCK)
            for c in range(0, ref.shape[1], 128):
                ref[rows, c : c + 128] = source[k, at : at + BLOCK, :]
                at += BLOCK
    return at


def for_shards(pieces, take, arriving=()):
    at = 0
    for n, ref in enumerate(pieces):
        if arriving:
            arriving[n].wait()

        def step(i, _, ref=ref, at=at):
            take(at + i, ref, i)
            return 0

        lax.fori_loop(0, ref.shape[0], step, 0, unroll=2)
        at += ref.shape[0]


def place_first(me_ref, pieces, code_ref, wq_ref, wk_ref, wv_ref, mod_ref, raw):
    devices = sum(ref.shape[0] for ref in pieces)
    samples = code_ref.shape[0]
    width = wq_ref.shape[1]
    step = 4 * width // devices
    lane = lax.broadcasted_iota(jnp.int32, (BLOCK, 128), 1)
    columns = code_ref[...].T
    code = [jnp.where(lane < 64, columns[:, s : s + 1], 1.0) for s in range(samples)]

    def take(k, source, i):
        shard = me_ref[0] ^ relative(k, devices)
        targets = ((wq_ref, BLOCK), (wk_ref, BLOCK), (wv_ref, BLOCK))
        at = place(source, i, shard, targets)
        cond = source[i, at : at + BLOCK, :].astype(F32)
        for s in range(samples):
            value = jnp.sum(cond * code[s], axis=0, keepdims=True)
            raw[s, pl.ds(shard, 1), :] = value + pltpu.roll(value, 64, 1)

    for_shards(pieces, take)
    each = devices // 4
    for s in range(samples):
        for kind in range(4):
            value = spread(raw[s, kind * each : (kind + 1) * each, :], step, width)
            mod_ref[s, kind : kind + 1, :] = value + 1.0 if kind % 2 == 0 else value


def place_second(me_ref, pieces, arriving, wo_ref, wu_ref, wd_ref, bu_ref, bd_ref, raw):
    devices = sum(ref.shape[0] for ref in pieces)
    width = wo_ref.shape[1]
    hidden = wu_ref.shape[1]

    def take(k, source, i):
        shard = me_ref[0] ^ relative(k, devices)
        targets = ((wu_ref, BLOCK), (wd_ref, hidden // devices), (wo_ref, BLOCK))
        at = place(source, i, shard, targets)
        extra = source[i, at : at + BLOCK, :].astype(F32)
        raw[0, pl.ds(shard, 1), :] = extra[0:1]
        raw[1, pl.ds(shard, 1), :] = extra[1:2]

    for_shards(pieces, take, arriving)
    each = devices // (hidden // width)
    for c in range(hidden // width):
        bu_ref[:, c * width : (c + 1) * width] = spread(
            raw[0, c * each : (c + 1) * each, :], hidden // devices, width
        )
    bd_ref[...] = spread(raw[1], width // devices, width)


def packs(width, devices):
    return width == devices * BLOCK


def gather_plain(wq, wk, wv, cond_weight, cond_bias, noise_code, wo, wu, bu, wd, bd):
    def full(x, axis=0):
        return lax.all_gather(x, AXES, axis=axis, tiled=True)

    mod = jnp.dot(
        noise_code, full(cond_weight, 1).astype(F32), precision=lax.Precision.HIGHEST
    ) + full(cond_bias).astype(F32)
    mod = mod.reshape(noise_code.shape[0], 4, wq.shape[1])
    mod = mod + jnp.array([1.0, 0.0, 1.0, 0.0], F32)[:, None]
    first = (full(wq), full(wk), full(wv), mod)
    biases = (full(bu)[None].astype(F32), full(bd)[None].astype(F32))
    return first, (full(wo), full(wu), full(wd)) + biases


def scatter_plain(sums, axes):
    return [
        lax.psum_scatter(x, AXES, scatter_dimension=axis, tiled=True)
        for x, axis in zip(sums, axes)
    ]


def add_kernel(own_ref, far_ref, *out_refs):
    size = out_refs[0].shape[0]
    for i, out_ref in enumerate(out_refs):
        part = slice(i * size, (i + 1) * size)
        out_ref[...] = own_ref[part] + far_ref[part]


def add_halves(own_half, far_half, parts):
    count, rows, lanes = own_half.shape
    return pl.pallas_call(
        add_kernel,
        out_shape=[jax.ShapeDtypeStruct((count // parts, rows, lanes), BF16)] * parts,
        compiler_params=plain(16),
    )(own_half, far_half)


def add_more_kernel(*refs):
    sources, outs = refs[: -refs[0].shape[0]], refs[-refs[0].shape[0] :]
    for i, out_ref in enumerate(outs):
        total = sources[0][i].astype(F32)
        for ref in sources[1:]:
            total = total + ref[i].astype(F32)
        out_ref[0] = total.astype(BF16)


def add_pieces(pieces):
    count, rows, lanes = pieces[0].shape
    return pl.pallas_call(
        add_more_kernel,
        out_shape=[jax.ShapeDtypeStruct((1, rows, lanes), BF16)] * count,
        compiler_params=plain(8),
    )(*pieces)


def last_kernel(me_ref, *refs, pieces):
    feed_refs, proj_refs = refs[: pieces[0]], refs[pieces[0] : sum(pieces)]
    outs = refs[sum(pieces) :]
    position = me_ref[0]

    def total(sources, at):
        value = sources[0][0, at : at + BLOCK, :].astype(F32)
        for ref in sources[1:]:
            value = value + ref[0, at : at + BLOCK, :].astype(F32)
        return value

    def own(value, step, row, height):
        shift = 128 - lax.rem(position * step, 128)
        return pltpu.roll(value, shift, 1)[row : row + height, 0:step]

    def unpack(sources, refs):
        at = 0
        for ref in refs:
            for rows, cols in blocks_of(ref):
                ref[rows, cols] = total(sources, at)
                at += BLOCK
        return at

    at = unpack(feed_refs, outs[:3])
    biases = total(feed_refs, at)
    for row, ref in enumerate(outs[3:5]):
        ref[...] = own(biases, ref.shape[1], row, 1)
    at = unpack(proj_refs, outs[5:8])
    step = outs[8].shape[1]
    outs[8][...] = own(total(proj_refs, at), step, 0, BLOCK)
    outs[9][...] = own(total(proj_refs, at + BLOCK), step, 0, 1)


def last_sum(me, feed_pieces, proj_pieces, shapes):
    pieces = (len(feed_pieces), len(proj_pieces))
    return pl.pallas_call(
        lambda *refs: last_kernel(*refs, pieces=pieces),
        out_shape=[jax.ShapeDtypeStruct(shape, F32) for shape in shapes],
        in_specs=[smem()] + [pl.BlockSpec(memory_space=pltpu.VMEM)] * sum(pieces),
        compiler_params=plain(60),
    )(me, *feed_pieces, *proj_pieces)


def smem():
    return pl.BlockSpec(memory_space=pltpu.SMEM)


def activate(rows, mod):
    hat, _ = layer_normalize(rows.astype(F32))
    return (hat * mod[0:1] + mod[1:2]).astype(BF16)


def project_kernel(*refs, pieces):
    nodes_ref = refs[0]
    s = pl.program_id(0)
    if pieces:
        me_ref, code_ref = refs[1:3]
        shards = refs[3 : 3 + pieces]
        wq_ref, wk_ref, wv_ref, mod_ref = refs[3 + pieces : 7 + pieces]
        act_ref, q_ref, k_ref, v_ref, raw = refs[7 + pieces :]

        @pl.when(s == 0)
        def _():
            place_first(me_ref, shards, code_ref, wq_ref, wk_ref, wv_ref, mod_ref, raw)

        mod = mod_ref[s]
    else:
        mod_ref, wq_ref, wk_ref, wv_ref, act_ref, q_ref, k_ref, v_ref = refs[1:]
        mod = mod_ref[0]
    act = activate(nodes_ref[0], mod)
    act_ref[0] = act
    q_ref[0] = product(act, wq_ref[...]).astype(BF16)
    k_ref[0] = product(act, wk_ref[...]).astype(BF16)
    v_ref[0] = product(act, wv_ref[...]).astype(BF16)


def project(nodes, weights=None, shards=None):
    samples, count, width = nodes.shape
    tile = per_sample((count, width))
    in_specs, args = [tile], [nodes]
    out_specs, out_shape, scratch, first = [], [], [], 0
    if shards is None:
        wq, wk, wv, mod = weights
        in_specs += [per_sample((4, width))] + [once((width, width))] * 3
        args += [mod, wq, wk, wv]
    else:
        me, code, *pieces = shards
        first = len(pieces)
        in_specs += [smem(), once(code.shape)] + [once(x.shape) for x in pieces]
        args += [me, code] + pieces
        square = jax.ShapeDtypeStruct((width, width), BF16)
        out_shape += [square] * 3 + [jax.ShapeDtypeStruct((samples, 4, width), F32)]
        out_specs += [once(x.shape) for x in out_shape]
        scratch = [pltpu.VMEM((samples, sum(x.shape[0] for x in pieces), 128), F32)]
    return pl.pallas_call(
        lambda *refs: project_kernel(*refs, pieces=first),
        grid=(samples,),
        in_specs=in_specs,
        out_specs=out_specs + [tile] * 4,
        out_shape=out_shape + [jax.ShapeDtypeStruct(nodes.shape, BF16)] * 4,
        scratch_shapes=scratch,
        compiler_params=params(60),
    )(*args)


def attend_kernel(*refs):
    h0, h1, h2, h3, bias_ref, mod_ref, wk_ref, wv_ref, own_act, q_ref, own_k, own_v = refs[:12]
    outs, buffers, sems = refs[12:17], refs[17:22], refs[22]
    act_buf, k_buf, v_buf, p_buf, att_buf = buffers
    s, last = pl.program_id(0), pl.num_programs(0) - 1
    heads_count = p_buf.shape[1]
    slot = lax.rem(s, 2)

    def copies(sample, place, arrays, some_heads):
        made = [(buffers[i].at[place], outs[i].at[sample], sems.at[place, i]) for i in arrays]
        for h in some_heads:
            made.append((p_buf.at[place, h], outs[3].at[sample, h], sems.at[place, 5 + h]))
        return [pltpu.make_async_copy(*parts) for parts in made]

    def wait_for(sample, place):
        for copy in copies(sample, place, (0, 1, 2, 4), range(heads_count)):
            copy.wait()

    @pl.when(s > 1)
    def _():
        wait_for(s - 2, slot)

    count = q_ref.shape[1]
    each = h0.shape[1]
    for buf, own in ((act_buf, own_act), (k_buf, own_k), (v_buf, own_v)):
        buf[slot, 0:count, :] = own[0]
    for d, ref in enumerate((h0, h1, h2, h3)):
        begin = count + d * each
        act_buf[slot, begin : begin + each, :] = activate(ref[0], mod_ref[0])
    far = act_buf[slot, count:, :]
    k_buf[slot, count:, :] = product(far, wk_ref[...]).astype(BF16)
    v_buf[slot, count:, :] = product(far, wv_ref[...]).astype(BF16)
    for copy in copies(s, slot, (0, 1, 2), ()):
        copy.start()
    factor = math.log2(math.e) * HEAD ** (-0.5)
    heads = [slice(h * HEAD, (h + 1) * HEAD) for h in range(heads_count)]

    def score(cols):
        return product_t(k_buf[slot, :, cols], q_ref[0, :, cols])

    following = score(heads[0])
    for h, cols in enumerate(heads):
        scores = following
        if h + 1 < heads_count:
            following = score(heads[h + 1])
        scores = scores * factor + bias_ref[...]
        top = jnp.max(scores, axis=0, keepdims=True)
        expo = jnp.exp2(scores - top)
        total = jnp.sum(expo, axis=0, keepdims=True)
        probs = (expo * (1.0 / total)).astype(BF16)
        p_buf[slot, h] = probs
        att_buf[slot, :, cols] = product(v_buf[slot, :, cols].T, probs).T.astype(BF16)
        if h == heads_count // 2 - 1:
            for copy in copies(s, slot, (), range(h + 1)):
                copy.start()
    for copy in copies(s, slot, (4,), range(heads_count // 2, heads_count)):
        copy.start()

    @pl.when(s == last)
    def _():
        wait_for(s, slot)

        @pl.when(s > 0)
        def _():
            wait_for(s - 1, 1 - slot)


def attend(halos, bias, mod, wk, wv, own):
    own_act, queries, own_k, own_v = own
    samples, count, width = queries.shape
    table = bias.shape[0]
    heads = width // HEAD
    each = halos[0].shape[1]
    tables = [(table, width)] * 3 + [(heads, table, count), (count, width)]
    act, keys, values, probs, attended = pl.pallas_call(
        attend_kernel,
        grid=(samples,),
        in_specs=[per_sample((each, width))] * 4
        + [once((table, count)), per_sample((4, width))]
        + [once((width, width))] * 2
        + [per_sample((count, width))] * 4,
        out_specs=[anywhere()] * len(tables),
        out_shape=[jax.ShapeDtypeStruct((samples,) + t, BF16) for t in tables],
        scratch_shapes=[pltpu.VMEM((2,) + t, BF16) for t in tables]
        + [pltpu.SemaphoreType.DMA((2, 5 + heads))],
        compiler_params=params(60),
    )(*halos, bias, mod, wk, wv, own_act, queries, own_k, own_v)
    return [act, queries, keys, values, probs], attended


def feed_kernel(*refs, shards):
    me_ref, nodes_ref, att_ref, cot_ref, mod_ref = refs[:5]
    scratch = 9 + (10 + shards if shards else 0)
    up_acc, down_acc, wo_acc, bu_acc, bd_acc, down_rows = refs[-9:-3]
    hid_buf, hid_sems, wd_sem = refs[-3:]
    if shards:
        pieces = refs[5 : 5 + shards]
        *piece_bufs, low_buf, high_buf, in_sems, out_sems = refs[-scratch:-15]
        wo_ref, wu_ref, wd_ref, bu_ref, bd_ref, raw = refs[-15:-9]
        outs = refs[5 + shards : -scratch]

        @pl.when(pl.program_id(0) == 0)
        def _():
            arriving = [
                pltpu.make_async_copy(piece, buf, in_sems.at[i])
                for i, (piece, buf) in enumerate(zip(pieces, piece_bufs))
            ]
            for copy in arriving:
                copy.start()
            place_second(
                me_ref, piece_bufs, arriving, wo_ref, wu_ref, wd_ref, bu_ref, bd_ref, raw
            )

    else:
        wo_ref, wu_ref, wd_ref, bu_ref, bd_ref = refs[5:10]
        outs = refs[10:-scratch]
    part_ref, gmid_ref, gatt_ref, gmod_ref, hid_ref = outs[:5]
    sums = outs[5:]
    if shards:
        down_copy = pltpu.make_async_copy(wd_ref, outs[5], wd_sem.at[0])
        sums = outs[6:]

        @pl.when(pl.program_id(0) == 0)
        def _():
            down_copy.start()

    s = pl.program_id(0)
    count, width = nodes_ref.shape[1:]
    hidden_size = wu_ref.shape[1]
    wide = hidden_size // width

    def add_to(ref, cols, value):
        ref[:, cols] = jnp.where(s == 0, 0.0, ref[:, cols]) + value

    slot = lax.rem(s, 2)

    def hid_copy(sample, place):
        return pltpu.make_async_copy(hid_buf.at[place], hid_ref.at[sample], hid_sems.at[place])

    @pl.when(s > 1)
    def _():
        hid_copy(s - 2, slot).wait()

    scale, shift = mod_ref[0, 2:3, :], mod_ref[0, 3:4, :]
    blocks = [slice(c * width, (c + 1) * width) for c in range(wide)]
    attended = att_ref[0]
    cot = cot_ref[0]
    middle = nodes_ref[0].astype(F32) + product(attended, wo_ref[...])
    cot_t = cot.T
    grad_ahead = product_t(cot, wd_ref[blocks[0], :])
    add_to(bd_acc, slice(0, width), jnp.sum(cot.astype(F32), axis=0, keepdims=True))
    hat, inverse = layer_normalize(middle)
    act = (hat * scale + shift).astype(BF16)
    act_t = act.T
    part_ref[0] = middle + bd_ref[...]
    grad_act = jnp.zeros((count, width), F32)

    pre_ahead = product(act, wu_ref[:, blocks[0]])
    ready = None
    for c, cols in enumerate(blocks):
        pre, grad_hidden = pre_ahead, grad_ahead
        if c + 1 < wide:
            pre_ahead = product(act, wu_ref[:, blocks[c + 1]])
            grad_ahead = product_t(cot, wd_ref[blocks[c + 1], :])
        if ready:
            old, hidden, low_pre = ready
            grad_act = grad_act + product_t(low_pre, wu_ref[:, old])
            add_to(down_acc, old, product(cot_t, hidden))
            add_to(up_acc, old, product(act_t, low_pre))
        pre = pre + bu_ref[:, cols]
        gate = 0.5 * jnp.tanh(0.5 * pre) + 0.5
        value = pre * gate
        low_pre = (grad_hidden * (gate + value * (1.0 - gate))).astype(BF16)
        add_to(bu_acc, cols, jnp.sum(low_pre.astype(F32), axis=0, keepdims=True))
        ready = (cols, value.astype(BF16), low_pre)
        hid_buf[slot, :, cols] = ready[1]
    hid_copy(s, slot).start()
    old, hidden, low_pre = ready
    grad_act = grad_act + product_t(low_pre, wu_ref[:, old])
    add_to(down_acc, old, product(cot_t, hidden))
    add_to(up_acc, old, product(act_t, low_pre))
    grad_middle = cot.astype(F32) + norm_back(grad_act * scale, hat, inverse)
    gmid_ref[0] = grad_middle
    branch = grad_middle.astype(BF16)
    gmod_ref[0, 0:1, :] = jnp.sum(grad_act * hat, axis=0, keepdims=True)
    gmod_ref[0, 1:2, :] = jnp.sum(grad_act, axis=0, keepdims=True)
    gatt_ref[0] = product_t(branch, wo_ref[...]).astype(BF16)
    add_to(wo_acc, slice(0, width), product(attended.T, branch))

    @pl.when(s == pl.num_programs(0) - 1)
    def _():
        hid_copy(s, slot).wait()

        @pl.when(s > 0)
        def _():
            hid_copy(s - 1, 1 - slot).wait()

        if shards:
            down_copy.wait()
        for c in range(wide):
            cols = slice(c * width, (c + 1) * width)
            down_rows[cols, :] = down_acc[:, cols].astype(down_rows.dtype).T
        if len(sums) > 2:
            for ref, value in zip(sums, (up_acc, down_rows, wo_acc, bu_acc, bd_acc)):
                ref[...] = value[...]
            return
        half = low_buf.shape[0]
        devices = 2 * half
        down = hidden_size // devices
        leaving = []

        for part, ref in ((1, high_buf), (0, low_buf)):

            def pack(i, _, part=part, ref=ref):
                shard = me_ref[0] ^ relative(i + part * half, devices)
                rows = pl.ds(pl.multiple_of(shard * BLOCK, BLOCK), BLOCK)
                at = 0
                for c in range(0, hidden_size, 128):
                    ref[i, at : at + BLOCK, :] = up_acc[rows, c : c + 128].astype(BF16)
                    at += BLOCK
                for r in range(0, down, BLOCK):
                    some = pl.ds(pl.multiple_of(shard * down + r, BLOCK), BLOCK)
                    for c in range(0, width, 128):
                        ref[i, at : at + BLOCK, :] = down_rows[some, c : c + 128].astype(BF16)
                        at += BLOCK
                for c in range(0, width, 128):
                    ref[i, at : at + BLOCK, :] = wo_acc[rows, c : c + 128].astype(BF16)
                    at += BLOCK
                up_tile = pl.multiple_of(((shard * down) // 128) * 128, 128)
                down_tile = pl.multiple_of(((shard * (width // devices)) // 128) * 128, 128)
                row = lax.broadcasted_iota(jnp.int32, (BLOCK, 128), 0)
                ref[i, at : at + BLOCK, :] = jnp.where(
                    row == 0, bu_acc[:, pl.ds(up_tile, 128)], bd_acc[:, pl.ds(down_tile, 128)]
                ).astype(BF16)
                return 0

            quarter = half // 4
            for q in range(4):
                some = slice(q * quarter, (q + 1) * quarter)
                lax.fori_loop(some.start, some.stop, pack, 0, unroll=4)
                leaving.append(
                    pltpu.make_async_copy(
                        ref.at[some], sums[part].at[some], out_sems.at[part, q]
                    )
                )
                leaving[-1].start()
        for copy in leaving:
            copy.wait()


def feed(me, nodes, attended, cot, mod, hidden, devices, weights=None, shards=None):
    samples, count, width = nodes.shape
    tile = per_sample((count, width))
    scratch = [
        pltpu.VMEM((width, hidden), F32),
        pltpu.VMEM((width, hidden), F32),
        pltpu.VMEM((width, width), F32),
        pltpu.VMEM((1, hidden), F32),
        pltpu.VMEM((1, width), F32),
        pltpu.VMEM((hidden, width), BF16 if shards else F32),
        pltpu.VMEM((2, count, hidden), BF16),
        pltpu.SemaphoreType.DMA((2,)),
        pltpu.SemaphoreType.DMA((1,)),
    ]
    down = [jax.ShapeDtypeStruct((hidden, width), BF16)] if shards else []
    if shards:
        rows = shards[0].shape[1]
        sums = [jax.ShapeDtypeStruct((devices // 2, rows, 128), BF16)] * 2
        extra = list(shards)
        scratch = [pltpu.VMEM(x.shape, BF16) for x in extra + sums] + [
            pltpu.SemaphoreType.DMA((len(extra),)),
            pltpu.SemaphoreType.DMA((2, 4)),
            pltpu.VMEM((width, width), BF16),
            pltpu.VMEM((width, hidden), BF16),
            pltpu.VMEM((hidden, width), BF16),
            pltpu.VMEM((1, hidden), F32),
            pltpu.VMEM((1, width), F32),
            pltpu.VMEM((2, devices, 128), F32),
        ] + scratch
    else:
        shapes = ((width, hidden), (hidden, width), (width, width), (1, hidden), (1, width))
        sums = [jax.ShapeDtypeStruct(shape, F32) for shape in shapes]
        extra = list(weights)
    return pl.pallas_call(
        lambda *refs: feed_kernel(*refs, shards=len(shards or ())),
        grid=(samples,),
        in_specs=[smem(), tile, tile, tile, per_sample((4, width))]
        + [anywhere() if shards else once(x.shape) for x in extra],
        out_specs=[tile, tile, tile, per_sample((2, width)), anywhere()]
        + [anywhere()] * len(down)
        + [anywhere() if shards else once(x.shape) for x in sums],
        out_shape=[
            jax.ShapeDtypeStruct((samples, count, width), F32),
            jax.ShapeDtypeStruct((samples, count, width), F32),
            jax.ShapeDtypeStruct((samples, count, width), BF16),
            jax.ShapeDtypeStruct((samples, 2, width), F32),
            jax.ShapeDtypeStruct((samples, count, hidden), BF16),
        ]
        + down
        + sums,
        scratch_shapes=scratch,
        compiler_params=params(60),
    )(me, nodes, attended, cot, mod, *extra)


def emit_kernel(hid_ref, wd_ref, part_ref, out_ref):
    out_ref[0] = (part_ref[0] + product(hid_ref[0], wd_ref[...])).astype(BF16)


def emit(hid, wd, part):
    samples, count, width = part.shape
    hidden = wd.shape[0]
    tile = per_sample((count, width))
    return pl.pallas_call(
        emit_kernel,
        grid=(samples,),
        in_specs=[per_sample((count, hidden)), once((hidden, width)), tile],
        out_specs=tile,
        out_shape=jax.ShapeDtypeStruct(part.shape, BF16),
        compiler_params=params(EMIT_LIMIT),
    )(hid, wd, part)


def attend_back_kernel(*refs, started, last, begin):
    me_ref, nodes_ref, h0, h1, h2, h3, code_ref, gmod_ref = refs[:8]
    act_ref, q_ref, k_ref, v_ref, p_ref, gatt_ref, wq_ref, wk_ref, wv_ref = refs[8:17]
    gmid_ref, mod_ref = refs[17:19]
    rest = refs[19:]
    if started:
        before, rest = rest[:5], rest[10:]
    base_ref, b0, b1, b2, b3 = rest[:5]
    gq, gk, gv, p_buf, p_sems, sum_sems = rest[-6:]
    if last:
        outs = rest[5:-11]
        sums = q_acc, k_acc, v_acc, cond_acc, bias_acc = rest[-11:-6]
    else:
        sums = q_acc, k_acc, v_acc, cond_acc, bias_acc = rest[5:10]
    s, steps = pl.program_id(0), pl.num_programs(0)
    slot = lax.rem(s, 2)

    def fetch(step, h):
        place = lax.rem(step, 2)
        return pltpu.make_async_copy(
            p_ref.at[begin + step, h], p_buf.at[place, h], p_sems.at[place, h]
        )

    def carry():
        return [
            pltpu.make_async_copy(old, new, sum_sems.at[i])
            for i, (old, new) in enumerate(zip(before, sums))
        ]

    @pl.when(s == 0)
    def _():
        for h in range(p_buf.shape[1]):
            fetch(s, h).start()
        if started:
            for copy in carry():
                copy.start()

    @pl.when(s + 1 < steps)
    def _():
        for h in range(p_buf.shape[1]):
            fetch(s + 1, h).start()

    def add_to(ref, cols, value):
        old = ref[:, cols]
        ref[:, cols] = (old if started else jnp.where(s == 0, 0.0, old)) + value

    count, width = nodes_ref.shape[1:]
    each = h0.shape[1]
    inv_root = HEAD ** (-0.5)

    heads = [slice(h * HEAD, (h + 1) * HEAD) for h in range(width // HEAD)]

    def grad_of_probs(cols):
        return product_t(v_ref[0, :, cols], gatt_ref[0, :, cols])

    def spread_back(cols, grad_scores):
        gk[:, cols] = (product(grad_scores, q_ref[0, :, cols]) * inv_root).astype(BF16)
        gq[:, cols] = (product(k_ref[0, :, cols].T, grad_scores) * inv_root).T.astype(BF16)

    act_t = act_ref[0].T

    def weigh(h):
        cols = slice(h * HEAD, (h + 2) * HEAD)
        add_to(q_acc, cols, product(act_t[:, 0:count], gq[:, cols]))
        add_to(k_acc, cols, product(act_t, gk[:, cols]))
        add_to(v_acc, cols, product(act_t, gv[:, cols]))

    following = grad_of_probs(heads[0])
    hat, inverse = layer_normalize(nodes_ref[0].astype(F32))
    ready = None
    for h, cols in enumerate(heads):
        grad_probs = following
        if h + 1 < len(heads):
            following = grad_of_probs(heads[h + 1])
        if h % 2 == 0:
            for i in range(h, min(h + 2, len(heads))):
                fetch(s, i).wait()
        if h == 2 and started:

            @pl.when(s == 0)
            def _():
                for copy in carry():
                    copy.wait()

        gv[:, cols] = product(p_buf[slot, h], gatt_ref[0, :, cols]).astype(BF16)
        if ready:
            spread_back(*ready)
        if h == 2:
            weigh(0)
        probs = p_buf[slot, h].astype(F32)
        inner = jnp.sum(probs * grad_probs, axis=0, keepdims=True)
        ready = (cols, (probs * (grad_probs - inner)).astype(BF16))
    spread_back(*ready)

    grad_act = (
        product_t(gq[...], wq_ref[...])
        + product_t(gk[0:count, :], wk_ref[...])
        + product_t(gv[0:count, :], wv_ref[...])
    )
    grad_far = product_t(gk[count:, :], wk_ref[...]) + product_t(gv[count:, :], wv_ref[...])
    for h in range(2, len(heads), 2):
        weigh(h)
    base_ref[0] = gmid_ref[0] + norm_back(grad_act * mod_ref[0, 0:1, :], hat, inverse)
    scale_sum = jnp.sum(grad_act * hat, axis=0, keepdims=True)
    shift_sum = jnp.sum(grad_act, axis=0, keepdims=True)
    for d, (far, back) in enumerate(zip((h0, h1, h2, h3), (b0, b1, b2, b3))):
        part = grad_far[d * each : (d + 1) * each]
        far_hat, _ = layer_normalize(far[0].astype(F32))
        scale_sum = scale_sum + jnp.sum(part * far_hat, axis=0, keepdims=True)
        shift_sum = shift_sum + jnp.sum(part, axis=0, keepdims=True)
        back[0] = part.astype(BF16)
    kinds = (scale_sum, shift_sum, gmod_ref[0, 0:1, :], gmod_ref[0, 1:2, :])
    columns = code_ref[...].T
    mine = lax.broadcasted_iota(jnp.int32, columns.shape, 1) == s + begin
    code = jnp.sum(jnp.where(mine, columns, 0.0), axis=1, keepdims=True)
    for kind, value in enumerate(kinds):
        cols = slice(kind * width, (kind + 1) * width)
        add_to(cond_acc, cols, code * value)
        add_to(bias_acc, cols, value)
    if not last:
        return

    @pl.when(s == pl.num_programs(0) - 1)
    def _():
        if len(outs) > 2:
            for ref, value in zip(outs, sums):
                ref[...] = value[...]
            return
        half = outs[0].shape[0]
        devices = 2 * half
        for part, ref in enumerate(outs):

            def pack(i, _, part=part, ref=ref):
                shard = me_ref[0] ^ relative(i + part * half, devices)
                rows = pl.ds(pl.multiple_of(shard * BLOCK, BLOCK), BLOCK)
                at = 0
                for value in (q_acc, k_acc, v_acc):
                    for c in range(0, width, 128):
                        ref[i, at : at + BLOCK, :] = value[rows, c : c + 128].astype(BF16)
                        at += BLOCK
                tile = pl.multiple_of(((shard * (4 * width // devices)) // 128) * 128, 128)
                ref[i, at : at + BLOCK, :] = cond_acc[:, pl.ds(tile, 128)].astype(BF16)
                at += BLOCK
                ref[i, at : at + BLOCK, :] = jnp.broadcast_to(
                    bias_acc[:, pl.ds(tile, 128)], (BLOCK, 128)
                ).astype(BF16)
                return 0

            lax.fori_loop(0, half, pack, 0, unroll=2)


def attend_back(
    me,
    nodes,
    halos,
    noise_code,
    gmod,
    saved,
    gatt,
    wq,
    wk,
    wv,
    gmid,
    mod,
    devices,
    begin,
    steps,
    carried=(),
):
    samples, count, width = nodes.shape
    act, queries, keys, values, probs = saved
    table = act.shape[1]
    heads = width // HEAD
    each = halos[0].shape[1]
    half = devices // 2
    codes = noise_code.shape[1]
    last = begin + steps == samples
    shapes = [(width, width)] * 3 + [(codes, 4 * width), (1, 4 * width)]
    sums = [jax.ShapeDtypeStruct(shape, F32) for shape in shapes]
    scratch = [
        pltpu.VMEM((count, width), BF16),
        pltpu.VMEM((table, width), BF16),
        pltpu.VMEM((table, width), BF16),
        pltpu.VMEM((2, heads, table, count), BF16),
        pltpu.SemaphoreType.DMA((2, heads)),
        pltpu.SemaphoreType.DMA((5,)),
    ]
    if last:
        scratch = [pltpu.VMEM(shape, F32) for shape in shapes] + scratch
        if packs(width, devices):
            rows = 3 * BLOCK * width // 128 + 2 * BLOCK
            sums = [jax.ShapeDtypeStruct((half, rows, 128), BF16)] * 2

    def tile(*shape):
        return per_sample(shape, begin)

    args = [me, nodes, *halos, noise_code, gmod, act, queries, keys, values, probs, gatt, wq, wk, wv]
    args += [gmid, mod]
    aliases = {len(args) + 5 + i: i for i in range(5)} if carried else {}
    return pl.pallas_call(
        lambda *refs: attend_back_kernel(*refs, started=bool(carried), last=last, begin=begin),
        grid=(steps,),
        in_specs=[smem(), tile(count, width)]
        + [tile(each, width)] * 4
        + [once(noise_code.shape), tile(2, width)]
        + [tile(table, width), tile(count, width), tile(table, width), tile(table, width)]
        + [anywhere(), tile(count, width)]
        + [once((width, width))] * 3
        + [tile(count, width), tile(4, width)]
        + ([anywhere()] * 5 + [anywhere()] * 5 if carried else []),
        out_specs=[tile(count, width)]
        + [tile(each, width)] * 4
        + [once(x.shape) for x in sums],
        out_shape=[jax.ShapeDtypeStruct((samples, count, width), F32)]
        + [jax.ShapeDtypeStruct((samples, each, width), BF16)] * 4
        + sums,
        scratch_shapes=scratch,
        input_output_aliases=aliases,
        compiler_params=params(46),
    )(*args, *carried)


def finish_kernel(nodes_ref, base_ref, b0, b1, b2, b3, send_ref, mod_ref, out_ref, far):
    count = nodes_ref.shape[1]
    each = b0.shape[1]
    row = lax.broadcasted_iota(jnp.int32, (count, 4 * each), 0)
    chosen = jnp.where(row == send_ref[...], 1.0, 0.0).astype(BF16)
    for d, ref in enumerate((b0, b1, b2, b3)):
        far[d * each : (d + 1) * each, :] = ref[0]
    grad_act = product(chosen, far[...])
    hat, inverse = layer_normalize(nodes_ref[0].astype(F32))
    out_ref[0] = base_ref[0] + norm_back(grad_act * mod_ref[0, 0:1, :], hat, inverse)


def finish(nodes, base, backs, send_rows, mod):
    samples, count, width = nodes.shape
    each = backs[0].shape[1]
    picks = send_rows.size
    tile = per_sample((count, width))
    return pl.pallas_call(
        finish_kernel,
        grid=(samples,),
        in_specs=[tile, tile]
        + [per_sample((each, width))] * 4
        + [whole((1, picks)), per_sample((4, width))],
        out_specs=tile,
        out_shape=jax.ShapeDtypeStruct((samples, count, width), F32),
        scratch_shapes=[pltpu.VMEM((picks, width), BF16)],
        compiler_params=params(16),
    )(nodes, base, *backs, send_rows.reshape(1, picks), mod)


def layer(
    nodes,
    neighbours,
    send_rows,
    noise_code,
    w_query,
    w_key,
    w_value,
    w_out,
    w_up,
    b_up,
    w_down,
    b_down,
    cond_weight,
    cond_bias,
    cotangent,
):
    devices = lax.axis_size("patch") * lax.axis_size("sample")
    position = lax.axis_index("patch") * lax.axis_size("sample") + lax.axis_index("sample")
    me = position.astype(jnp.int32).reshape(1)
    width = nodes.shape[2]
    hidden = w_up.shape[1]
    offsets = (1, -1, STRIDE, -STRIDE)

    samples, count, _ = nodes.shape
    table = count + send_rows.size
    if not packs(width, devices):
        return plain_body(
            me,
            nodes,
            neighbours,
            send_rows,
            noise_code,
            (w_query, w_key, w_value, cond_weight, cond_bias, noise_code),
            (w_out, w_up, b_up, w_down, b_down),
            cotangent,
            devices,
        )
    z_side, plane, (core,) = stage_groups(devices)

    def swaps(pieces, group):
        return [swap(x, c, devices) for x, c in zip(pieces, group)]

    def cores(pieces):
        return [swap(x, core, devices) for x in pieces]

    def shifts(blocks, sign):
        return [from_behind(x, sign * o) for x, o in zip(blocks, offsets)]

    *sends, first, second = begin(
        nodes,
        send_rows,
        (w_query, w_key, w_value, cond_weight, cond_bias, w_out, w_up, b_up, w_down, b_down),
    )
    far = swaps([first] * 3, z_side)
    far_second = swaps([second] * 3, z_side)
    bias = slot_bias(neighbours, table)
    halos = shifts([after(x, bias) for x in sends], 1)
    held = join([first] + far)
    low_first = [held] + swaps([held] * 3, plane)
    high_first = cores(low_first)
    wq, wk, wv, mod, *own = project(nodes, shards=[me, noise_code] + low_first + high_first)
    held_second = join([second] + far_second)
    low_second = [held_second] + swaps([held_second] * 3, plane)
    saved, attended = attend(halos, bias, mod, wk, wv, own)
    high_second = cores(low_second)
    part, gmid, gatt, gmod, hid, down_whole, low_feed, high_feed = feed(
        me,
        nodes,
        attended,
        cotangent,
        mod,
        hidden,
        devices,
        shards=low_second + high_second,
    )
    back = (me, nodes, halos, noise_code, gmod, saved, gatt, wq, wk, wv, gmid, mod, devices)
    (got_feed,) = cores([high_feed])
    *arrays, s0, s1, s2, s3, s4 = attend_back(*back, 0, 1)
    own_feed, *parts = add_halves(low_feed, got_feed, 4)
    feed_far = swaps(parts, plane)
    carried = (after(s0, own_feed), s1, s2, s3, s4, *arrays)
    base, *rest = attend_back(*back, 1, samples - 1, carried)
    low_proj, high_proj = rest[4:]
    (got_proj,) = cores([high_proj])
    own_feed, *parts = add_pieces([own_feed] + feed_far)
    feed_last = swaps(parts, z_side)
    own_proj, *parts = add_halves(low_proj, got_proj, 4)
    proj_far = swaps(parts, plane)
    backs = shifts(rest[:4], -1)
    result = emit(hid, down_whole, after(part, own_feed))
    own_proj, *parts = add_pieces([own_proj] + proj_far)
    proj_last = swaps(parts, z_side)
    grad_nodes = finish(nodes, base, backs, send_rows, mod)
    down, thin = hidden // devices, width // devices
    step = 4 * width // devices
    (
        grad_up,
        grad_down,
        grad_out,
        grad_b_up,
        grad_b_down,
        grad_query,
        grad_key,
        grad_value,
        grad_cond,
        grad_cond_bias,
    ) = last_sum(
        me,
        [own_feed] + feed_last,
        [own_proj] + proj_last,
        ((BLOCK, hidden), (down, width), (BLOCK, width), (1, down), (1, thin))
        + ((BLOCK, width),) * 3
        + ((BLOCK, step), (1, step)),
    )
    grad_b_up, grad_b_down, grad_cond_bias = grad_b_up[0], grad_b_down[0], grad_cond_bias[0]
    return (
        result,
        grad_nodes,
        grad_query,
        grad_key,
        grad_value,
        grad_out,
        grad_up,
        grad_b_up,
        grad_down,
        grad_b_down,
        grad_cond,
        grad_cond_bias,
    )


def plain_body(
    me, nodes, neighbours, send_rows, noise_code, first, second, cotangent, devices
):
    samples, count, _ = nodes.shape
    hidden = second[1].shape[1]
    offsets = (1, -1, STRIDE, -STRIDE)
    bias = slot_bias(neighbours, count + send_rows.size)
    sends = begin(nodes, send_rows)
    halos = [from_behind(block, offset) for block, offset in zip(sends, offsets)]
    (wq, wk, wv, mod), weights = gather_plain(*first, *second)
    own = project(nodes, weights=(wq, wk, wv, mod))
    saved, attended = attend(halos, bias, mod, wk, wv, own)
    part, gmid, gatt, gmod, hid, *sums = feed(
        me, nodes, attended, cotangent, mod, hidden, devices, weights=weights
    )
    result = emit(hid, weights[2], part)
    sums[3:] = [x[0] for x in sums[3:]]
    grad_up, grad_down, grad_out, grad_b_up, grad_b_down = scatter_plain(sums, (0,) * 5)
    base, *rest = attend_back(
        me, nodes, halos, noise_code, gmod, saved, gatt, wq, wk, wv, gmid, mod, devices, 0, samples
    )
    backs = [from_behind(block, -offset) for block, offset in zip(rest[:4], offsets)]
    rest[-1] = rest[-1][0]
    grad_query, grad_key, grad_value, grad_cond, grad_cond_bias = scatter_plain(
        rest[4:], (0, 0, 0, 1, 0)
    )
    grad_nodes = finish(nodes, base, backs, send_rows, mod)
    return (
        result,
        grad_nodes,
        grad_query,
        grad_key,
        grad_value,
        grad_out,
        grad_up,
        grad_b_up,
        grad_down,
        grad_b_down,
        grad_cond,
        grad_cond_bias,
    )


def solution(mesh):
    both = P(("patch", "sample"), None)
    flat = P(("patch", "sample"))
    split = P("sample", "patch", None)
    cond = P(None, ("patch", "sample"))
    return jax.shard_map(
        layer,
        mesh=mesh,
        in_specs=(
            split,
            P("patch", None),
            P("patch", None),
            P("sample", None),
            both,
            both,
            both,
            both,
            both,
            flat,
            both,
            flat,
            cond,
            flat,
            split,
        ),
        out_specs=(split, split, both, both, both, both, both, flat, both, flat, cond, flat),
        check_vma=False,
    )
```
